128 devices in a mesh: pipe: 4 (over y), dp: 32 (over z, x, core).
Axes of the slice: x: 4, y: 4, z: 4, core: 2. Of those that a mesh axis runs over, the one named last changes fastest.
Arguments:
- x_in: bfloat16 [4, 1024, 4096], P(None, 'dp'), may hold values from -6 to 6
- cotangent: bfloat16 [4, 1024, 4096], P(None, 'dp'), may hold values from -6 to 6
- weights: bfloat16 [4, 64, 64, 2048], P('pipe', 'dp'), as said below
- live_rows: int32 [4, 64, 32], P('pipe'), may hold values from 0 to 63, as said below
- moment: float32 [4, 64, 64, 2048], P('pipe', 'dp'), may hold values from -0.125 to 0.125
- second: float32 [4, 64, 64, 2048], P('pipe', 'dp'), may hold values from 1.2207031e-05 to 0.00024414062
Outputs:
- weights_out: bfloat16 [4, 64, 64, 2048], P('pipe', 'dp')
- moment_out: float32 [4, 64, 64, 2048], P('pipe', 'dp')
- second_out: float32 [4, 64, 64, 2048], P('pipe', 'dp')
The draws below stay inside these ranges and needn't reach their ends.
Inputs may be any that keep to these rules, and one draw needn't show every extreme that they name: `live_rows`: for each layer and block column the 32 entries are distinct block rows. `weights`: entry [l, j, b, k * 64 + a] is the weight from input feature live_rows[l, j, k] * 64 + a to output feature j * 64 + b; unstored blocks are zero.
All inputs are finite; a program needn't handle non-finite values.
Results may differ from the reference program's by a relative error of at most 0.009.
Values may be sent and summed in bfloat16 or wider, within the bound.
A program may use at most 256 MiB of HBM per device.

```python
import math
import jax
import jax.numpy as jnp
from jax import lax

D = 4096
HEAD = 128
BLOCK = 64
MICRO = 4
TOK_DEV = 32
NB = 64
LIVE = 32
HEADS = 32
ROWS = 1024
TOKENS = 4096
LAYERS = 4
N_DP = 32


def live_pattern(key):
    sub_key = jax.random.fold_in(key, 7)
    key_list = jax.random.split(sub_key, LAYERS * NB)
    shuffled = jax.vmap(lambda one_key: jax.random.permutation(one_key, NB))(key_list)
    return shuffled[:, :LIVE].reshape(LAYERS, NB, LIVE).astype(jnp.int32)


def draw_live_rows(key, part):
    return live_pattern(key)


def draw_weights(key, part):
    live_index = live_pattern(key)
    entry_key, head_key, block_key, column_key = jax.random.split(jax.random.fold_in(key, 11), 4)
    shape_five = (LAYERS, NB, BLOCK, LIVE, BLOCK)
    entries = jax.random.normal(entry_key, shape_five, jnp.float32)
    head_scale = jnp.exp(jax.random.uniform(head_key, (LAYERS, HEADS), jnp.float32, math.log(0.3), math.log(3.0)))
    block_scale = jnp.exp(jax.random.uniform(block_key, (LAYERS, NB, LIVE), jnp.float32, math.log(0.25), math.log(4.0)))
    column_scale = (1.0 + 2.0 * jnp.arange(NB, dtype=jnp.float32) / (NB - 1)) * jnp.exp(jax.random.uniform(column_key, (LAYERS, NB), jnp.float32, math.log(0.7), math.log(1.4)))
    layer_index = jnp.arange(LAYERS, dtype=jnp.int32)[:, None, None]
    row_scale = head_scale[layer_index, live_index // (HEAD // BLOCK)]
    factor = 0.3 / math.sqrt(LIVE * BLOCK) * row_scale * column_scale[:, :, None] * block_scale
    values = entries * factor[:, :, None, :, None]
    return values.reshape(LAYERS, NB, BLOCK, LIVE * BLOCK).astype(jnp.bfloat16)


def block_levels(rng, shape, shards, least, high):
    factor_of = 1.0
    for axis_at, parts in shards:
        draws = jax.random.uniform(jax.random.fold_in(jax.random.fold_in(rng, 6), axis_at), (parts,), jnp.float32, least / len(shards), high / len(shards))
        factor_of = factor_of * jnp.repeat(jnp.exp(draws), shape[axis_at] // parts).reshape((-1,) + (1,) * (len(shape) - 1 - axis_at))
    return factor_of


def normal_values(key, dims, deviation, bound, shards=(), kind=jnp.bfloat16):
    values = deviation * jax.random.normal(key, dims, jnp.float32)
    if shards:
        values = values * block_levels(key, dims, shards, -0.22, 0.18)
    return jnp.clip(values, -bound, bound).astype(kind)


def setup_inputs(seed: int = 0) -> dict:
    arg_keys = jax.random.split(jax.random.key(seed), 7)
    return {
        "x_in": normal_values(arg_keys[0], (MICRO, ROWS, D), 1.0, 6.0, ((1, 32),)),
        "cotangent": normal_values(arg_keys[1], (MICRO, ROWS, D), 1.0, 6.0, ((1, 32),)),
        "weights": draw_weights(jax.random.fold_in(arg_keys[6], 71), 0),
        "live_rows": draw_live_rows(jax.random.fold_in(arg_keys[6], 71), 0),
        "moment": normal_values(arg_keys[4], (LAYERS, NB, BLOCK, LIVE * BLOCK), (0.5 / TOKENS ** 0.5), 0.125, ((0, 4), (1, 32)), jnp.float32),
        "second": jnp.clip(jnp.exp(math.log(0.00024414062) - 2.9957323 * jax.random.uniform(arg_keys[5], (LAYERS, NB, BLOCK, LIVE * BLOCK), jnp.float32) ** block_levels(arg_keys[5], (LAYERS, NB, BLOCK, LIVE * BLOCK), ((0, 4), (1, 32)), -0.2, 0.2)), 1.220703143189894e-05, 0.00024414062),
    }


highest = lax.Precision.HIGHEST

def expand(packed, live_index):
    column_count, block_size, wide = packed.shape
    live_count = live_index.shape[1]
    values = packed.astype(jnp.float32).reshape(column_count, block_size, live_count, block_size).transpose(0, 2, 3, 1)
    column_ids = jnp.broadcast_to(jnp.arange(column_count, dtype=jnp.int32)[:, None], (column_count, live_count))
    expanded = jnp.zeros((column_count, block_size, column_count, block_size), jnp.float32)
    expanded = expanded.at[live_index, :, column_ids, :].set(values)
    return expanded.reshape(column_count * block_size, column_count * block_size)

def pack(expanded, live_index):
    column_count, live_count = live_index.shape
    column_ids = jnp.broadcast_to(jnp.arange(column_count, dtype=jnp.int32)[:, None], (column_count, live_count))
    four_way = expanded.reshape(column_count, BLOCK, column_count, BLOCK)[live_index, :, column_ids, :]
    return four_way.transpose(0, 3, 1, 2).reshape(column_count, BLOCK, live_count * BLOCK)

def weight_grad(normed, grad_pre, live_index):
    summed = jnp.zeros((NB, BLOCK, LIVE * BLOCK), jnp.float32)
    for member in range(N_DP):
        normed_part = normed[:, member * TOK_DEV:(member + 1) * TOK_DEV].reshape(-1, D).astype(jnp.float32)
        grad_part = grad_pre[:, member * TOK_DEV:(member + 1) * TOK_DEV].reshape(-1, D).astype(jnp.float32)
        expanded = jnp.dot(normed_part.T, grad_part, precision=highest) * (1.0 / TOKENS)
        rounded = lax.optimization_barrier(pack(expanded, live_index).astype(jnp.bfloat16))
        summed = summed + rounded.astype(jnp.float32)
    return summed

def shrink(magnitude, threshold):
    return jnp.maximum(magnitude - threshold, 0.0) / jnp.maximum(magnitude, threshold)

def tree_prox(stepped, live_index):
    blocked = stepped.reshape(NB, BLOCK, LIVE, BLOCK)
    magnitude = jnp.sqrt(lax.optimization_barrier(jnp.sum(blocked * blocked, axis=(1, 3))))
    leafed = blocked * shrink(magnitude, 0.15 * math.sqrt(BLOCK / LIVE))[:, None, :, None]
    block_squares = lax.optimization_barrier(jnp.sum(leafed * leafed, axis=(1, 3)))
    head_index = live_index // (HEAD // BLOCK)
    onehot = (head_index[:, :, None] == jnp.arange(HEADS, dtype=jnp.int32)[None, None, :]).astype(jnp.float32)
    head_squares = lax.optimization_barrier(jnp.sum(onehot * block_squares[:, :, None], axis=(0, 1)))
    head_factor = shrink(jnp.sqrt(head_squares), 0.45 * math.sqrt(HEAD))
    headed = leafed * lax.optimization_barrier(jnp.sum(onehot * head_factor[None, None, :], axis=2))[:, None, :, None]
    layer_squares = jnp.sum(headed * headed)
    layer_factor = shrink(jnp.sqrt(layer_squares), 0.45 * math.sqrt(D))
    return (headed * layer_factor).astype(jnp.bfloat16).reshape(NB, BLOCK, LIVE * BLOCK)

def reference(x_in, cotangent, weights, live_rows, moment, second):
    expanded_list = [expand(weights[layer], live_rows[layer]) for layer in range(LAYERS)]
    hidden = x_in
    saved = []
    for layer in range(LAYERS):
        as_float = hidden.astype(jnp.float32)
        inverse_rms = lax.rsqrt(lax.optimization_barrier(jnp.mean(as_float * as_float, axis=-1, keepdims=True)) + 1e-05)
        normed = (as_float * inverse_rms).astype(jnp.bfloat16)
        pre_act = jnp.dot(normed.reshape(-1, D).astype(jnp.float32), expanded_list[layer], precision=highest).reshape(hidden.shape)
        saved.append((hidden, normed, pre_act))
        hidden = (as_float + jax.nn.silu(pre_act)).astype(jnp.bfloat16)
    arriving = cotangent
    grads = [None] * LAYERS
    for layer in reversed(range(LAYERS)):
        entering, normed, pre_act = saved[layer]
        as_float = entering.astype(jnp.float32)
        inverse_rms = lax.rsqrt(lax.optimization_barrier(jnp.mean(as_float * as_float, axis=-1, keepdims=True)) + 1e-05)
        sigmoid_z = jax.nn.sigmoid(pre_act)
        grad_pre = (arriving.astype(jnp.float32) * (sigmoid_z * (1.0 + pre_act * (1.0 - sigmoid_z)))).astype(jnp.bfloat16)
        grad_normed = jnp.dot(grad_pre.reshape(-1, D).astype(jnp.float32), expanded_list[layer].T, precision=highest).reshape(entering.shape)
        scaled = as_float * inverse_rms
        arriving = (arriving.astype(jnp.float32) + inverse_rms * (grad_normed - scaled * lax.optimization_barrier(jnp.mean(grad_normed * scaled, axis=-1, keepdims=True)))).astype(jnp.bfloat16)
        grads[layer] = weight_grad(normed, grad_pre, live_rows[layer])
    rate = 0.1 / math.sqrt(LIVE * BLOCK)
    new_weights, new_moment, new_second = ([], [], [])
    for layer in range(LAYERS):
        gradient = grads[layer]
        moment_new = 0.9 * moment[layer] + 0.1 * gradient
        second_new = 0.95 * second[layer] + 0.05 * gradient * gradient
        stepped = weights[layer].astype(jnp.float32) - rate * moment_new / (jnp.sqrt(second_new) + 1e-08)
        new_weights.append(tree_prox(stepped, live_rows[layer]))
        new_moment.append(moment_new)
        new_second.append(second_new)
    return (jnp.stack(new_weights), jnp.stack(new_moment), jnp.stack(new_second))
```

```python
import math

import jax
import jax.numpy as jnp
from jax import lax
from jax.experimental import pallas as pl
from jax.experimental.pallas import tpu as pltpu
from jax.sharding import PartitionSpec as P

HEAD = 128


def shifted(value, axis, steps):
    count = lax.axis_size(axis)
    leading, last = (max(0, -steps), min(count, count - steps))
    return lax.ppermute(value, axis, [(source, source + steps) for source in range(leading, last)])


def shrink(magnitude, threshold):
    return jnp.maximum(magnitude - threshold, 0.0) / jnp.maximum(magnitude, threshold)


def pick_half(tile, index, want_odd):
    rolled = pltpu.roll(tile, 64, 1)
    keep = (index % 2) == want_odd
    return jnp.where(keep, tile, rolled)


def expand_kernel(table_ref, w_ref, o_ref):
    j = pl.program_id(0)
    rows = w_ref.shape[1]
    lane = lax.broadcasted_iota(jnp.int32, (rows, 128), 1)
    pairs = o_ref.shape[2] // 128
    for p in range(pairs):
        k0 = table_ref[j * 2 * pairs + 2 * p]
        k1 = table_ref[j * 2 * pairs + 2 * p + 1]
        s0 = pl.multiple_of((jnp.maximum(k0, 0) // 2) * 128, 128)
        s1 = pl.multiple_of((jnp.maximum(k1, 0) // 2) * 128, 128)
        t0 = w_ref[0, :, pl.ds(s0, 128)].astype(jnp.float32)
        t1 = w_ref[0, :, pl.ds(s1, 128)].astype(jnp.float32)
        low = jnp.where(k0 >= 0, pick_half(t0, k0, 0), 0.0)
        high = jnp.where(k1 >= 0, pick_half(t1, k1, 1), 0.0)
        o_ref[0, :, p * 128:(p + 1) * 128] = jnp.where(lane < 64, low, high).astype(o_ref.dtype)


def pack_kernel(table_ref, g_ref, o_ref):
    j = pl.program_id(0)
    rows = g_ref.shape[1]
    lane = lax.broadcasted_iota(jnp.int32, (rows, 128), 1)
    pairs = o_ref.shape[2] // 128
    for q in range(pairs):
        r0 = table_ref[j * 2 * pairs + 2 * q]
        r1 = table_ref[j * 2 * pairs + 2 * q + 1]
        s0 = pl.multiple_of((r0 // 2) * 128, 128)
        s1 = pl.multiple_of((r1 // 2) * 128, 128)
        t0 = g_ref[0, :, pl.ds(s0, 128)].astype(jnp.float32)
        t1 = g_ref[0, :, pl.ds(s1, 128)].astype(jnp.float32)
        low = pick_half(t0, r0, 0)
        high = pick_half(t1, r1, 1)
        o_ref[0, :, q * 128:(q + 1) * 128] = jnp.where(lane < 64, low, high).astype(o_ref.dtype)


def expand_dense(section_weights, live_index):
    column_count, block_size, wide = section_weights.shape
    live_count = live_index.shape[1]
    features = column_count * block_size
    targets = jnp.arange(column_count, dtype=jnp.int32)
    hit = live_index[:, :, None] == targets[None, None, :]
    k_ids = jnp.arange(live_count, dtype=jnp.int32)[None, :, None]
    inverse = jnp.where(
        jnp.any(hit, axis=1), jnp.sum(jnp.where(hit, k_ids, 0), axis=1), -1
    ).astype(jnp.int32)
    out = pl.pallas_call(
        expand_kernel,
        out_shape=jax.ShapeDtypeStruct((column_count, block_size, features), section_weights.dtype),
        grid_spec=pltpu.PrefetchScalarGridSpec(
            num_scalar_prefetch=1,
            grid=(column_count,),
            in_specs=[pl.BlockSpec((1, block_size, wide), lambda j, tbl: (j, 0, 0))],
            out_specs=pl.BlockSpec((1, block_size, features), lambda j, tbl: (j, 0, 0)),
        ),
        cost_estimate=pl.CostEstimate(
            flops=0, transcendentals=0, bytes_accessed=3 * column_count * block_size * wide * 2
        ),
    )(inverse.reshape(-1), section_weights)
    return out.reshape(features, features)


def pack_dense(dense_grad, live_index):
    column_count, live_count = live_index.shape
    features = dense_grad.shape[0]
    block_size = features // column_count
    wide = live_count * block_size
    return pl.pallas_call(
        pack_kernel,
        out_shape=jax.ShapeDtypeStruct((column_count, block_size, wide), dense_grad.dtype),
        grid_spec=pltpu.PrefetchScalarGridSpec(
            num_scalar_prefetch=1,
            grid=(column_count,),
            in_specs=[pl.BlockSpec((1, block_size, features), lambda j, tbl: (j, 0, 0))],
            out_specs=pl.BlockSpec((1, block_size, wide), lambda j, tbl: (j, 0, 0)),
        ),
        cost_estimate=pl.CostEstimate(
            flops=0, transcendentals=0, bytes_accessed=3 * column_count * block_size * wide * 2
        ),
    )(live_index.reshape(-1).astype(jnp.int32), dense_grad.reshape(column_count, block_size, features))


def layer_forward(entering, dense_t):
    as_float = entering.astype(jnp.float32)
    inverse_rms = lax.rsqrt(jnp.mean(as_float * as_float, axis=-1, keepdims=True) + 1e-05)
    normed = (as_float * inverse_rms).astype(jnp.bfloat16)
    pre_act = lax.dot_general(
        normed, dense_t, (((1,), (1,)), ((), ())), preferred_element_type=jnp.float32
    )
    return ((as_float + jax.nn.silu(pre_act)).astype(jnp.bfloat16), normed, pre_act)


def layer_backward(arriving, entering, pre_act, dense_t):
    as_float = entering.astype(jnp.float32)
    inverse_rms = lax.rsqrt(jnp.mean(as_float * as_float, axis=-1, keepdims=True) + 1e-05)
    sigmoid_z = jax.nn.sigmoid(pre_act)
    grad_pre = (
        arriving.astype(jnp.float32) * (sigmoid_z * (1.0 + pre_act * (1.0 - sigmoid_z)))
    ).astype(jnp.bfloat16)
    grad_normed = jnp.dot(grad_pre, dense_t, preferred_element_type=jnp.float32)
    scaled = as_float * inverse_rms
    leaving = (
        arriving.astype(jnp.float32)
        + inverse_rms
        * (grad_normed - scaled * jnp.mean(grad_normed * scaled, axis=-1, keepdims=True))
    ).astype(jnp.bfloat16)
    return (leaving, grad_pre)


def local(x_in, cotangent, weights, live_rows, moment, second):
    sections = lax.axis_size("pipe")
    section_index = lax.axis_index("pipe")
    micro_count, tokens, features = x_in.shape
    column_count = live_rows.shape[1]
    live_count = live_rows.shape[2]
    own_columns = weights.shape[1]
    block_size = weights.shape[2]
    live_index = live_rows[0]
    section_weights = lax.all_gather(weights[0], "dp", axis=0, tiled=True)
    dense_t = expand_dense(section_weights, live_index)
    tick_count = micro_count + sections - 1

    incoming = jnp.zeros((tokens, features), jnp.bfloat16)
    kept_in, kept_normed, kept_pre = [], [], []
    for tick_index in range(tick_count):
        entering = jnp.where(section_index == 0, x_in[min(tick_index, micro_count - 1)], incoming)
        outgoing, normed, pre_act = layer_forward(entering, dense_t)
        kept_in.append(entering)
        kept_normed.append(normed)
        kept_pre.append(pre_act)
        if tick_index + 1 < tick_count:
            incoming = shifted(outgoing, "pipe", 1)
    saved_in = lax.dynamic_slice_in_dim(jnp.stack(kept_in), section_index, micro_count, 0)
    saved_normed = lax.dynamic_slice_in_dim(jnp.stack(kept_normed), section_index, micro_count, 0)
    saved_pre = lax.dynamic_slice_in_dim(jnp.stack(kept_pre), section_index, micro_count, 0)

    incoming_grad = jnp.zeros((tokens, features), jnp.bfloat16)
    kept_grad = []
    for tick_index in range(tick_count):
        slot_index = jnp.clip(tick_index - (sections - 1 - section_index), 0, micro_count - 1)
        arriving = jnp.where(
            section_index == sections - 1,
            cotangent[min(tick_index, micro_count - 1)],
            incoming_grad,
        )
        leaving, grad_pre = layer_backward(
            arriving, saved_in[slot_index], saved_pre[slot_index], dense_t
        )
        kept_grad.append(grad_pre)
        if tick_index + 1 < tick_count:
            incoming_grad = shifted(leaving, "pipe", -1)
    saved_grad = lax.dynamic_slice_in_dim(
        jnp.stack(kept_grad), sections - 1 - section_index, micro_count, 0
    )

    all_rows = micro_count * tokens
    inverse_tokens = 1.0 / (all_rows * lax.axis_size("dp"))
    dense_grad = (
        lax.dot_general(
            saved_grad.reshape(all_rows, features),
            saved_normed.reshape(all_rows, features),
            (((0,), (0,)), ((), ())),
            preferred_element_type=jnp.float32,
        )
        * inverse_tokens
    ).astype(jnp.bfloat16)
    partial = pack_dense(dense_grad, live_index)
    gradient = lax.psum_scatter(partial, "dp", scatter_dimension=0, tiled=True).astype(jnp.float32)

    rate = 0.1 / math.sqrt(live_count * block_size)
    moment_new = 0.9 * moment[0] + 0.1 * gradient
    second_new = 0.95 * second[0] + 0.05 * gradient * gradient
    stepped = weights[0].astype(jnp.float32) - rate * moment_new / (jnp.sqrt(second_new) + 1e-08)
    own_index = lax.dynamic_slice_in_dim(
        live_index, lax.axis_index("dp") * own_columns, own_columns, 0
    )
    blocked = stepped.reshape(own_columns, block_size, live_count, block_size)
    magnitude = jnp.sqrt(jnp.sum(blocked * blocked, axis=(1, 3)))
    leafed = (
        blocked * shrink(magnitude, 0.15 * math.sqrt(block_size / live_count))[:, None, :, None]
    )
    block_squares = jnp.sum(leafed * leafed, axis=(1, 3))
    head_count = features // HEAD
    head_index = own_index // (HEAD // block_size)
    onehot = (
        head_index[:, :, None] == jnp.arange(head_count, dtype=jnp.int32)[None, None, :]
    ).astype(jnp.float32)
    head_squares = lax.psum(jnp.sum(onehot * block_squares[:, :, None], axis=(0, 1)), "dp")
    head_factor = shrink(jnp.sqrt(head_squares), 0.45 * math.sqrt(HEAD))
    headed = leafed * jnp.sum(onehot * head_factor[None, None, :], axis=2)[:, None, :, None]
    layer_squares = jnp.sum(head_factor * head_factor * head_squares)
    layer_factor = shrink(jnp.sqrt(layer_squares), 0.45 * math.sqrt(features))
    weights_out = (
        (headed * layer_factor)
        .astype(jnp.bfloat16)
        .reshape(own_columns, block_size, live_count * block_size)
    )
    return (weights_out[None], moment_new[None], second_new[None])


def solution(mesh):
    placed = (
        P(None, "dp", None),
        P(None, "dp", None),
        P("pipe", "dp", None, None),
        P("pipe", None, None),
        P("pipe", "dp", None, None),
        P("pipe", "dp", None, None),
    )
    return jax.shard_map(
        local,
        mesh=mesh,
        in_specs=placed,
        out_specs=(
            P("pipe", "dp", None, None),
            P("pipe", "dp", None, None),
            P("pipe", "dp", None, None),
        ),
        check_vma=False,
    )
```

```python
import math

import jax
import jax.numpy as jnp
from jax import lax
from jax.experimental import pallas as pl
from jax.experimental.pallas import tpu as pltpu
from jax.sharding import PartitionSpec as P

HEAD = 128


def shifted(value, axis, steps):
    count = lax.axis_size(axis)
    leading, last = (max(0, -steps), min(count, count - steps))
    return lax.ppermute(value, axis, [(source, source + steps) for source in range(leading, last)])


def shrink(magnitude, threshold):
    return jnp.maximum(magnitude - threshold, 0.0) / jnp.maximum(magnitude, threshold)


def pick_half(tile, index, want_odd):
    rolled = pltpu.roll(tile, 64, 1)
    keep = (index % 2) == want_odd
    return jnp.where(keep, tile, rolled)


def expand_kernel(table_ref, w_ref, o_ref):
    j = pl.program_id(0)
    rows = w_ref.shape[1]
    lane = lax.broadcasted_iota(jnp.int32, (rows, 128), 1)
    pairs = o_ref.shape[2] // 128
    for p in range(pairs):
        k0 = table_ref[j * 2 * pairs + 2 * p]
        k1 = table_ref[j * 2 * pairs + 2 * p + 1]
        s0 = pl.multiple_of((jnp.maximum(k0, 0) // 2) * 128, 128)
        s1 = pl.multiple_of((jnp.maximum(k1, 0) // 2) * 128, 128)
        t0 = w_ref[0, :, pl.ds(s0, 128)]
        t1 = w_ref[0, :, pl.ds(s1, 128)]
        zero = jnp.zeros_like(t0)
        low = jnp.where(k0 >= 0, pick_half(t0, k0, 0), zero)
        high = jnp.where(k1 >= 0, pick_half(t1, k1, 1), zero)
        o_ref[0, :, p * 128:(p + 1) * 128] = jnp.where(lane < 64, low, high)


def pack_kernel(table_ref, g_ref, o_ref):
    j = pl.program_id(0)
    rows = g_ref.shape[1]
    lane = lax.broadcasted_iota(jnp.int32, (rows, 128), 1)
    pairs = o_ref.shape[2] // 128
    for q in range(pairs):
        r0 = table_ref[j * 2 * pairs + 2 * q]
        r1 = table_ref[j * 2 * pairs + 2 * q + 1]
        s0 = pl.multiple_of((r0 // 2) * 128, 128)
        s1 = pl.multiple_of((r1 // 2) * 128, 128)
        t0 = g_ref[0, :, pl.ds(s0, 128)]
        t1 = g_ref[0, :, pl.ds(s1, 128)]
        low = pick_half(t0, r0, 0)
        high = pick_half(t1, r1, 1)
        o_ref[0, :, q * 128:(q + 1) * 128] = jnp.where(lane < 64, low, high)


def expand_dense(section_weights, live_index):
    column_count, block_size, wide = section_weights.shape
    live_count = live_index.shape[1]
    features = column_count * block_size
    targets = jnp.arange(column_count, dtype=jnp.int32)
    hit = live_index[:, :, None] == targets[None, None, :]
    k_ids = jnp.arange(live_count, dtype=jnp.int32)[None, :, None]
    inverse = jnp.where(
        jnp.any(hit, axis=1), jnp.sum(jnp.where(hit, k_ids, 0), axis=1), -1
    ).astype(jnp.int32)
    out = pl.pallas_call(
        expand_kernel,
        out_shape=jax.ShapeDtypeStruct((column_count, block_size, features), section_weights.dtype),
        grid_spec=pltpu.PrefetchScalarGridSpec(
            num_scalar_prefetch=1,
            grid=(column_count,),
            in_specs=[pl.BlockSpec((1, block_size, wide), lambda j, tbl: (j, 0, 0))],
            out_specs=pl.BlockSpec((1, block_size, features), lambda j, tbl: (j, 0, 0)),
        ),
        cost_estimate=pl.CostEstimate(
            flops=0, transcendentals=0, bytes_accessed=3 * column_count * block_size * wide * 2
        ),
    )(inverse.reshape(-1), section_weights)
    return out.reshape(features, features)


def pack_dense(dense_grad, live_index):
    column_count, live_count = live_index.shape
    features = dense_grad.shape[0]
    block_size = features // column_count
    wide = live_count * block_size
    return pl.pallas_call(
        pack_kernel,
        out_shape=jax.ShapeDtypeStruct((column_count, block_size, wide), dense_grad.dtype),
        grid_spec=pltpu.PrefetchScalarGridSpec(
            num_scalar_prefetch=1,
            grid=(column_count,),
            in_specs=[pl.BlockSpec((1, block_size, features), lambda j, tbl: (j, 0, 0))],
            out_specs=pl.BlockSpec((1, block_size, wide), lambda j, tbl: (j, 0, 0)),
        ),
        cost_estimate=pl.CostEstimate(
            flops=0, transcendentals=0, bytes_accessed=3 * column_count * block_size * wide * 2
        ),
    )(live_index.reshape(-1).astype(jnp.int32), dense_grad.reshape(column_count, block_size, features))


def spread_kernel(x_ref, o_ref, recv_ref, send_sem, recv_sem):
    count = recv_ref.shape[0]
    me = lax.axis_index("dp")
    pipe = lax.axis_index("pipe")
    barrier = pltpu.get_barrier_semaphore()
    for step in range(1, count):
        peer = lax.rem(me + step, count)
        pl.semaphore_signal(barrier, inc=1, device_id=(pipe, peer), device_id_type=pl.DeviceIdType.MESH)
    pl.semaphore_wait(barrier, count - 1)
    copies = []
    for step in range(1, count):
        peer = lax.rem(me + step, count)
        copy = pltpu.make_async_remote_copy(
            src_ref=x_ref,
            dst_ref=recv_ref.at[me],
            send_sem=send_sem.at[step],
            recv_sem=recv_sem.at[me],
            device_id=(pipe, peer),
            device_id_type=pl.DeviceIdType.MESH,
        )
        copy.start()
        copies.append(copy)
    total = x_ref[...]
    for step in range(1, count):
        source = lax.rem(me + count - step, count)
        arrival = pltpu.make_async_remote_copy(
            src_ref=x_ref,
            dst_ref=recv_ref.at[source],
            send_sem=send_sem.at[step],
            recv_sem=recv_sem.at[source],
            device_id=(pipe, source),
            device_id_type=pl.DeviceIdType.MESH,
        )
        arrival.wait_recv()
        total = total + recv_ref[source]
    for copy in copies:
        copy.wait_send()
    o_ref[...] = total


def spread_sum(values):
    count = lax.axis_size("dp")
    padded = jnp.zeros((8, 128), jnp.float32).at[0, : values.shape[0]].set(values)
    out = pl.pallas_call(
        spread_kernel,
        out_shape=jax.ShapeDtypeStruct((8, 128), jnp.float32),
        in_specs=[pl.BlockSpec(memory_space=pltpu.VMEM)],
        out_specs=pl.BlockSpec(memory_space=pltpu.VMEM),
        scratch_shapes=[
            pltpu.VMEM((count, 8, 128), jnp.float32),
            pltpu.SemaphoreType.DMA((count,)),
            pltpu.SemaphoreType.DMA((count,)),
        ],
        compiler_params=pltpu.CompilerParams(collective_id=0, has_side_effects=True),
    )(padded)
    return out[0, : values.shape[0]]


def layer_forward(entering, dense_t):
    as_float = entering.astype(jnp.float32)
    inverse_rms = lax.rsqrt(jnp.mean(as_float * as_float, axis=-1, keepdims=True) + 1e-05)
    normed = (as_float * inverse_rms).astype(jnp.bfloat16)
    pre_act = lax.dot_general(
        normed, dense_t, (((1,), (1,)), ((), ())), preferred_element_type=jnp.float32
    )
    return ((as_float + jax.nn.silu(pre_act)).astype(jnp.bfloat16), normed, pre_act)


def layer_backward(arriving, entering, pre_act, dense_t):
    as_float = entering.astype(jnp.float32)
    inverse_rms = lax.rsqrt(jnp.mean(as_float * as_float, axis=-1, keepdims=True) + 1e-05)
    sigmoid_z = jax.nn.sigmoid(pre_act)
    grad_pre = (
        arriving.astype(jnp.float32) * (sigmoid_z * (1.0 + pre_act * (1.0 - sigmoid_z)))
    ).astype(jnp.bfloat16)
    grad_normed = jnp.dot(grad_pre, dense_t, preferred_element_type=jnp.float32)
    scaled = as_float * inverse_rms
    leaving = (
        arriving.astype(jnp.float32)
        + inverse_rms
        * (grad_normed - scaled * jnp.mean(grad_normed * scaled, axis=-1, keepdims=True))
    ).astype(jnp.bfloat16)
    return (leaving, grad_pre)


def local(x_in, cotangent, weights, live_rows, moment, second):
    sections = lax.axis_size("pipe")
    section_index = lax.axis_index("pipe")
    micro_count, tokens, features = x_in.shape
    column_count = live_rows.shape[1]
    live_count = live_rows.shape[2]
    own_columns = weights.shape[1]
    block_size = weights.shape[2]
    live_index = live_rows[0]
    section_weights = lax.all_gather(weights[0], "dp", axis=0, tiled=True)
    dense_t = expand_dense(section_weights, live_index)
    tick_count = micro_count + sections - 1

    incoming = jnp.zeros((tokens, features), jnp.bfloat16)
    kept_in, kept_normed, kept_pre = [], [], []
    for tick_index in range(tick_count):
        entering = jnp.where(section_index == 0, x_in[min(tick_index, micro_count - 1)], incoming)
        outgoing, normed, pre_act = layer_forward(entering, dense_t)
        kept_in.append(entering)
        kept_normed.append(normed)
        kept_pre.append(pre_act)
        if tick_index + 1 < tick_count:
            incoming = shifted(outgoing, "pipe", 1)
    saved_in = lax.dynamic_slice_in_dim(jnp.stack(kept_in), section_index, micro_count, 0)
    saved_normed = lax.dynamic_slice_in_dim(jnp.stack(kept_normed), section_index, micro_count, 0)
    saved_pre = lax.dynamic_slice_in_dim(jnp.stack(kept_pre), section_index, micro_count, 0)

    incoming_grad = jnp.zeros((tokens, features), jnp.bfloat16)
    kept_grad = []
    for tick_index in range(tick_count):
        slot_index = jnp.clip(tick_index - (sections - 1 - section_index), 0, micro_count - 1)
        arriving = jnp.where(
            section_index == sections - 1,
            cotangent[min(tick_index, micro_count - 1)],
            incoming_grad,
        )
        leaving, grad_pre = layer_backward(
            arriving, saved_in[slot_index], saved_pre[slot_index], dense_t
        )
        kept_grad.append(grad_pre)
        if tick_index + 1 < tick_count:
            incoming_grad = shifted(leaving, "pipe", -1)
    saved_grad = lax.dynamic_slice_in_dim(
        jnp.stack(kept_grad), sections - 1 - section_index, micro_count, 0
    )

    all_rows = micro_count * tokens
    inverse_tokens = 1.0 / (all_rows * lax.axis_size("dp"))
    dense_grad = (
        lax.dot_general(
            saved_grad.reshape(all_rows, features),
            saved_normed.reshape(all_rows, features),
            (((0,), (0,)), ((), ())),
            preferred_element_type=jnp.float32,
        )
        * inverse_tokens
    ).astype(jnp.bfloat16)
    partial = pack_dense(dense_grad, live_index)
    gradient = lax.psum_scatter(partial, "dp", scatter_dimension=0, tiled=True).astype(jnp.float32)

    rate = 0.1 / math.sqrt(live_count * block_size)
    moment_new = 0.9 * moment[0] + 0.1 * gradient
    second_new = 0.95 * second[0] + 0.05 * gradient * gradient
    stepped = weights[0].astype(jnp.float32) - rate * moment_new / (jnp.sqrt(second_new) + 1e-08)
    own_index = lax.dynamic_slice_in_dim(
        live_index, lax.axis_index("dp") * own_columns, own_columns, 0
    )
    blocked = stepped.reshape(own_columns, block_size, live_count, block_size)
    magnitude = jnp.sqrt(jnp.sum(blocked * blocked, axis=(1, 3)))
    leafed = (
        blocked * shrink(magnitude, 0.15 * math.sqrt(block_size / live_count))[:, None, :, None]
    )
    block_squares = jnp.sum(leafed * leafed, axis=(1, 3))
    head_count = features // HEAD
    head_index = own_index // (HEAD // block_size)
    onehot = (
        head_index[:, :, None] == jnp.arange(head_count, dtype=jnp.int32)[None, None, :]
    ).astype(jnp.float32)
    head_partial = jnp.sum(onehot * block_squares[:, :, None], axis=(0, 1))
    head_squares = spread_sum(head_partial)
    head_factor = shrink(jnp.sqrt(head_squares), 0.45 * math.sqrt(HEAD))
    headed = leafed * jnp.sum(onehot * head_factor[None, None, :], axis=2)[:, None, :, None]
    layer_squares = jnp.sum(head_factor * head_factor * head_squares)
    layer_factor = shrink(jnp.sqrt(layer_squares), 0.45 * math.sqrt(features))
    weights_out = (
        (headed * layer_factor)
        .astype(jnp.bfloat16)
        .reshape(own_columns, block_size, live_count * block_size)
    )
    return (weights_out[None], moment_new[None], second_new[None])


def solution(mesh):
    placed = (
        P(None, "dp", None),
        P(None, "dp", None),
        P("pipe", "dp", None, None),
        P("pipe", None, None),
        P("pipe", "dp", None, None),
        P("pipe", "dp", None, None),
    )
    return jax.shard_map(
        local,
        mesh=mesh,
        in_specs=placed,
        out_specs=(
            P("pipe", "dp", None, None),
            P("pipe", "dp", None, None),
            P("pipe", "dp", None, None),
        ),
        check_vma=False,
    )
```

```python
import math

import jax
import jax.numpy as jnp
from jax import lax
from jax.experimental import pallas as pl
from jax.experimental.pallas import tpu as pltpu
from jax.sharding import PartitionSpec as P

HEAD = 128


def shifted(value, axis, steps):
    count = lax.axis_size(axis)
    leading, last = (max(0, -steps), min(count, count - steps))
    return lax.ppermute(value, axis, [(source, source + steps) for source in range(leading, last)])


def shrink(magnitude, threshold):
    return jnp.maximum(magnitude - threshold, 0.0) / jnp.maximum(magnitude, threshold)


def pick_half(tile, index, want_odd):
    rolled = pltpu.roll(tile, 64, 1)
    keep = (index % 2) == want_odd
    return jnp.where(keep, tile, rolled)


def expand_kernel(table_ref, w_ref, o_ref):
    j = pl.program_id(0)
    rows = w_ref.shape[1]
    lane = lax.broadcasted_iota(jnp.int32, (rows, 128), 1)
    pairs = o_ref.shape[2] // 128
    for p in range(pairs):
        k0 = table_ref[j * 2 * pairs + 2 * p]
        k1 = table_ref[j * 2 * pairs + 2 * p + 1]
        s0 = pl.multiple_of((jnp.maximum(k0, 0) // 2) * 128, 128)
        s1 = pl.multiple_of((jnp.maximum(k1, 0) // 2) * 128, 128)
        t0 = w_ref[0, :, pl.ds(s0, 128)]
        t1 = w_ref[0, :, pl.ds(s1, 128)]
        zero = jnp.zeros_like(t0)
        low = jnp.where(k0 >= 0, pick_half(t0, k0, 0), zero)
        high = jnp.where(k1 >= 0, pick_half(t1, k1, 1), zero)
        o_ref[0, :, p * 128:(p + 1) * 128] = jnp.where(lane < 64, low, high)


def pack_kernel(table_ref, g_ref, o_ref):
    j = pl.program_id(0)
    rows = g_ref.shape[1]
    lane = lax.broadcasted_iota(jnp.int32, (rows, 128), 1)
    pairs = o_ref.shape[2] // 128
    for q in range(pairs):
        r0 = table_ref[j * 2 * pairs + 2 * q]
        r1 = table_ref[j * 2 * pairs + 2 * q + 1]
        s0 = pl.multiple_of((r0 // 2) * 128, 128)
        s1 = pl.multiple_of((r1 // 2) * 128, 128)
        t0 = g_ref[0, :, pl.ds(s0, 128)]
        t1 = g_ref[0, :, pl.ds(s1, 128)]
        low = pick_half(t0, r0, 0)
        high = pick_half(t1, r1, 1)
        o_ref[0, :, q * 128:(q + 1) * 128] = jnp.where(lane < 64, low, high)


def gathered_place(j, cores, chips, own):
    e = j % own
    device = j // own
    return ((device % cores) * chips + device // cores) * own + e


def expand_dense(section_weights, live_index, cores, chips, own):
    column_count, block_size, wide = section_weights.shape
    live_count = live_index.shape[1]
    features = column_count * block_size
    targets = jnp.arange(column_count, dtype=jnp.int32)
    hit = live_index[:, :, None] == targets[None, None, :]
    k_ids = jnp.arange(live_count, dtype=jnp.int32)[None, :, None]
    inverse = jnp.where(
        jnp.any(hit, axis=1), jnp.sum(jnp.where(hit, k_ids, 0), axis=1), -1
    ).astype(jnp.int32)
    out = pl.pallas_call(
        expand_kernel,
        out_shape=jax.ShapeDtypeStruct((column_count, block_size, features), section_weights.dtype),
        grid_spec=pltpu.PrefetchScalarGridSpec(
            num_scalar_prefetch=1,
            grid=(column_count,),
            in_specs=[
                pl.BlockSpec(
                    (1, block_size, wide),
                    lambda j, tbl: (gathered_place(j, cores, chips, own), 0, 0),
                )
            ],
            out_specs=pl.BlockSpec((1, block_size, features), lambda j, tbl: (j, 0, 0)),
        ),
        cost_estimate=pl.CostEstimate(
            flops=0, transcendentals=0, bytes_accessed=3 * column_count * block_size * wide * 2
        ),
    )(inverse.reshape(-1), section_weights)
    return out.reshape(features, features)


def pack_dense(dense_grad, live_index, cores, chips, own):
    column_count, live_count = live_index.shape
    features = dense_grad.shape[0]
    block_size = features // column_count
    wide = live_count * block_size
    return pl.pallas_call(
        pack_kernel,
        out_shape=jax.ShapeDtypeStruct((column_count, block_size, wide), dense_grad.dtype),
        grid_spec=pltpu.PrefetchScalarGridSpec(
            num_scalar_prefetch=1,
            grid=(column_count,),
            in_specs=[pl.BlockSpec((1, block_size, features), lambda j, tbl: (j, 0, 0))],
            out_specs=pl.BlockSpec(
                (1, block_size, wide), lambda j, tbl: (gathered_place(j, cores, chips, own), 0, 0)
            ),
        ),
        cost_estimate=pl.CostEstimate(
            flops=0, transcendentals=0, bytes_accessed=3 * column_count * block_size * wide * 2
        ),
    )(live_index.reshape(-1).astype(jnp.int32), dense_grad.reshape(column_count, block_size, features))


def spread_kernel(x_ref, o_ref, recv_ref, send_sem, recv_sem):
    count = recv_ref.shape[0]
    cores = lax.axis_size("core")
    me = lax.axis_index("chip") * cores + lax.axis_index("core")
    pipe = lax.axis_index("pipe")
    barrier = pltpu.get_barrier_semaphore()
    for step in range(1, count):
        peer = lax.rem(me + step, count)
        pl.semaphore_signal(barrier, inc=1, device_id=(pipe, peer // cores, peer % cores), device_id_type=pl.DeviceIdType.MESH)
    pl.semaphore_wait(barrier, count - 1)
    copies = []
    for step in range(1, count):
        peer = lax.rem(me + step, count)
        copy = pltpu.make_async_remote_copy(
            src_ref=x_ref,
            dst_ref=recv_ref.at[me],
            send_sem=send_sem.at[step],
            recv_sem=recv_sem.at[me],
            device_id=(pipe, peer // cores, peer % cores),
            device_id_type=pl.DeviceIdType.MESH,
        )
        copy.start()
        copies.append(copy)
    total = x_ref[...]
    for step in range(1, count):
        source = lax.rem(me + count - step, count)
        arrival = pltpu.make_async_remote_copy(
            src_ref=x_ref,
            dst_ref=recv_ref.at[source],
            send_sem=send_sem.at[step],
            recv_sem=recv_sem.at[source],
            device_id=(pipe, source // cores, source % cores),
            device_id_type=pl.DeviceIdType.MESH,
        )
        arrival.wait_recv()
        total = total + recv_ref[source]
    for copy in copies:
        copy.wait_send()
    o_ref[...] = total


def spread_sum(values):
    count = lax.axis_size("chip") * lax.axis_size("core")
    padded = jnp.zeros((8, 128), jnp.float32).at[0, : values.shape[0]].set(values)
    out = pl.pallas_call(
        spread_kernel,
        out_shape=jax.ShapeDtypeStruct((8, 128), jnp.float32),
        in_specs=[pl.BlockSpec(memory_space=pltpu.VMEM)],
        out_specs=pl.BlockSpec(memory_space=pltpu.VMEM),
        scratch_shapes=[
            pltpu.VMEM((count, 8, 128), jnp.float32),
            pltpu.SemaphoreType.DMA((count,)),
            pltpu.SemaphoreType.DMA((count,)),
        ],
        compiler_params=pltpu.CompilerParams(collective_id=0, has_side_effects=True),
    )(padded)
    return out[0, : values.shape[0]]


def layer_forward(entering, dense_t):
    as_float = entering.astype(jnp.float32)
    inverse_rms = lax.rsqrt(jnp.mean(as_float * as_float, axis=-1, keepdims=True) + 1e-05)
    normed = (as_float * inverse_rms).astype(jnp.bfloat16)
    pre_act = lax.dot_general(
        normed, dense_t, (((1,), (1,)), ((), ())), preferred_element_type=jnp.float32
    )
    return ((as_float + jax.nn.silu(pre_act)).astype(jnp.bfloat16), normed, pre_act)


def layer_backward(arriving, entering, pre_act, dense_t):
    as_float = entering.astype(jnp.float32)
    inverse_rms = lax.rsqrt(jnp.mean(as_float * as_float, axis=-1, keepdims=True) + 1e-05)
    sigmoid_z = jax.nn.sigmoid(pre_act)
    grad_pre = (
        arriving.astype(jnp.float32) * (sigmoid_z * (1.0 + pre_act * (1.0 - sigmoid_z)))
    ).astype(jnp.bfloat16)
    grad_normed = jnp.dot(grad_pre, dense_t, preferred_element_type=jnp.float32)
    scaled = as_float * inverse_rms
    leaving = (
        arriving.astype(jnp.float32)
        + inverse_rms
        * (grad_normed - scaled * jnp.mean(grad_normed * scaled, axis=-1, keepdims=True))
    ).astype(jnp.bfloat16)
    return (leaving, grad_pre)


def local(x_in, cotangent, weights, live_rows, moment, second):
    sections = lax.axis_size("pipe")
    section_index = lax.axis_index("pipe")
    micro_count, tokens, features = x_in.shape
    column_count = live_rows.shape[1]
    live_count = live_rows.shape[2]
    own_columns = weights.shape[1]
    block_size = weights.shape[2]
    live_index = live_rows[0]
    cores = lax.axis_size("core")
    chips = lax.axis_size("chip")
    dp_size = cores * chips
    dp_index = lax.axis_index("chip") * cores + lax.axis_index("core")
    section_weights = lax.all_gather(
        lax.all_gather(weights[0], "chip", axis=0, tiled=True), "core", axis=0, tiled=True
    )
    dense_t = expand_dense(section_weights, live_index, cores, chips, own_columns)
    tick_count = micro_count + sections - 1

    incoming = jnp.zeros((tokens, features), jnp.bfloat16)
    kept_in, kept_normed, kept_pre = [], [], []
    for tick_index in range(tick_count):
        entering = jnp.where(section_index == 0, x_in[min(tick_index, micro_count - 1)], incoming)
        outgoing, normed, pre_act = layer_forward(entering, dense_t)
        kept_in.append(entering)
        kept_normed.append(normed)
        kept_pre.append(pre_act)
        if tick_index + 1 < tick_count:
            incoming = shifted(outgoing, "pipe", 1)
    saved_in = lax.dynamic_slice_in_dim(jnp.stack(kept_in), section_index, micro_count, 0)
    saved_normed = lax.dynamic_slice_in_dim(jnp.stack(kept_normed), section_index, micro_count, 0)
    saved_pre = lax.dynamic_slice_in_dim(jnp.stack(kept_pre), section_index, micro_count, 0)

    incoming_grad = jnp.zeros((tokens, features), jnp.bfloat16)
    kept_grad = []
    for tick_index in range(tick_count):
        slot_index = jnp.clip(tick_index - (sections - 1 - section_index), 0, micro_count - 1)
        arriving = jnp.where(
            section_index == sections - 1,
            cotangent[min(tick_index, micro_count - 1)],
            incoming_grad,
        )
        leaving, grad_pre = layer_backward(
            arriving, saved_in[slot_index], saved_pre[slot_index], dense_t
        )
        kept_grad.append(grad_pre)
        if tick_index + 1 < tick_count:
            incoming_grad = shifted(leaving, "pipe", -1)
    saved_grad = lax.dynamic_slice_in_dim(
        jnp.stack(kept_grad), sections - 1 - section_index, micro_count, 0
    )

    all_rows = micro_count * tokens
    inverse_tokens = 1.0 / (all_rows * dp_size)
    dense_grad = (
        lax.dot_general(
            saved_grad.reshape(all_rows, features),
            saved_normed.reshape(all_rows, features),
            (((0,), (0,)), ((), ())),
            preferred_element_type=jnp.float32,
        )
        * inverse_tokens
    ).astype(jnp.bfloat16)
    partial = pack_dense(dense_grad, live_index, cores, chips, own_columns)
    gradient = lax.psum_scatter(
        lax.psum_scatter(partial, "core", scatter_dimension=0, tiled=True),
        "chip",
        scatter_dimension=0,
        tiled=True,
    ).astype(jnp.float32)

    rate = 0.1 / math.sqrt(live_count * block_size)
    moment_new = 0.9 * moment[0] + 0.1 * gradient
    second_new = 0.95 * second[0] + 0.05 * gradient * gradient
    stepped = weights[0].astype(jnp.float32) - rate * moment_new / (jnp.sqrt(second_new) + 1e-08)
    own_index = lax.dynamic_slice_in_dim(
        live_index, dp_index * own_columns, own_columns, 0
    )
    blocked = stepped.reshape(own_columns, block_size, live_count, block_size)
    magnitude = jnp.sqrt(jnp.sum(blocked * blocked, axis=(1, 3)))
    leafed = (
        blocked * shrink(magnitude, 0.15 * math.sqrt(block_size / live_count))[:, None, :, None]
    )
    block_squares = jnp.sum(leafed * leafed, axis=(1, 3))
    head_count = features // HEAD
    head_index = own_index // (HEAD // block_size)
    onehot = (
        head_index[:, :, None] == jnp.arange(head_count, dtype=jnp.int32)[None, None, :]
    ).astype(jnp.float32)
    head_partial = jnp.sum(onehot * block_squares[:, :, None], axis=(0, 1))
    head_squares = spread_sum(head_partial)
    head_factor = shrink(jnp.sqrt(head_squares), 0.45 * math.sqrt(HEAD))
    headed = leafed * jnp.sum(onehot * head_factor[None, None, :], axis=2)[:, None, :, None]
    layer_squares = jnp.sum(head_factor * head_factor * head_squares)
    layer_factor = shrink(jnp.sqrt(layer_squares), 0.45 * math.sqrt(features))
    weights_out = (
        (headed * layer_factor)
        .astype(jnp.bfloat16)
        .reshape(own_columns, block_size, live_count * block_size)
    )
    return (weights_out[None], moment_new[None], second_new[None])


def solution(mesh):
    pipe_size, dp_size = mesh.devices.shape
    split = jax.sharding.Mesh(
        mesh.devices.reshape(pipe_size, dp_size // 2, 2), ("pipe", "chip", "core")
    )
    dp = ("chip", "core")
    placed = (
        P(None, dp, None),
        P(None, dp, None),
        P("pipe", dp, None, None),
        P("pipe", None, None),
        P("pipe", dp, None, None),
        P("pipe", dp, None, None),
    )
    return jax.shard_map(
        local,
        mesh=split,
        in_specs=placed,
        out_specs=(
            P("pipe", dp, None, None),
            P("pipe", dp, None, None),
            P("pipe", dp, None, None),
        ),
        check_vma=False,
    )
```

```python
import math

import jax
import jax.numpy as jnp
from jax import lax
from jax.experimental import pallas as pl
from jax.experimental.pallas import tpu as pltpu
from jax.sharding import PartitionSpec as P

HEAD = 128


def shifted(value, axis, steps):
    count = lax.axis_size(axis)
    leading, last = (max(0, -steps), min(count, count - steps))
    return lax.ppermute(value, axis, [(source, source + steps) for source in range(leading, last)])


def shrink(magnitude, threshold):
    return jnp.maximum(magnitude - threshold, 0.0) / jnp.maximum(magnitude, threshold)


def expand_kernel(table_ref, t_ref, o_ref):
    p = pl.program_id(0)
    block = 64
    blocks = o_ref.shape[0] // block
    lane = lax.broadcasted_iota(jnp.int32, (block, o_ref.shape[1]), 1)
    for r in range(blocks):
        k0 = table_ref[(2 * p) * blocks + r]
        k1 = table_ref[(2 * p + 1) * blocks + r]
        s0 = pl.multiple_of(jnp.maximum(k0, 0) * block, block)
        s1 = pl.multiple_of(jnp.maximum(k1, 0) * block, block)
        t0 = t_ref[pl.ds(s0, block), :]
        t1 = t_ref[pl.ds(s1, block), :]
        zero = jnp.zeros_like(t0)
        t0 = jnp.where(k0 >= 0, t0, zero)
        t1 = jnp.where(k1 >= 0, t1, zero)
        o_ref[r * block:(r + 1) * block, :] = jnp.where(lane < block, t0, t1)


def pack_kernel(table_ref, g_ref, o_ref):
    p = pl.program_id(0)
    block = 64
    live_count = o_ref.shape[1] // block
    lane = lax.broadcasted_iota(jnp.int32, (block, o_ref.shape[2]), 1)
    for k in range(live_count):
        r0 = table_ref[(2 * p) * live_count + k]
        r1 = table_ref[(2 * p + 1) * live_count + k]
        s0 = pl.multiple_of(r0 * block, block)
        s1 = pl.multiple_of(r1 * block, block)
        t0 = g_ref[pl.ds(s0, block), :]
        t1 = g_ref[pl.ds(s1, block), :]
        o_ref[0, k * block:(k + 1) * block, :] = jnp.where(lane < block, t0, t1)


def expand_dense(paired_weights, live_index):
    pair_count, wide, two_blocks = paired_weights.shape
    column_count, live_count = live_index.shape
    block_size = two_blocks // 2
    features = column_count * block_size
    targets = jnp.arange(column_count, dtype=jnp.int32)
    hit = live_index[:, :, None] == targets[None, None, :]
    k_ids = jnp.arange(live_count, dtype=jnp.int32)[None, :, None]
    inverse = jnp.where(
        jnp.any(hit, axis=1), jnp.sum(jnp.where(hit, k_ids, 0), axis=1), -1
    ).astype(jnp.int32)
    return pl.pallas_call(
        expand_kernel,
        out_shape=jax.ShapeDtypeStruct((features, features), paired_weights.dtype),
        grid_spec=pltpu.PrefetchScalarGridSpec(
            num_scalar_prefetch=1,
            grid=(pair_count,),
            in_specs=[pl.BlockSpec((None, wide, two_blocks), lambda p, tbl: (p, 0, 0))],
            out_specs=pl.BlockSpec((features, two_blocks), lambda p, tbl: (0, p)),
        ),
        cost_estimate=pl.CostEstimate(
            flops=0, transcendentals=0, bytes_accessed=3 * pair_count * wide * two_blocks * 2
        ),
    )(inverse.reshape(-1), paired_weights)


def pack_dense(dense_grad, live_index):
    column_count, live_count = live_index.shape
    features = dense_grad.shape[0]
    block_size = features // column_count
    wide = live_count * block_size
    pair_count = column_count // 2
    return pl.pallas_call(
        pack_kernel,
        out_shape=jax.ShapeDtypeStruct((pair_count, wide, 2 * block_size), dense_grad.dtype),
        grid_spec=pltpu.PrefetchScalarGridSpec(
            num_scalar_prefetch=1,
            grid=(pair_count,),
            in_specs=[pl.BlockSpec((features, 2 * block_size), lambda p, tbl: (0, p))],
            out_specs=pl.BlockSpec((1, wide, 2 * block_size), lambda p, tbl: (p, 0, 0)),
        ),
        cost_estimate=pl.CostEstimate(
            flops=0, transcendentals=0, bytes_accessed=3 * pair_count * wide * 2 * block_size * 2
        ),
    )(live_index.reshape(-1).astype(jnp.int32), dense_grad)


def spread_kernel(x_ref, o_ref, recv_ref, send_sem, recv_sem):
    count = recv_ref.shape[0]
    me = lax.axis_index("dp")
    pipe = lax.axis_index("pipe")
    barrier = pltpu.get_barrier_semaphore()
    for step in range(1, count):
        peer = lax.rem(me + step, count)
        pl.semaphore_signal(barrier, inc=1, device_id=(pipe, peer), device_id_type=pl.DeviceIdType.MESH)
    pl.semaphore_wait(barrier, count - 1)
    copies = []
    for step in range(1, count):
        peer = lax.rem(me + step, count)
        copy = pltpu.make_async_remote_copy(
            src_ref=x_ref,
            dst_ref=recv_ref.at[me],
            send_sem=send_sem.at[step],
            recv_sem=recv_sem.at[me],
            device_id=(pipe, peer),
            device_id_type=pl.DeviceIdType.MESH,
        )
        copy.start()
        copies.append(copy)
    total = x_ref[...]
    for step in range(1, count):
        source = lax.rem(me + count - step, count)
        arrival = pltpu.make_async_remote_copy(
            src_ref=x_ref,
            dst_ref=recv_ref.at[source],
            send_sem=send_sem.at[step],
            recv_sem=recv_sem.at[source],
            device_id=(pipe, source),
            device_id_type=pl.DeviceIdType.MESH,
        )
        arrival.wait_recv()
        total = total + recv_ref[source]
    for copy in copies:
        copy.wait_send()
    o_ref[...] = total


def spread_sum(values):
    count = lax.axis_size("dp")
    padded = jnp.zeros((8, 128), jnp.float32).at[0, : values.shape[0]].set(values)
    out = pl.pallas_call(
        spread_kernel,
        out_shape=jax.ShapeDtypeStruct((8, 128), jnp.float32),
        in_specs=[pl.BlockSpec(memory_space=pltpu.VMEM)],
        out_specs=pl.BlockSpec(memory_space=pltpu.VMEM),
        scratch_shapes=[
            pltpu.VMEM((count, 8, 128), jnp.float32),
            pltpu.SemaphoreType.DMA((count,)),
            pltpu.SemaphoreType.DMA((count,)),
        ],
        compiler_params=pltpu.CompilerParams(collective_id=0, has_side_effects=True),
    )(padded)
    return out[0, : values.shape[0]]


def layer_forward(entering, dense_w):
    as_float = entering.astype(jnp.float32)
    inverse_rms = lax.rsqrt(jnp.mean(as_float * as_float, axis=-1, keepdims=True) + 1e-05)
    normed = (as_float * inverse_rms).astype(jnp.bfloat16)
    pre_act = jnp.dot(normed, dense_w, preferred_element_type=jnp.float32)
    return ((as_float + jax.nn.silu(pre_act)).astype(jnp.bfloat16), normed, pre_act)


def layer_backward(arriving, entering, pre_act, dense_w):
    as_float = entering.astype(jnp.float32)
    inverse_rms = lax.rsqrt(jnp.mean(as_float * as_float, axis=-1, keepdims=True) + 1e-05)
    sigmoid_z = jax.nn.sigmoid(pre_act)
    grad_pre = (
        arriving.astype(jnp.float32) * (sigmoid_z * (1.0 + pre_act * (1.0 - sigmoid_z)))
    ).astype(jnp.bfloat16)
    grad_normed = lax.dot_general(
        grad_pre, dense_w, (((1,), (1,)), ((), ())), preferred_element_type=jnp.float32
    )
    scaled = as_float * inverse_rms
    leaving = (
        arriving.astype(jnp.float32)
        + inverse_rms
        * (grad_normed - scaled * jnp.mean(grad_normed * scaled, axis=-1, keepdims=True))
    ).astype(jnp.bfloat16)
    return (leaving, grad_pre)


def local(x_in, cotangent, weights, live_rows, moment, second):
    sections = lax.axis_size("pipe")
    section_index = lax.axis_index("pipe")
    micro_count, tokens, features = x_in.shape
    column_count = live_rows.shape[1]
    live_count = live_rows.shape[2]
    own_columns = weights.shape[1]
    block_size = weights.shape[2]
    live_index = live_rows[0]
    own_pair = weights[0].transpose(2, 0, 1).reshape(1, live_count * block_size, own_columns * block_size)
    paired_weights = lax.all_gather(own_pair, "dp", axis=0, tiled=True)
    dense_w = expand_dense(paired_weights, live_index)
    tick_count = micro_count + sections - 1

    incoming = jnp.zeros((tokens, features), jnp.bfloat16)
    kept_in, kept_normed, kept_pre = [], [], []
    for tick_index in range(tick_count):
        entering = jnp.where(section_index == 0, x_in[min(tick_index, micro_count - 1)], incoming)
        outgoing, normed, pre_act = layer_forward(entering, dense_w)
        kept_in.append(entering)
        kept_normed.append(normed)
        kept_pre.append(pre_act)
        if tick_index + 1 < tick_count:
            incoming = shifted(outgoing, "pipe", 1)
    saved_in = lax.dynamic_slice_in_dim(jnp.stack(kept_in), section_index, micro_count, 0)
    saved_normed = lax.dynamic_slice_in_dim(jnp.stack(kept_normed), section_index, micro_count, 0)
    saved_pre = lax.dynamic_slice_in_dim(jnp.stack(kept_pre), section_index, micro_count, 0)

    incoming_grad = jnp.zeros((tokens, features), jnp.bfloat16)
    kept_grad = []
    for tick_index in range(tick_count):
        slot_index = jnp.clip(tick_index - (sections - 1 - section_index), 0, micro_count - 1)
        arriving = jnp.where(
            section_index == sections - 1,
            cotangent[min(tick_index, micro_count - 1)],
            incoming_grad,
        )
        leaving, grad_pre = layer_backward(
            arriving, saved_in[slot_index], saved_pre[slot_index], dense_w
        )
        kept_grad.append(grad_pre)
        if tick_index + 1 < tick_count:
            incoming_grad = shifted(leaving, "pipe", -1)
    saved_grad = lax.dynamic_slice_in_dim(
        jnp.stack(kept_grad), sections - 1 - section_index, micro_count, 0
    )

    all_rows = micro_count * tokens
    inverse_tokens = 1.0 / (all_rows * lax.axis_size("dp"))
    dense_grad = (
        lax.dot_general(
            saved_normed.reshape(all_rows, features),
            saved_grad.reshape(all_rows, features),
            (((0,), (0,)), ((), ())),
            preferred_element_type=jnp.float32,
        )
        * inverse_tokens
    ).astype(jnp.bfloat16)
    partial = pack_dense(dense_grad, live_index)
    own_grad = lax.psum_scatter(partial, "dp", scatter_dimension=0, tiled=True)
    gradient = (
        own_grad.reshape(live_count * block_size, own_columns, block_size)
        .transpose(1, 2, 0)
        .astype(jnp.float32)
    )

    rate = 0.1 / math.sqrt(live_count * block_size)
    moment_new = 0.9 * moment[0] + 0.1 * gradient
    second_new = 0.95 * second[0] + 0.05 * gradient * gradient
    stepped = weights[0].astype(jnp.float32) - rate * moment_new / (jnp.sqrt(second_new) + 1e-08)
    own_index = lax.dynamic_slice_in_dim(
        live_index, lax.axis_index("dp") * own_columns, own_columns, 0
    )
    blocked = stepped.reshape(own_columns, block_size, live_count, block_size)
    magnitude = jnp.sqrt(jnp.sum(blocked * blocked, axis=(1, 3)))
    leafed = (
        blocked * shrink(magnitude, 0.15 * math.sqrt(block_size / live_count))[:, None, :, None]
    )
    block_squares = jnp.sum(leafed * leafed, axis=(1, 3))
    head_count = features // HEAD
    head_index = own_index // (HEAD // block_size)
    onehot = (
        head_index[:, :, None] == jnp.arange(head_count, dtype=jnp.int32)[None, None, :]
    ).astype(jnp.float32)
    head_partial = jnp.sum(onehot * block_squares[:, :, None], axis=(0, 1))
    head_squares = spread_sum(head_partial)
    head_factor = shrink(jnp.sqrt(head_squares), 0.45 * math.sqrt(HEAD))
    headed = leafed * jnp.sum(onehot * head_factor[None, None, :], axis=2)[:, None, :, None]
    layer_squares = jnp.sum(head_factor * head_factor * head_squares)
    layer_factor = shrink(jnp.sqrt(layer_squares), 0.45 * math.sqrt(features))
    weights_out = (
        (headed * layer_factor)
        .astype(jnp.bfloat16)
        .reshape(own_columns, block_size, live_count * block_size)
    )
    return (weights_out[None], moment_new[None], second_new[None])


def solution(mesh):
    placed = (
        P(None, "dp", None),
        P(None, "dp", None),
        P("pipe", "dp", None, None),
        P("pipe", None, None),
        P("pipe", "dp", None, None),
        P("pipe", "dp", None, None),
    )
    return jax.shard_map(
        local,
        mesh=mesh,
        in_specs=placed,
        out_specs=(
            P("pipe", "dp", None, None),
            P("pipe", "dp", None, None),
            P("pipe", "dp", None, None),
        ),
        check_vma=False,
    )
```

```python
import math

import jax
import jax.numpy as jnp
from jax import lax
from jax.experimental import pallas as pl
from jax.experimental.pallas import tpu as pltpu
from jax.sharding import PartitionSpec as P

HEAD = 128


def shifted(value, axis, steps):
    count = lax.axis_size(axis)
    leading, last = (max(0, -steps), min(count, count - steps))
    return lax.ppermute(value, axis, [(source, source + steps) for source in range(leading, last)])


def shrink(magnitude, threshold):
    return jnp.maximum(magnitude - threshold, 0.0) / jnp.maximum(magnitude, threshold)


def expand_kernel(table_ref, t_ref, o_ref):
    p = pl.program_id(0)
    block = 64
    blocks = o_ref.shape[0] // block
    lane = lax.broadcasted_iota(jnp.int32, (block, o_ref.shape[1]), 1)
    for r in range(blocks):
        k0 = table_ref[(2 * p) * blocks + r]
        k1 = table_ref[(2 * p + 1) * blocks + r]
        s0 = pl.multiple_of(jnp.maximum(k0, 0) * block, block)
        s1 = pl.multiple_of(jnp.maximum(k1, 0) * block, block)
        t0 = t_ref[pl.ds(s0, block), :]
        t1 = t_ref[pl.ds(s1, block), :]
        zero = jnp.zeros_like(t0)
        t0 = jnp.where(k0 >= 0, t0, zero)
        t1 = jnp.where(k1 >= 0, t1, zero)
        o_ref[r * block:(r + 1) * block, :] = jnp.where(lane < block, t0, t1)


def pack_kernel(table_ref, g_ref, o_ref):
    p = pl.program_id(0)
    block = 64
    live_count = o_ref.shape[1] // block
    lane = lax.broadcasted_iota(jnp.int32, (block, o_ref.shape[2]), 1)
    for k in range(live_count):
        r0 = table_ref[(2 * p) * live_count + k]
        r1 = table_ref[(2 * p + 1) * live_count + k]
        s0 = pl.multiple_of(r0 * block, block)
        s1 = pl.multiple_of(r1 * block, block)
        t0 = g_ref[pl.ds(s0, block), :]
        t1 = g_ref[pl.ds(s1, block), :]
        o_ref[0, k * block:(k + 1) * block, :] = jnp.where(lane < block, t0, t1)


def expand_dense(paired_weights, live_index):
    pair_count, wide, two_blocks = paired_weights.shape
    column_count, live_count = live_index.shape
    block_size = two_blocks // 2
    features = column_count * block_size
    targets = jnp.arange(column_count, dtype=jnp.int32)
    hit = live_index[:, :, None] == targets[None, None, :]
    k_ids = jnp.arange(live_count, dtype=jnp.int32)[None, :, None]
    inverse = jnp.where(
        jnp.any(hit, axis=1), jnp.sum(jnp.where(hit, k_ids, 0), axis=1), -1
    ).astype(jnp.int32)
    return pl.pallas_call(
        expand_kernel,
        out_shape=jax.ShapeDtypeStruct((features, features), paired_weights.dtype),
        grid_spec=pltpu.PrefetchScalarGridSpec(
            num_scalar_prefetch=1,
            grid=(pair_count,),
            in_specs=[pl.BlockSpec((None, wide, two_blocks), lambda p, tbl: (p, 0, 0))],
            out_specs=pl.BlockSpec((features, two_blocks), lambda p, tbl: (0, p)),
        ),
        cost_estimate=pl.CostEstimate(
            flops=0, transcendentals=0, bytes_accessed=3 * pair_count * wide * two_blocks * 2
        ),
    )(inverse.reshape(-1), paired_weights)


def pack_dense(dense_grad, live_index):
    column_count, live_count = live_index.shape
    features = dense_grad.shape[0]
    block_size = features // column_count
    wide = live_count * block_size
    pair_count = column_count // 2
    return pl.pallas_call(
        pack_kernel,
        out_shape=jax.ShapeDtypeStruct((pair_count, wide, 2 * block_size), dense_grad.dtype),
        grid_spec=pltpu.PrefetchScalarGridSpec(
            num_scalar_prefetch=1,
            grid=(pair_count,),
            in_specs=[pl.BlockSpec((features, 2 * block_size), lambda p, tbl: (0, p))],
            out_specs=pl.BlockSpec((1, wide, 2 * block_size), lambda p, tbl: (p, 0, 0)),
        ),
        cost_estimate=pl.CostEstimate(
            flops=0, transcendentals=0, bytes_accessed=3 * pair_count * wide * 2 * block_size * 2
        ),
    )(live_index.reshape(-1).astype(jnp.int32), dense_grad)


def spread_kernel(x_ref, o_ref, recv_ref, send_sem, recv_sem):
    count = recv_ref.shape[0]
    me = lax.axis_index("dp")
    pipe = lax.axis_index("pipe")
    barrier = pltpu.get_barrier_semaphore()
    for step in range(1, count):
        peer = lax.rem(me + step, count)
        pl.semaphore_signal(barrier, inc=1, device_id=(pipe, peer), device_id_type=pl.DeviceIdType.MESH)
    pl.semaphore_wait(barrier, count - 1)
    copies = []
    for step in range(1, count):
        peer = lax.rem(me + step, count)
        copy = pltpu.make_async_remote_copy(
            src_ref=x_ref,
            dst_ref=recv_ref.at[me],
            send_sem=send_sem.at[step],
            recv_sem=recv_sem.at[me],
            device_id=(pipe, peer),
            device_id_type=pl.DeviceIdType.MESH,
        )
        copy.start()
        copies.append(copy)
    total = x_ref[...]
    for step in range(1, count):
        source = lax.rem(me + count - step, count)
        arrival = pltpu.make_async_remote_copy(
            src_ref=x_ref,
            dst_ref=recv_ref.at[source],
            send_sem=send_sem.at[step],
            recv_sem=recv_sem.at[source],
            device_id=(pipe, source),
            device_id_type=pl.DeviceIdType.MESH,
        )
        arrival.wait_recv()
        total = total + recv_ref[source]
    for copy in copies:
        copy.wait_send()
    o_ref[...] = total


def spread_sum(values):
    count = lax.axis_size("dp")
    padded = jnp.zeros((8, 128), jnp.float32).at[0, : values.shape[0]].set(values)
    out = pl.pallas_call(
        spread_kernel,
        out_shape=jax.ShapeDtypeStruct((8, 128), jnp.float32),
        in_specs=[pl.BlockSpec(memory_space=pltpu.VMEM)],
        out_specs=pl.BlockSpec(memory_space=pltpu.VMEM),
        scratch_shapes=[
            pltpu.VMEM((count, 8, 128), jnp.float32),
            pltpu.SemaphoreType.DMA((count,)),
            pltpu.SemaphoreType.DMA((count,)),
        ],
        compiler_params=pltpu.CompilerParams(collective_id=0, has_side_effects=True),
    )(padded)
    return out[0, : values.shape[0]]


def layer_forward(entering, dense_w):
    as_float = entering.astype(jnp.float32)
    inverse_rms = lax.rsqrt(jnp.mean(as_float * as_float, axis=-1, keepdims=True) + 1e-05)
    normed = (as_float * inverse_rms).astype(jnp.bfloat16)
    pre_act = jnp.dot(normed, dense_w, preferred_element_type=jnp.float32)
    return ((as_float + jax.nn.silu(pre_act)).astype(jnp.bfloat16), normed, pre_act)


def layer_backward(arriving, entering, pre_act, dense_w):
    as_float = entering.astype(jnp.float32)
    inverse_rms = lax.rsqrt(jnp.mean(as_float * as_float, axis=-1, keepdims=True) + 1e-05)
    sigmoid_z = jax.nn.sigmoid(pre_act)
    grad_pre = (
        arriving.astype(jnp.float32) * (sigmoid_z * (1.0 + pre_act * (1.0 - sigmoid_z)))
    ).astype(jnp.bfloat16)
    grad_normed = lax.dot_general(
        grad_pre, dense_w, (((1,), (1,)), ((), ())), preferred_element_type=jnp.float32
    )
    scaled = as_float * inverse_rms
    leaving = (
        arriving.astype(jnp.float32)
        + inverse_rms
        * (grad_normed - scaled * jnp.mean(grad_normed * scaled, axis=-1, keepdims=True))
    ).astype(jnp.bfloat16)
    return (leaving, grad_pre)


def local(x_in, cotangent, weights, live_rows, moment, second):
    sections = lax.axis_size("pipe")
    section_index = lax.axis_index("pipe")
    group = 2
    micro_total, micro_tokens, features = x_in.shape
    micro_count = micro_total // group
    tokens = micro_tokens * group
    x_in = x_in.reshape(micro_count, tokens, features)
    cotangent = cotangent.reshape(micro_count, tokens, features)
    column_count = live_rows.shape[1]
    live_count = live_rows.shape[2]
    own_columns = weights.shape[1]
    block_size = weights.shape[2]
    live_index = live_rows[0]
    own_pair = weights[0].transpose(2, 0, 1).reshape(1, live_count * block_size, own_columns * block_size)
    paired_weights = lax.all_gather(own_pair, "dp", axis=0, tiled=True)
    dense_w = expand_dense(paired_weights, live_index)
    tick_count = micro_count + sections - 1

    incoming = jnp.zeros((tokens, features), jnp.bfloat16)
    kept_in, kept_normed, kept_pre = [], [], []
    for tick_index in range(tick_count):
        entering = jnp.where(section_index == 0, x_in[min(tick_index, micro_count - 1)], incoming)
        outgoing, normed, pre_act = layer_forward(entering, dense_w)
        kept_in.append(entering)
        kept_normed.append(normed)
        kept_pre.append(pre_act)
        if tick_index + 1 < tick_count:
            incoming = shifted(outgoing, "pipe", 1)
    saved_in = lax.dynamic_slice_in_dim(jnp.stack(kept_in), section_index, micro_count, 0)
    saved_normed = lax.dynamic_slice_in_dim(jnp.stack(kept_normed), section_index, micro_count, 0)
    saved_pre = lax.dynamic_slice_in_dim(jnp.stack(kept_pre), section_index, micro_count, 0)

    incoming_grad = jnp.zeros((tokens, features), jnp.bfloat16)
    kept_grad = []
    for tick_index in range(tick_count):
        slot_index = jnp.clip(tick_index - (sections - 1 - section_index), 0, micro_count - 1)
        arriving = jnp.where(
            section_index == sections - 1,
            cotangent[min(tick_index, micro_count - 1)],
            incoming_grad,
        )
        leaving, grad_pre = layer_backward(
            arriving, saved_in[slot_index], saved_pre[slot_index], dense_w
        )
        kept_grad.append(grad_pre)
        if tick_index + 1 < tick_count:
            incoming_grad = shifted(leaving, "pipe", -1)
    saved_grad = lax.dynamic_slice_in_dim(
        jnp.stack(kept_grad), sections - 1 - section_index, micro_count, 0
    )

    all_rows = micro_count * tokens
    inverse_tokens = 1.0 / (all_rows * lax.axis_size("dp"))
    dense_grad = (
        lax.dot_general(
            saved_normed.reshape(all_rows, features),
            saved_grad.reshape(all_rows, features),
            (((0,), (0,)), ((), ())),
            preferred_element_type=jnp.float32,
        )
        * inverse_tokens
    ).astype(jnp.bfloat16)
    partial = pack_dense(dense_grad, live_index)
    own_grad = lax.psum_scatter(partial, "dp", scatter_dimension=0, tiled=True)
    gradient = (
        own_grad.reshape(live_count * block_size, own_columns, block_size)
        .transpose(1, 2, 0)
        .astype(jnp.float32)
    )

    rate = 0.1 / math.sqrt(live_count * block_size)
    moment_new = 0.9 * moment[0] + 0.1 * gradient
    second_new = 0.95 * second[0] + 0.05 * gradient * gradient
    stepped = weights[0].astype(jnp.float32) - rate * moment_new / (jnp.sqrt(second_new) + 1e-08)
    own_index = lax.dynamic_slice_in_dim(
        live_index, lax.axis_index("dp") * own_columns, own_columns, 0
    )
    blocked = stepped.reshape(own_columns, block_size, live_count, block_size)
    magnitude = jnp.sqrt(jnp.sum(blocked * blocked, axis=(1, 3)))
    leafed = (
        blocked * shrink(magnitude, 0.15 * math.sqrt(block_size / live_count))[:, None, :, None]
    )
    block_squares = jnp.sum(leafed * leafed, axis=(1, 3))
    head_count = features // HEAD
    head_index = own_index // (HEAD // block_size)
    onehot = (
        head_index[:, :, None] == jnp.arange(head_count, dtype=jnp.int32)[None, None, :]
    ).astype(jnp.float32)
    head_partial = jnp.sum(onehot * block_squares[:, :, None], axis=(0, 1))
    head_squares = spread_sum(head_partial)
    head_factor = shrink(jnp.sqrt(head_squares), 0.45 * math.sqrt(HEAD))
    headed = leafed * jnp.sum(onehot * head_factor[None, None, :], axis=2)[:, None, :, None]
    layer_squares = jnp.sum(head_factor * head_factor * head_squares)
    layer_factor = shrink(jnp.sqrt(layer_squares), 0.45 * math.sqrt(features))
    weights_out = (
        (headed * layer_factor)
        .astype(jnp.bfloat16)
        .reshape(own_columns, block_size, live_count * block_size)
    )
    return (weights_out[None], moment_new[None], second_new[None])


def solution(mesh):
    placed = (
        P(None, "dp", None),
        P(None, "dp", None),
        P("pipe", "dp", None, None),
        P("pipe", None, None),
        P("pipe", "dp", None, None),
        P("pipe", "dp", None, None),
    )
    return jax.shard_map(
        local,
        mesh=mesh,
        in_specs=placed,
        out_specs=(
            P("pipe", "dp", None, None),
            P("pipe", "dp", None, None),
            P("pipe", "dp", None, None),
        ),
        check_vma=False,
    )
```

```python
import functools
import math

import jax
import jax.numpy as jnp
from jax import lax
from jax.experimental import pallas as pl
from jax.experimental.pallas import tpu as pltpu
from jax.sharding import PartitionSpec as P

HEAD = 128


def shifted(value, axis, steps):
    count = lax.axis_size(axis)
    leading, last = (max(0, -steps), min(count, count - steps))
    return lax.ppermute(value, axis, [(source, source + steps) for source in range(leading, last)])


def shrink(magnitude, threshold):
    return jnp.maximum(magnitude - threshold, 0.0) / jnp.maximum(magnitude, threshold)


def expand_kernel(table_ref, t_ref, o_ref):
    p = pl.program_id(0)
    block = 64
    blocks = o_ref.shape[0] // block
    lane = lax.broadcasted_iota(jnp.int32, (block, o_ref.shape[1]), 1)

    def one_block(r, carry):
        k0 = table_ref[(2 * p) * blocks + r]
        k1 = table_ref[(2 * p + 1) * blocks + r]
        s0 = pl.multiple_of(jnp.maximum(k0, 0) * block, block)
        s1 = pl.multiple_of(jnp.maximum(k1, 0) * block, block)
        t0 = t_ref[pl.ds(s0, block), :]
        t1 = t_ref[pl.ds(s1, block), :]
        zero = jnp.zeros_like(t0)
        t0 = jnp.where(k0 >= 0, t0, zero)
        t1 = jnp.where(k1 >= 0, t1, zero)
        o_ref[pl.ds(pl.multiple_of(r * block, block), block), :] = jnp.where(lane < block, t0, t1)
        return carry

    lax.fori_loop(0, blocks, one_block, 0, unroll=4)


def pack_kernel(first_k, live_count, table_ref, g_ref, o_ref):
    p = pl.program_id(0)
    block = 64
    part_count = o_ref.shape[1] // block
    lane = lax.broadcasted_iota(jnp.int32, (block, o_ref.shape[2]), 1)

    def one_block(k, carry):
        r0 = table_ref[(2 * p) * live_count + first_k + k]
        r1 = table_ref[(2 * p + 1) * live_count + first_k + k]
        s0 = pl.multiple_of(r0 * block, block)
        s1 = pl.multiple_of(r1 * block, block)
        t0 = g_ref[pl.ds(s0, block), :]
        t1 = g_ref[pl.ds(s1, block), :]
        o_ref[0, pl.ds(pl.multiple_of(k * block, block), block), :] = jnp.where(lane < block, t0, t1)
        return carry

    lax.fori_loop(0, part_count, one_block, 0, unroll=4)


def expand_dense(paired_weights, live_index):
    pair_count, wide, two_blocks = paired_weights.shape
    column_count, live_count = live_index.shape
    block_size = two_blocks // 2
    features = column_count * block_size
    targets = jnp.arange(column_count, dtype=jnp.int32)
    hit = live_index[:, :, None] == targets[None, None, :]
    k_ids = jnp.arange(live_count, dtype=jnp.int32)[None, :, None]
    inverse = jnp.where(
        jnp.any(hit, axis=1), jnp.sum(jnp.where(hit, k_ids, 0), axis=1), -1
    ).astype(jnp.int32)
    return pl.pallas_call(
        expand_kernel,
        out_shape=jax.ShapeDtypeStruct((features, features), paired_weights.dtype),
        grid_spec=pltpu.PrefetchScalarGridSpec(
            num_scalar_prefetch=1,
            grid=(pair_count,),
            in_specs=[pl.BlockSpec((None, wide, two_blocks), lambda p, tbl: (p, 0, 0))],
            out_specs=pl.BlockSpec((features, two_blocks), lambda p, tbl: (0, p)),
        ),
        cost_estimate=pl.CostEstimate(
            flops=0, transcendentals=0, bytes_accessed=3 * pair_count * wide * two_blocks * 2
        ),
    )(inverse.reshape(-1), paired_weights)


def pack_dense(dense_grad, live_index, first_k, part_count):
    column_count, live_count = live_index.shape
    features = dense_grad.shape[0]
    block_size = features // column_count
    wide = part_count * block_size
    pair_count = column_count // 2
    return pl.pallas_call(
        functools.partial(pack_kernel, first_k, live_count),
        out_shape=jax.ShapeDtypeStruct((pair_count, wide, 2 * block_size), dense_grad.dtype),
        grid_spec=pltpu.PrefetchScalarGridSpec(
            num_scalar_prefetch=1,
            grid=(pair_count,),
            in_specs=[pl.BlockSpec((features, 2 * block_size), lambda p, tbl: (0, p))],
            out_specs=pl.BlockSpec((1, wide, 2 * block_size), lambda p, tbl: (p, 0, 0)),
        ),
        cost_estimate=pl.CostEstimate(
            flops=0, transcendentals=0, bytes_accessed=3 * pair_count * wide * 2 * block_size * 2
        ),
    )(live_index.reshape(-1).astype(jnp.int32), dense_grad)


def spread_kernel(x_ref, o_ref, recv_ref, send_sem, recv_sem):
    count = recv_ref.shape[0]
    me = lax.axis_index("dp")
    pipe = lax.axis_index("pipe")
    barrier = pltpu.get_barrier_semaphore()
    for step in range(1, count):
        peer = lax.rem(me + step, count)
        pl.semaphore_signal(barrier, inc=1, device_id=(pipe, peer), device_id_type=pl.DeviceIdType.MESH)
    pl.semaphore_wait(barrier, count - 1)
    copies = []
    for step in range(1, count):
        peer = lax.rem(me + step, count)
        copy = pltpu.make_async_remote_copy(
            src_ref=x_ref,
            dst_ref=recv_ref.at[me],
            send_sem=send_sem.at[step],
            recv_sem=recv_sem.at[me],
            device_id=(pipe, peer),
            device_id_type=pl.DeviceIdType.MESH,
        )
        copy.start()
        copies.append(copy)
    total = x_ref[...]
    for step in range(1, count):
        source = lax.rem(me + count - step, count)
        arrival = pltpu.make_async_remote_copy(
            src_ref=x_ref,
            dst_ref=recv_ref.at[source],
            send_sem=send_sem.at[step],
            recv_sem=recv_sem.at[source],
            device_id=(pipe, source),
            device_id_type=pl.DeviceIdType.MESH,
        )
        arrival.wait_recv()
        total = total + recv_ref[source]
    for copy in copies:
        copy.wait_send()
    o_ref[...] = total


def spread_sum(values):
    count = lax.axis_size("dp")
    padded = jnp.zeros((8, 128), jnp.float32).at[0, : values.shape[0]].set(values)
    out = pl.pallas_call(
        spread_kernel,
        out_shape=jax.ShapeDtypeStruct((8, 128), jnp.float32),
        in_specs=[pl.BlockSpec(memory_space=pltpu.VMEM)],
        out_specs=pl.BlockSpec(memory_space=pltpu.VMEM),
        scratch_shapes=[
            pltpu.VMEM((count, 8, 128), jnp.float32),
            pltpu.SemaphoreType.DMA((count,)),
            pltpu.SemaphoreType.DMA((count,)),
        ],
        compiler_params=pltpu.CompilerParams(collective_id=0, has_side_effects=True),
    )(padded)
    return out[0, : values.shape[0]]


def layer_forward(entering, dense_w):
    as_float = entering.astype(jnp.float32)
    inverse_rms = lax.rsqrt(jnp.mean(as_float * as_float, axis=-1, keepdims=True) + 1e-05)
    normed = (as_float * inverse_rms).astype(jnp.bfloat16)
    pre_act = jnp.dot(normed, dense_w, preferred_element_type=jnp.float32)
    return ((as_float + jax.nn.silu(pre_act)).astype(jnp.bfloat16), normed, pre_act)


def layer_backward(arriving, entering, pre_act, dense_w):
    as_float = entering.astype(jnp.float32)
    inverse_rms = lax.rsqrt(jnp.mean(as_float * as_float, axis=-1, keepdims=True) + 1e-05)
    sigmoid_z = jax.nn.sigmoid(pre_act)
    grad_pre = (
        arriving.astype(jnp.float32) * (sigmoid_z * (1.0 + pre_act * (1.0 - sigmoid_z)))
    ).astype(jnp.bfloat16)
    grad_normed = lax.dot_general(
        grad_pre, dense_w, (((1,), (1,)), ((), ())), preferred_element_type=jnp.float32
    )
    scaled = as_float * inverse_rms
    leaving = (
        arriving.astype(jnp.float32)
        + inverse_rms
        * (grad_normed - scaled * jnp.mean(grad_normed * scaled, axis=-1, keepdims=True))
    ).astype(jnp.bfloat16)
    return (leaving, grad_pre)


def local(x_in, cotangent, weights, live_rows, moment, second):
    sections = lax.axis_size("pipe")
    section_index = lax.axis_index("pipe")
    group = 2
    micro_total, micro_tokens, features = x_in.shape
    micro_count = micro_total // group
    tokens = micro_tokens * group
    x_in = x_in.reshape(micro_count, tokens, features)
    cotangent = cotangent.reshape(micro_count, tokens, features)
    column_count = live_rows.shape[1]
    live_count = live_rows.shape[2]
    own_columns = weights.shape[1]
    block_size = weights.shape[2]
    live_index = live_rows[0]
    own_pair = weights[0].transpose(2, 0, 1).reshape(1, live_count * block_size, own_columns * block_size)
    paired_weights = lax.all_gather(own_pair, "dp", axis=0, tiled=True)
    dense_w = expand_dense(paired_weights, live_index)
    tick_count = micro_count + sections - 1

    incoming = jnp.zeros((tokens, features), jnp.bfloat16)
    kept_in, kept_normed, kept_pre = [], [], []
    for tick_index in range(tick_count):
        entering = jnp.where(section_index == 0, x_in[min(tick_index, micro_count - 1)], incoming)
        outgoing, normed, pre_act = layer_forward(entering, dense_w)
        kept_in.append(entering)
        kept_normed.append(normed)
        kept_pre.append(pre_act)
        if tick_index + 1 < tick_count:
            incoming = shifted(outgoing, "pipe", 1)
    saved_in = lax.dynamic_slice_in_dim(jnp.stack(kept_in), section_index, micro_count, 0)
    saved_normed = lax.dynamic_slice_in_dim(jnp.stack(kept_normed), section_index, micro_count, 0)
    saved_pre = lax.dynamic_slice_in_dim(jnp.stack(kept_pre), section_index, micro_count, 0)

    incoming_grad = jnp.zeros((tokens, features), jnp.bfloat16)
    kept_grad = []
    for tick_index in range(tick_count):
        slot_index = jnp.clip(tick_index - (sections - 1 - section_index), 0, micro_count - 1)
        arriving = jnp.where(
            section_index == sections - 1,
            cotangent[min(tick_index, micro_count - 1)],
            incoming_grad,
        )
        leaving, grad_pre = layer_backward(
            arriving, saved_in[slot_index], saved_pre[slot_index], dense_w
        )
        kept_grad.append(grad_pre)
        if tick_index + 1 < tick_count:
            incoming_grad = shifted(leaving, "pipe", -1)
    saved_grad = lax.dynamic_slice_in_dim(
        jnp.stack(kept_grad), sections - 1 - section_index, micro_count, 0
    )

    all_rows = micro_count * tokens
    inverse_tokens = 1.0 / (all_rows * lax.axis_size("dp"))
    dense_grad = (
        lax.dot_general(
            saved_normed.reshape(all_rows, features),
            saved_grad.reshape(all_rows, features),
            (((0,), (0,)), ((), ())),
            preferred_element_type=jnp.float32,
        )
        * inverse_tokens
    ).astype(jnp.bfloat16)
    half_k = live_count // 2
    own_grad = jnp.concatenate(
        [
            lax.psum_scatter(
                pack_dense(dense_grad, live_index, first_k, half_k), "dp", scatter_dimension=0, tiled=True
            )
            for first_k in (0, half_k)
        ],
        axis=1,
    )
    gradient = (
        own_grad.reshape(live_count * block_size, own_columns, block_size)
        .transpose(1, 2, 0)
        .astype(jnp.float32)
    )

    rate = 0.1 / math.sqrt(live_count * block_size)
    moment_new = 0.9 * moment[0] + 0.1 * gradient
    second_new = 0.95 * second[0] + 0.05 * gradient * gradient
    stepped = weights[0].astype(jnp.float32) - rate * moment_new / (jnp.sqrt(second_new) + 1e-08)
    own_index = lax.dynamic_slice_in_dim(
        live_index, lax.axis_index("dp") * own_columns, own_columns, 0
    )
    blocked = stepped.reshape(own_columns, block_size, live_count, block_size)
    magnitude = jnp.sqrt(jnp.sum(blocked * blocked, axis=(1, 3)))
    leafed = (
        blocked * shrink(magnitude, 0.15 * math.sqrt(block_size / live_count))[:, None, :, None]
    )
    block_squares = jnp.sum(leafed * leafed, axis=(1, 3))
    head_count = features // HEAD
    head_index = own_index // (HEAD // block_size)
    onehot = (
        head_index[:, :, None] == jnp.arange(head_count, dtype=jnp.int32)[None, None, :]
    ).astype(jnp.float32)
    head_partial = jnp.sum(onehot * block_squares[:, :, None], axis=(0, 1))
    head_squares = spread_sum(head_partial)
    head_factor = shrink(jnp.sqrt(head_squares), 0.45 * math.sqrt(HEAD))
    headed = leafed * jnp.sum(onehot * head_factor[None, None, :], axis=2)[:, None, :, None]
    layer_squares = jnp.sum(head_factor * head_factor * head_squares)
    layer_factor = shrink(jnp.sqrt(layer_squares), 0.45 * math.sqrt(features))
    weights_out = (
        (headed * layer_factor)
        .astype(jnp.bfloat16)
        .reshape(own_columns, block_size, live_count * block_size)
    )
    return (weights_out[None], moment_new[None], second_new[None])


def solution(mesh):
    placed = (
        P(None, "dp", None),
        P(None, "dp", None),
        P("pipe", "dp", None, None),
        P("pipe", None, None),
        P("pipe", "dp", None, None),
        P("pipe", "dp", None, None),
    )
    return jax.shard_map(
        local,
        mesh=mesh,
        in_specs=placed,
        out_specs=(
            P("pipe", "dp", None, None),
            P("pipe", "dp", None, None),
            P("pipe", "dp", None, None),
        ),
        check_vma=False,
    )
```

```python
import math

import jax
import jax.numpy as jnp
from jax import lax
from jax.experimental import pallas as pl
from jax.experimental.pallas import tpu as pltpu
from jax.sharding import PartitionSpec as P

HEAD = 128


def shifted(value, axis, steps):
    count = lax.axis_size(axis)
    leading, last = (max(0, -steps), min(count, count - steps))
    return lax.ppermute(value, axis, [(source, source + steps) for source in range(leading, last)])


def shrink(magnitude, threshold):
    return jnp.maximum(magnitude - threshold, 0.0) / jnp.maximum(magnitude, threshold)


def expand_kernel(table_ref, t_ref, o_ref):
    p = pl.program_id(0)
    block = 64
    blocks = o_ref.shape[0] // block
    lane = lax.broadcasted_iota(jnp.int32, (block, o_ref.shape[1]), 1)
    for r in range(blocks):
        k0 = table_ref[(2 * p) * blocks + r]
        k1 = table_ref[(2 * p + 1) * blocks + r]
        s0 = pl.multiple_of(jnp.maximum(k0, 0) * block, block)
        s1 = pl.multiple_of(jnp.maximum(k1, 0) * block, block)
        t0 = t_ref[pl.ds(s0, block), :]
        t1 = t_ref[pl.ds(s1, block), :]
        zero = jnp.zeros_like(t0)
        t0 = jnp.where(k0 >= 0, t0, zero)
        t1 = jnp.where(k1 >= 0, t1, zero)
        o_ref[r * block:(r + 1) * block, :] = jnp.where(lane < block, t0, t1)


def pack_kernel(table_ref, g_ref, o_ref):
    p = pl.program_id(0)
    block = 64
    live_count = o_ref.shape[1] // block
    lane = lax.broadcasted_iota(jnp.int32, (block, o_ref.shape[2]), 1)
    for k in range(live_count):
        r0 = table_ref[(2 * p) * live_count + k]
        r1 = table_ref[(2 * p + 1) * live_count + k]
        s0 = pl.multiple_of(r0 * block, block)
        s1 = pl.multiple_of(r1 * block, block)
        t0 = g_ref[pl.ds(s0, block), :]
        t1 = g_ref[pl.ds(s1, block), :]
        o_ref[0, k * block:(k + 1) * block, :] = jnp.where(lane < block, t0, t1)


def expand_dense(paired_weights, live_index):
    pair_count, wide, two_blocks = paired_weights.shape
    column_count, live_count = live_index.shape
    block_size = two_blocks // 2
    features = column_count * block_size
    targets = jnp.arange(column_count, dtype=jnp.int32)
    hit = live_index[:, :, None] == targets[None, None, :]
    k_ids = jnp.arange(live_count, dtype=jnp.int32)[None, :, None]
    inverse = jnp.where(
        jnp.any(hit, axis=1), jnp.sum(jnp.where(hit, k_ids, 0), axis=1), -1
    ).astype(jnp.int32)
    return pl.pallas_call(
        expand_kernel,
        out_shape=jax.ShapeDtypeStruct((features, features), paired_weights.dtype),
        grid_spec=pltpu.PrefetchScalarGridSpec(
            num_scalar_prefetch=1,
            grid=(pair_count,),
            in_specs=[pl.BlockSpec((None, wide, two_blocks), lambda p, tbl: (p, 0, 0))],
            out_specs=pl.BlockSpec((features, two_blocks), lambda p, tbl: (0, p)),
        ),
        cost_estimate=pl.CostEstimate(
            flops=0, transcendentals=0, bytes_accessed=3 * pair_count * wide * two_blocks * 2
        ),
    )(inverse.reshape(-1), paired_weights)


def pack_dense(dense_grad, live_index):
    column_count, live_count = live_index.shape
    features = dense_grad.shape[0]
    block_size = features // column_count
    wide = live_count * block_size
    pair_count = column_count // 2
    return pl.pallas_call(
        pack_kernel,
        out_shape=jax.ShapeDtypeStruct((pair_count, wide, 2 * block_size), dense_grad.dtype),
        grid_spec=pltpu.PrefetchScalarGridSpec(
            num_scalar_prefetch=1,
            grid=(pair_count,),
            in_specs=[pl.BlockSpec((features, 2 * block_size), lambda p, tbl: (0, p))],
            out_specs=pl.BlockSpec((1, wide, 2 * block_size), lambda p, tbl: (p, 0, 0)),
        ),
        cost_estimate=pl.CostEstimate(
            flops=0, transcendentals=0, bytes_accessed=3 * pair_count * wide * 2 * block_size * 2
        ),
    )(live_index.reshape(-1).astype(jnp.int32), dense_grad)


def spread_kernel(x_ref, o_ref, recv_ref, send_sem, recv_sem):
    count = recv_ref.shape[0]
    me = lax.axis_index("dp")
    pipe = lax.axis_index("pipe")
    barrier = pltpu.get_barrier_semaphore()
    for step in range(1, count):
        peer = lax.rem(me + step, count)
        pl.semaphore_signal(barrier, inc=1, device_id=(pipe, peer), device_id_type=pl.DeviceIdType.MESH)
    pl.semaphore_wait(barrier, count - 1)
    copies = []
    for step in range(1, count):
        peer = lax.rem(me + step, count)
        copy = pltpu.make_async_remote_copy(
            src_ref=x_ref,
            dst_ref=recv_ref.at[me],
            send_sem=send_sem.at[step],
            recv_sem=recv_sem.at[me],
            device_id=(pipe, peer),
            device_id_type=pl.DeviceIdType.MESH,
        )
        copy.start()
        copies.append(copy)
    total = x_ref[...]
    for step in range(1, count):
        source = lax.rem(me + count - step, count)
        arrival = pltpu.make_async_remote_copy(
            src_ref=x_ref,
            dst_ref=recv_ref.at[source],
            send_sem=send_sem.at[step],
            recv_sem=recv_sem.at[source],
            device_id=(pipe, source),
            device_id_type=pl.DeviceIdType.MESH,
        )
        arrival.wait_recv()
        total = total + recv_ref[source]
    for copy in copies:
        copy.wait_send()
    o_ref[...] = total


def spread_sum(values):
    count = lax.axis_size("dp")
    padded = jnp.zeros((8, 128), jnp.float32).at[0, : values.shape[0]].set(values)
    out = pl.pallas_call(
        spread_kernel,
        out_shape=jax.ShapeDtypeStruct((8, 128), jnp.float32),
        in_specs=[pl.BlockSpec(memory_space=pltpu.VMEM)],
        out_specs=pl.BlockSpec(memory_space=pltpu.VMEM),
        scratch_shapes=[
            pltpu.VMEM((count, 8, 128), jnp.float32),
            pltpu.SemaphoreType.DMA((count,)),
            pltpu.SemaphoreType.DMA((count,)),
        ],
        compiler_params=pltpu.CompilerParams(collective_id=0, has_side_effects=True),
    )(padded)
    return out[0, : values.shape[0]]


def forward_mm_kernel(u_ref, w_ref, o_ref):
    @pl.when(pl.program_id(0) == 0)
    def _():
        o_ref[...] = jnp.zeros_like(o_ref)

    o_ref[...] += jnp.dot(u_ref[...], w_ref[...], preferred_element_type=jnp.float32)


def backward_mm_kernel(g_ref, w_ref, o_ref):
    o_ref[...] = lax.dot_general(
        g_ref[...], w_ref[...], (((1,), (1,)), ((), ())), preferred_element_type=jnp.float32
    )


STRIPE = 512


def forward_mm(normed, dense_w):
    tokens, features = normed.shape
    return pl.pallas_call(
        forward_mm_kernel,
        out_shape=jax.ShapeDtypeStruct((tokens, dense_w.shape[1]), jnp.float32),
        grid=(features // STRIPE,),
        in_specs=[
            pl.BlockSpec((tokens, STRIPE), lambda k: (0, k)),
            pl.BlockSpec((STRIPE, dense_w.shape[1]), lambda k: (k, 0)),
        ],
        out_specs=pl.BlockSpec((tokens, dense_w.shape[1]), lambda k: (0, 0)),
        cost_estimate=pl.CostEstimate(
            flops=2 * tokens * features * dense_w.shape[1],
            transcendentals=0,
            bytes_accessed=dense_w.size * 2,
        ),
    )(normed, dense_w)


def backward_mm(grad_pre, dense_w):
    tokens, columns = grad_pre.shape
    features = dense_w.shape[0]
    return pl.pallas_call(
        backward_mm_kernel,
        out_shape=jax.ShapeDtypeStruct((tokens, features), jnp.float32),
        grid=(features // STRIPE,),
        in_specs=[
            pl.BlockSpec((tokens, columns), lambda n: (0, 0)),
            pl.BlockSpec((STRIPE, columns), lambda n: (n, 0)),
        ],
        out_specs=pl.BlockSpec((tokens, STRIPE), lambda n: (0, n)),
        cost_estimate=pl.CostEstimate(
            flops=2 * tokens * features * columns,
            transcendentals=0,
            bytes_accessed=dense_w.size * 2,
        ),
    )(grad_pre, dense_w)


def layer_forward(entering, dense_w):
    as_float = entering.astype(jnp.float32)
    inverse_rms = lax.rsqrt(jnp.mean(as_float * as_float, axis=-1, keepdims=True) + 1e-05)
    normed = (as_float * inverse_rms).astype(jnp.bfloat16)
    pre_act = forward_mm(normed, dense_w)
    return ((as_float + jax.nn.silu(pre_act)).astype(jnp.bfloat16), normed, pre_act)


def layer_backward(arriving, entering, pre_act, dense_w):
    as_float = entering.astype(jnp.float32)
    inverse_rms = lax.rsqrt(jnp.mean(as_float * as_float, axis=-1, keepdims=True) + 1e-05)
    sigmoid_z = jax.nn.sigmoid(pre_act)
    grad_pre = (
        arriving.astype(jnp.float32) * (sigmoid_z * (1.0 + pre_act * (1.0 - sigmoid_z)))
    ).astype(jnp.bfloat16)
    grad_normed = backward_mm(grad_pre, dense_w)
    scaled = as_float * inverse_rms
    leaving = (
        arriving.astype(jnp.float32)
        + inverse_rms
        * (grad_normed - scaled * jnp.mean(grad_normed * scaled, axis=-1, keepdims=True))
    ).astype(jnp.bfloat16)
    return (leaving, grad_pre)


def local(x_in, cotangent, weights, live_rows, moment, second):
    sections = lax.axis_size("pipe")
    section_index = lax.axis_index("pipe")
    group = 2
    micro_total, micro_tokens, features = x_in.shape
    micro_count = micro_total // group
    tokens = micro_tokens * group
    x_in = x_in.reshape(micro_count, tokens, features)
    cotangent = cotangent.reshape(micro_count, tokens, features)
    column_count = live_rows.shape[1]
    live_count = live_rows.shape[2]
    own_columns = weights.shape[1]
    block_size = weights.shape[2]
    live_index = live_rows[0]
    own_pair = weights[0].transpose(2, 0, 1).reshape(1, live_count * block_size, own_columns * block_size)
    paired_weights = lax.all_gather(own_pair, "dp", axis=0, tiled=True)
    dense_w = expand_dense(paired_weights, live_index)
    tick_count = micro_count + sections - 1

    incoming = jnp.zeros((tokens, features), jnp.bfloat16)
    kept_in, kept_normed, kept_pre = [], [], []
    for tick_index in range(tick_count):
        entering = jnp.where(section_index == 0, x_in[min(tick_index, micro_count - 1)], incoming)
        outgoing, normed, pre_act = layer_forward(entering, dense_w)
        kept_in.append(entering)
        kept_normed.append(normed)
        kept_pre.append(pre_act)
        if tick_index + 1 < tick_count:
            incoming = shifted(outgoing, "pipe", 1)
    saved_in = lax.dynamic_slice_in_dim(jnp.stack(kept_in), section_index, micro_count, 0)
    saved_normed = lax.dynamic_slice_in_dim(jnp.stack(kept_normed), section_index, micro_count, 0)
    saved_pre = lax.dynamic_slice_in_dim(jnp.stack(kept_pre), section_index, micro_count, 0)

    incoming_grad = jnp.zeros((tokens, features), jnp.bfloat16)
    kept_grad = []
    for tick_index in range(tick_count):
        slot_index = jnp.clip(tick_index - (sections - 1 - section_index), 0, micro_count - 1)
        arriving = jnp.where(
            section_index == sections - 1,
            cotangent[min(tick_index, micro_count - 1)],
            incoming_grad,
        )
        leaving, grad_pre = layer_backward(
            arriving, saved_in[slot_index], saved_pre[slot_index], dense_w
        )
        kept_grad.append(grad_pre)
        if tick_index + 1 < tick_count:
            incoming_grad = shifted(leaving, "pipe", -1)
    saved_grad = lax.dynamic_slice_in_dim(
        jnp.stack(kept_grad), sections - 1 - section_index, micro_count, 0
    )

    all_rows = micro_count * tokens
    inverse_tokens = 1.0 / (all_rows * lax.axis_size("dp"))
    dense_grad = (
        lax.dot_general(
            saved_normed.reshape(all_rows, features),
            saved_grad.reshape(all_rows, features),
            (((0,), (0,)), ((), ())),
            preferred_element_type=jnp.float32,
        )
        * inverse_tokens
    ).astype(jnp.bfloat16)
    partial = pack_dense(dense_grad, live_index)
    own_grad = lax.psum_scatter(partial, "dp", scatter_dimension=0, tiled=True)
    gradient = (
        own_grad.reshape(live_count * block_size, own_columns, block_size)
        .transpose(1, 2, 0)
        .astype(jnp.float32)
    )

    rate = 0.1 / math.sqrt(live_count * block_size)
    moment_new = 0.9 * moment[0] + 0.1 * gradient
    second_new = 0.95 * second[0] + 0.05 * gradient * gradient
    stepped = weights[0].astype(jnp.float32) - rate * moment_new / (jnp.sqrt(second_new) + 1e-08)
    own_index = lax.dynamic_slice_in_dim(
        live_index, lax.axis_index("dp") * own_columns, own_columns, 0
    )
    blocked = stepped.reshape(own_columns, block_size, live_count, block_size)
    magnitude = jnp.sqrt(jnp.sum(blocked * blocked, axis=(1, 3)))
    leafed = (
        blocked * shrink(magnitude, 0.15 * math.sqrt(block_size / live_count))[:, None, :, None]
    )
    block_squares = jnp.sum(leafed * leafed, axis=(1, 3))
    head_count = features // HEAD
    head_index = own_index // (HEAD // block_size)
    onehot = (
        head_index[:, :, None] == jnp.arange(head_count, dtype=jnp.int32)[None, None, :]
    ).astype(jnp.float32)
    head_partial = jnp.sum(onehot * block_squares[:, :, None], axis=(0, 1))
    head_squares = spread_sum(head_partial)
    head_factor = shrink(jnp.sqrt(head_squares), 0.45 * math.sqrt(HEAD))
    headed = leafed * jnp.sum(onehot * head_factor[None, None, :], axis=2)[:, None, :, None]
    layer_squares = jnp.sum(head_factor * head_factor * head_squares)
    layer_factor = shrink(jnp.sqrt(layer_squares), 0.45 * math.sqrt(features))
    weights_out = (
        (headed * layer_factor)
        .astype(jnp.bfloat16)
        .reshape(own_columns, block_size, live_count * block_size)
    )
    return (weights_out[None], moment_new[None], second_new[None])


def solution(mesh):
    placed = (
        P(None, "dp", None),
        P(None, "dp", None),
        P("pipe", "dp", None, None),
        P("pipe", None, None),
        P("pipe", "dp", None, None),
        P("pipe", "dp", None, None),
    )
    return jax.shard_map(
        local,
        mesh=mesh,
        in_specs=placed,
        out_specs=(
            P("pipe", "dp", None, None),
            P("pipe", "dp", None, None),
            P("pipe", "dp", None, None),
        ),
        check_vma=False,
    )
```

```python
import math

import jax
import jax.numpy as jnp
from jax import lax
from jax.experimental import pallas as pl
from jax.experimental.pallas import tpu as pltpu
from jax.sharding import PartitionSpec as P

HEAD = 128


def shifted(value, axis, steps):
    count = lax.axis_size(axis)
    leading, last = (max(0, -steps), min(count, count - steps))
    return lax.ppermute(value, axis, [(source, source + steps) for source in range(leading, last)])


def shrink(magnitude, threshold):
    return jnp.maximum(magnitude - threshold, 0.0) / jnp.maximum(magnitude, threshold)


def expand_kernel(table_ref, t_ref, o_ref):
    per_step = t_ref.shape[0]
    block = 64
    blocks = o_ref.shape[0] // block
    lane = lax.broadcasted_iota(jnp.int32, (block, 2 * block), 1)
    for pp in range(per_step):
        p = pl.program_id(0) * per_step + pp
        for r in range(blocks):
            k0 = table_ref[(2 * p) * blocks + r]
            k1 = table_ref[(2 * p + 1) * blocks + r]
            s0 = pl.multiple_of(jnp.maximum(k0, 0) * block, block)
            s1 = pl.multiple_of(jnp.maximum(k1, 0) * block, block)
            t0 = t_ref[pp, pl.ds(s0, block), :]
            t1 = t_ref[pp, pl.ds(s1, block), :]
            zero = jnp.zeros_like(t0)
            t0 = jnp.where(k0 >= 0, t0, zero)
            t1 = jnp.where(k1 >= 0, t1, zero)
            o_ref[r * block:(r + 1) * block, pp * 2 * block:(pp + 1) * 2 * block] = jnp.where(
                lane < block, t0, t1
            )


def pack_kernel(table_ref, g_ref, o_ref):
    per_step = o_ref.shape[0]
    block = 64
    live_count = o_ref.shape[1] // block
    lane = lax.broadcasted_iota(jnp.int32, (block, 2 * block), 1)
    for pp in range(per_step):
        p = pl.program_id(0) * per_step + pp
        for k in range(live_count):
            r0 = table_ref[(2 * p) * live_count + k]
            r1 = table_ref[(2 * p + 1) * live_count + k]
            s0 = pl.multiple_of(r0 * block, block)
            s1 = pl.multiple_of(r1 * block, block)
            t0 = g_ref[pl.ds(s0, block), pp * 2 * block:(pp + 1) * 2 * block]
            t1 = g_ref[pl.ds(s1, block), pp * 2 * block:(pp + 1) * 2 * block]
            o_ref[pp, k * block:(k + 1) * block, :] = jnp.where(lane < block, t0, t1)


PAIRS_PER_STEP = 2


def expand_dense(paired_weights, live_index):
    pair_count, wide, two_blocks = paired_weights.shape
    column_count, live_count = live_index.shape
    block_size = two_blocks // 2
    features = column_count * block_size
    targets = jnp.arange(column_count, dtype=jnp.int32)
    hit = live_index[:, :, None] == targets[None, None, :]
    k_ids = jnp.arange(live_count, dtype=jnp.int32)[None, :, None]
    inverse = jnp.where(
        jnp.any(hit, axis=1), jnp.sum(jnp.where(hit, k_ids, 0), axis=1), -1
    ).astype(jnp.int32)
    return pl.pallas_call(
        expand_kernel,
        out_shape=jax.ShapeDtypeStruct((features, features), paired_weights.dtype),
        grid_spec=pltpu.PrefetchScalarGridSpec(
            num_scalar_prefetch=1,
            grid=(pair_count // PAIRS_PER_STEP,),
            in_specs=[pl.BlockSpec((PAIRS_PER_STEP, wide, two_blocks), lambda q, tbl: (q, 0, 0))],
            out_specs=pl.BlockSpec((features, PAIRS_PER_STEP * two_blocks), lambda q, tbl: (0, q)),
        ),
        cost_estimate=pl.CostEstimate(
            flops=0, transcendentals=0, bytes_accessed=3 * pair_count * wide * two_blocks * 2
        ),
    )(inverse.reshape(-1), paired_weights)


def pack_dense(dense_grad, live_index):
    column_count, live_count = live_index.shape
    features = dense_grad.shape[0]
    block_size = features // column_count
    wide = live_count * block_size
    pair_count = column_count // 2
    return pl.pallas_call(
        pack_kernel,
        out_shape=jax.ShapeDtypeStruct((pair_count, wide, 2 * block_size), dense_grad.dtype),
        grid_spec=pltpu.PrefetchScalarGridSpec(
            num_scalar_prefetch=1,
            grid=(pair_count // PAIRS_PER_STEP,),
            in_specs=[
                pl.BlockSpec((features, PAIRS_PER_STEP * 2 * block_size), lambda q, tbl: (0, q))
            ],
            out_specs=pl.BlockSpec((PAIRS_PER_STEP, wide, 2 * block_size), lambda q, tbl: (q, 0, 0)),
        ),
        cost_estimate=pl.CostEstimate(
            flops=0, transcendentals=0, bytes_accessed=3 * pair_count * wide * 2 * block_size * 2
        ),
    )(live_index.reshape(-1).astype(jnp.int32), dense_grad)


def spread_kernel(x_ref, o_ref, recv_ref, send_sem, recv_sem):
    count = recv_ref.shape[0]
    me = lax.axis_index("dp")
    pipe = lax.axis_index("pipe")
    barrier = pltpu.get_barrier_semaphore()
    for step in range(1, count):
        peer = lax.rem(me + step, count)
        pl.semaphore_signal(barrier, inc=1, device_id=(pipe, peer), device_id_type=pl.DeviceIdType.MESH)
    pl.semaphore_wait(barrier, count - 1)
    copies = []
    for step in range(1, count):
        peer = lax.rem(me + step, count)
        copy = pltpu.make_async_remote_copy(
            src_ref=x_ref,
            dst_ref=recv_ref.at[me],
            send_sem=send_sem.at[step],
            recv_sem=recv_sem.at[me],
            device_id=(pipe, peer),
            device_id_type=pl.DeviceIdType.MESH,
        )
        copy.start()
        copies.append(copy)
    total = x_ref[...]
    for step in range(1, count):
        source = lax.rem(me + count - step, count)
        arrival = pltpu.make_async_remote_copy(
            src_ref=x_ref,
            dst_ref=recv_ref.at[source],
            send_sem=send_sem.at[step],
            recv_sem=recv_sem.at[source],
            device_id=(pipe, source),
            device_id_type=pl.DeviceIdType.MESH,
        )
        arrival.wait_recv()
        total = total + recv_ref[source]
    for copy in copies:
        copy.wait_send()
    o_ref[...] = total


def spread_sum(values):
    count = lax.axis_size("dp")
    padded = jnp.zeros((8, 128), jnp.float32).at[0, : values.shape[0]].set(values)
    out = pl.pallas_call(
        spread_kernel,
        out_shape=jax.ShapeDtypeStruct((8, 128), jnp.float32),
        in_specs=[pl.BlockSpec(memory_space=pltpu.VMEM)],
        out_specs=pl.BlockSpec(memory_space=pltpu.VMEM),
        scratch_shapes=[
            pltpu.VMEM((count, 8, 128), jnp.float32),
            pltpu.SemaphoreType.DMA((count,)),
            pltpu.SemaphoreType.DMA((count,)),
        ],
        compiler_params=pltpu.CompilerParams(collective_id=0, has_side_effects=True),
    )(padded)
    return out[0, : values.shape[0]]


def layer_forward(entering, dense_w):
    as_float = entering.astype(jnp.float32)
    inverse_rms = lax.rsqrt(jnp.mean(as_float * as_float, axis=-1, keepdims=True) + 1e-05)
    normed = (as_float * inverse_rms).astype(jnp.bfloat16)
    pre_act = jnp.dot(normed, dense_w, preferred_element_type=jnp.float32)
    return ((as_float + jax.nn.silu(pre_act)).astype(jnp.bfloat16), normed, pre_act)


def layer_backward(arriving, entering, pre_act, dense_w):
    as_float = entering.astype(jnp.float32)
    inverse_rms = lax.rsqrt(jnp.mean(as_float * as_float, axis=-1, keepdims=True) + 1e-05)
    sigmoid_z = jax.nn.sigmoid(pre_act)
    grad_pre = (
        arriving.astype(jnp.float32) * (sigmoid_z * (1.0 + pre_act * (1.0 - sigmoid_z)))
    ).astype(jnp.bfloat16)
    grad_normed = lax.dot_general(
        grad_pre, dense_w, (((1,), (1,)), ((), ())), preferred_element_type=jnp.float32
    )
    scaled = as_float * inverse_rms
    leaving = (
        arriving.astype(jnp.float32)
        + inverse_rms
        * (grad_normed - scaled * jnp.mean(grad_normed * scaled, axis=-1, keepdims=True))
    ).astype(jnp.bfloat16)
    return (leaving, grad_pre)


def local(x_in, cotangent, weights, live_rows, moment, second):
    sections = lax.axis_size("pipe")
    section_index = lax.axis_index("pipe")
    group = 2
    micro_total, micro_tokens, features = x_in.shape
    micro_count = micro_total // group
    tokens = micro_tokens * group
    x_in = x_in.reshape(micro_count, tokens, features)
    cotangent = cotangent.reshape(micro_count, tokens, features)
    column_count = live_rows.shape[1]
    live_count = live_rows.shape[2]
    own_columns = weights.shape[1]
    block_size = weights.shape[2]
    live_index = live_rows[0]
    own_pair = weights[0].transpose(2, 0, 1).reshape(1, live_count * block_size, own_columns * block_size)
    paired_weights = lax.all_gather(own_pair, "dp", axis=0, tiled=True)
    dense_w = expand_dense(paired_weights, live_index)
    tick_count = micro_count + sections - 1

    incoming = jnp.zeros((tokens, features), jnp.bfloat16)
    kept_in, kept_normed, kept_pre = [], [], []
    for tick_index in range(tick_count):
        entering = jnp.where(section_index == 0, x_in[min(tick_index, micro_count - 1)], incoming)
        outgoing, normed, pre_act = layer_forward(entering, dense_w)
        kept_in.append(entering)
        kept_normed.append(normed)
        kept_pre.append(pre_act)
        if tick_index + 1 < tick_count:
            incoming = shifted(outgoing, "pipe", 1)
    saved_in = lax.dynamic_slice_in_dim(jnp.stack(kept_in), section_index, micro_count, 0)
    saved_normed = lax.dynamic_slice_in_dim(jnp.stack(kept_normed), section_index, micro_count, 0)
    saved_pre = lax.dynamic_slice_in_dim(jnp.stack(kept_pre), section_index, micro_count, 0)

    incoming_grad = jnp.zeros((tokens, features), jnp.bfloat16)
    kept_grad = []
    for tick_index in range(tick_count):
        slot_index = jnp.clip(tick_index - (sections - 1 - section_index), 0, micro_count - 1)
        arriving = jnp.where(
            section_index == sections - 1,
            cotangent[min(tick_index, micro_count - 1)],
            incoming_grad,
        )
        leaving, grad_pre = layer_backward(
            arriving, saved_in[slot_index], saved_pre[slot_index], dense_w
        )
        kept_grad.append(grad_pre)
        if tick_index + 1 < tick_count:
            incoming_grad = shifted(leaving, "pipe", -1)
    saved_grad = lax.dynamic_slice_in_dim(
        jnp.stack(kept_grad), sections - 1 - section_index, micro_count, 0
    )

    all_rows = micro_count * tokens
    inverse_tokens = 1.0 / (all_rows * lax.axis_size("dp"))
    dense_grad = (
        lax.dot_general(
            saved_normed.reshape(all_rows, features),
            saved_grad.reshape(all_rows, features),
            (((0,), (0,)), ((), ())),
            preferred_element_type=jnp.float32,
        )
        * inverse_tokens
    ).astype(jnp.bfloat16)
    partial = pack_dense(dense_grad, live_index)
    own_grad = lax.psum_scatter(partial, "dp", scatter_dimension=0, tiled=True)
    gradient = (
        own_grad.reshape(live_count * block_size, own_columns, block_size)
        .transpose(1, 2, 0)
        .astype(jnp.float32)
    )

    rate = 0.1 / math.sqrt(live_count * block_size)
    moment_new = 0.9 * moment[0] + 0.1 * gradient
    second_new = 0.95 * second[0] + 0.05 * gradient * gradient
    stepped = weights[0].astype(jnp.float32) - rate * moment_new / (jnp.sqrt(second_new) + 1e-08)
    own_index = lax.dynamic_slice_in_dim(
        live_index, lax.axis_index("dp") * own_columns, own_columns, 0
    )
    blocked = stepped.reshape(own_columns, block_size, live_count, block_size)
    magnitude = jnp.sqrt(jnp.sum(blocked * blocked, axis=(1, 3)))
    leafed = (
        blocked * shrink(magnitude, 0.15 * math.sqrt(block_size / live_count))[:, None, :, None]
    )
    block_squares = jnp.sum(leafed * leafed, axis=(1, 3))
    head_count = features // HEAD
    head_index = own_index // (HEAD // block_size)
    onehot = (
        head_index[:, :, None] == jnp.arange(head_count, dtype=jnp.int32)[None, None, :]
    ).astype(jnp.float32)
    head_partial = jnp.sum(onehot * block_squares[:, :, None], axis=(0, 1))
    head_squares = spread_sum(head_partial)
    head_factor = shrink(jnp.sqrt(head_squares), 0.45 * math.sqrt(HEAD))
    headed = leafed * jnp.sum(onehot * head_factor[None, None, :], axis=2)[:, None, :, None]
    layer_squares = jnp.sum(head_factor * head_factor * head_squares)
    layer_factor = shrink(jnp.sqrt(layer_squares), 0.45 * math.sqrt(features))
    weights_out = (
        (headed * layer_factor)
        .astype(jnp.bfloat16)
        .reshape(own_columns, block_size, live_count * block_size)
    )
    return (weights_out[None], moment_new[None], second_new[None])


def solution(mesh):
    placed = (
        P(None, "dp", None),
        P(None, "dp", None),
        P("pipe", "dp", None, None),
        P("pipe", None, None),
        P("pipe", "dp", None, None),
        P("pipe", "dp", None, None),
    )
    return jax.shard_map(
        local,
        mesh=mesh,
        in_specs=placed,
        out_specs=(
            P("pipe", "dp", None, None),
            P("pipe", "dp", None, None),
            P("pipe", "dp", None, None),
        ),
        check_vma=False,
    )
```

```python
import math

import jax
import jax.numpy as jnp
from jax import lax
from jax.experimental import pallas as pl
from jax.experimental.pallas import tpu as pltpu
from jax.sharding import PartitionSpec as P

HEAD = 128


def shifted(value, axis, steps):
    count = lax.axis_size(axis)
    leading, last = (max(0, -steps), min(count, count - steps))
    return lax.ppermute(value, axis, [(source, source + steps) for source in range(leading, last)])


def shrink(magnitude, threshold):
    return jnp.maximum(magnitude - threshold, 0.0) / jnp.maximum(magnitude, threshold)


def expand_kernel(table_ref, t_ref, o_ref):
    per_step = t_ref.shape[0]
    block = 64
    blocks = o_ref.shape[0] // block
    lane = lax.broadcasted_iota(jnp.int32, (block, 2 * block), 1)
    for pp in range(per_step):
        p = pl.program_id(0) * per_step + pp
        for r in range(blocks):
            k0 = table_ref[(2 * p) * blocks + r]
            k1 = table_ref[(2 * p + 1) * blocks + r]
            s0 = pl.multiple_of(jnp.maximum(k0, 0) * block, block)
            s1 = pl.multiple_of(jnp.maximum(k1, 0) * block, block)
            t0 = t_ref[pp, pl.ds(s0, block), :]
            t1 = t_ref[pp, pl.ds(s1, block), :]
            zero = jnp.zeros_like(t0)
            t0 = jnp.where(k0 >= 0, t0, zero)
            t1 = jnp.where(k1 >= 0, t1, zero)
            o_ref[r * block:(r + 1) * block, pp * 2 * block:(pp + 1) * 2 * block] = jnp.where(
                lane < block, t0, t1
            )


def pack_kernel(table_ref, g_ref, o_ref):
    per_step = o_ref.shape[0]
    block = 64
    live_count = o_ref.shape[1] // block
    lane = lax.broadcasted_iota(jnp.int32, (block, 2 * block), 1)
    for pp in range(per_step):
        p = pl.program_id(0) * per_step + pp
        for k in range(live_count):
            r0 = table_ref[(2 * p) * live_count + k]
            r1 = table_ref[(2 * p + 1) * live_count + k]
            s0 = pl.multiple_of(r0 * block, block)
            s1 = pl.multiple_of(r1 * block, block)
            t0 = g_ref[pl.ds(s0, block), pp * 2 * block:(pp + 1) * 2 * block]
            t1 = g_ref[pl.ds(s1, block), pp * 2 * block:(pp + 1) * 2 * block]
            o_ref[pp, k * block:(k + 1) * block, :] = jnp.where(lane < block, t0, t1)


PAIRS_PER_STEP = 4


def expand_dense(paired_weights, live_index):
    pair_count, wide, two_blocks = paired_weights.shape
    column_count, live_count = live_index.shape
    block_size = two_blocks // 2
    features = column_count * block_size
    targets = jnp.arange(column_count, dtype=jnp.int32)
    hit = live_index[:, :, None] == targets[None, None, :]
    k_ids = jnp.arange(live_count, dtype=jnp.int32)[None, :, None]
    inverse = jnp.where(
        jnp.any(hit, axis=1), jnp.sum(jnp.where(hit, k_ids, 0), axis=1), -1
    ).astype(jnp.int32)
    return pl.pallas_call(
        expand_kernel,
        out_shape=jax.ShapeDtypeStruct((features, features), paired_weights.dtype),
        grid_spec=pltpu.PrefetchScalarGridSpec(
            num_scalar_prefetch=1,
            grid=(pair_count // PAIRS_PER_STEP,),
            in_specs=[pl.BlockSpec((PAIRS_PER_STEP, wide, two_blocks), lambda q, tbl: (q, 0, 0))],
            out_specs=pl.BlockSpec((features, PAIRS_PER_STEP * two_blocks), lambda q, tbl: (0, q)),
        ),
        cost_estimate=pl.CostEstimate(
            flops=0, transcendentals=0, bytes_accessed=3 * pair_count * wide * two_blocks * 2
        ),
    )(inverse.reshape(-1), paired_weights)


def pack_dense(dense_grad, live_index):
    column_count, live_count = live_index.shape
    features = dense_grad.shape[0]
    block_size = features // column_count
    wide = live_count * block_size
    pair_count = column_count // 2
    return pl.pallas_call(
        pack_kernel,
        out_shape=jax.ShapeDtypeStruct((pair_count, wide, 2 * block_size), dense_grad.dtype),
        grid_spec=pltpu.PrefetchScalarGridSpec(
            num_scalar_prefetch=1,
            grid=(pair_count // PAIRS_PER_STEP,),
            in_specs=[
                pl.BlockSpec((features, PAIRS_PER_STEP * 2 * block_size), lambda q, tbl: (0, q))
            ],
            out_specs=pl.BlockSpec((PAIRS_PER_STEP, wide, 2 * block_size), lambda q, tbl: (q, 0, 0)),
        ),
        cost_estimate=pl.CostEstimate(
            flops=0, transcendentals=0, bytes_accessed=3 * pair_count * wide * 2 * block_size * 2
        ),
    )(live_index.reshape(-1).astype(jnp.int32), dense_grad)


def spread_kernel(x_ref, o_ref, recv_ref, send_sem, recv_sem):
    count = recv_ref.shape[0]
    me = lax.axis_index("dp")
    pipe = lax.axis_index("pipe")
    barrier = pltpu.get_barrier_semaphore()
    for step in range(1, count):
        peer = lax.rem(me + step, count)
        pl.semaphore_signal(barrier, inc=1, device_id=(pipe, peer), device_id_type=pl.DeviceIdType.MESH)
    pl.semaphore_wait(barrier, count - 1)
    copies = []
    for step in range(1, count):
        peer = lax.rem(me + step, count)
        copy = pltpu.make_async_remote_copy(
            src_ref=x_ref,
            dst_ref=recv_ref.at[me],
            send_sem=send_sem.at[step],
            recv_sem=recv_sem.at[me],
            device_id=(pipe, peer),
            device_id_type=pl.DeviceIdType.MESH,
        )
        copy.start()
        copies.append(copy)
    total = x_ref[...]
    for step in range(1, count):
        source = lax.rem(me + count - step, count)
        arrival = pltpu.make_async_remote_copy(
            src_ref=x_ref,
            dst_ref=recv_ref.at[source],
            send_sem=send_sem.at[step],
            recv_sem=recv_sem.at[source],
            device_id=(pipe, source),
            device_id_type=pl.DeviceIdType.MESH,
        )
        arrival.wait_recv()
        total = total + recv_ref[source]
    for copy in copies:
        copy.wait_send()
    o_ref[...] = total


def spread_sum(values):
    count = lax.axis_size("dp")
    padded = jnp.zeros((8, 128), jnp.float32).at[0, : values.shape[0]].set(values)
    out = pl.pallas_call(
        spread_kernel,
        out_shape=jax.ShapeDtypeStruct((8, 128), jnp.float32),
        in_specs=[pl.BlockSpec(memory_space=pltpu.VMEM)],
        out_specs=pl.BlockSpec(memory_space=pltpu.VMEM),
        scratch_shapes=[
            pltpu.VMEM((count, 8, 128), jnp.float32),
            pltpu.SemaphoreType.DMA((count,)),
            pltpu.SemaphoreType.DMA((count,)),
        ],
        compiler_params=pltpu.CompilerParams(collective_id=0, has_side_effects=True),
    )(padded)
    return out[0, : values.shape[0]]


def layer_forward(entering, dense_w):
    as_float = entering.astype(jnp.float32)
    inverse_rms = lax.rsqrt(jnp.mean(as_float * as_float, axis=-1, keepdims=True) + 1e-05)
    normed = (as_float * inverse_rms).astype(jnp.bfloat16)
    pre_act = jnp.dot(normed, dense_w, preferred_element_type=jnp.float32)
    return ((as_float + jax.nn.silu(pre_act)).astype(jnp.bfloat16), normed, pre_act)


def layer_backward(arriving, entering, pre_act, dense_w):
    as_float = entering.astype(jnp.float32)
    inverse_rms = lax.rsqrt(jnp.mean(as_float * as_float, axis=-1, keepdims=True) + 1e-05)
    sigmoid_z = jax.nn.sigmoid(pre_act)
    grad_pre = (
        arriving.astype(jnp.float32) * (sigmoid_z * (1.0 + pre_act * (1.0 - sigmoid_z)))
    ).astype(jnp.bfloat16)
    grad_normed = lax.dot_general(
        grad_pre, dense_w, (((1,), (1,)), ((), ())), preferred_element_type=jnp.float32
    )
    scaled = as_float * inverse_rms
    leaving = (
        arriving.astype(jnp.float32)
        + inverse_rms
        * (grad_normed - scaled * jnp.mean(grad_normed * scaled, axis=-1, keepdims=True))
    ).astype(jnp.bfloat16)
    return (leaving, grad_pre)


def local(x_in, cotangent, weights, live_rows, moment, second):
    sections = lax.axis_size("pipe")
    section_index = lax.axis_index("pipe")
    group = 2
    micro_total, micro_tokens, features = x_in.shape
    micro_count = micro_total // group
    tokens = micro_tokens * group
    x_in = x_in.reshape(micro_count, tokens, features)
    cotangent = cotangent.reshape(micro_count, tokens, features)
    column_count = live_rows.shape[1]
    live_count = live_rows.shape[2]
    own_columns = weights.shape[1]
    block_size = weights.shape[2]
    live_index = live_rows[0]
    own_pair = weights[0].transpose(2, 0, 1).reshape(1, live_count * block_size, own_columns * block_size)
    paired_weights = lax.all_gather(own_pair, "dp", axis=0, tiled=True)
    dense_w = expand_dense(paired_weights, live_index)
    tick_count = micro_count + sections - 1

    incoming = jnp.zeros((tokens, features), jnp.bfloat16)
    kept_in, kept_normed, kept_pre = [], [], []
    for tick_index in range(tick_count):
        entering = jnp.where(section_index == 0, x_in[min(tick_index, micro_count - 1)], incoming)
        outgoing, normed, pre_act = layer_forward(entering, dense_w)
        kept_in.append(entering)
        kept_normed.append(normed)
        kept_pre.append(pre_act)
        if tick_index + 1 < tick_count:
            incoming = shifted(outgoing, "pipe", 1)
    saved_in = lax.dynamic_slice_in_dim(jnp.stack(kept_in), section_index, micro_count, 0)
    saved_normed = lax.dynamic_slice_in_dim(jnp.stack(kept_normed), section_index, micro_count, 0)
    saved_pre = lax.dynamic_slice_in_dim(jnp.stack(kept_pre), section_index, micro_count, 0)

    incoming_grad = jnp.zeros((tokens, features), jnp.bfloat16)
    kept_grad = []
    for tick_index in range(tick_count):
        slot_index = jnp.clip(tick_index - (sections - 1 - section_index), 0, micro_count - 1)
        arriving = jnp.where(
            section_index == sections - 1,
            cotangent[min(tick_index, micro_count - 1)],
            incoming_grad,
        )
        leaving, grad_pre = layer_backward(
            arriving, saved_in[slot_index], saved_pre[slot_index], dense_w
        )
        kept_grad.append(grad_pre)
        if tick_index + 1 < tick_count:
            incoming_grad = shifted(leaving, "pipe", -1)
    saved_grad = lax.dynamic_slice_in_dim(
        jnp.stack(kept_grad), sections - 1 - section_index, micro_count, 0
    )

    all_rows = micro_count * tokens
    inverse_tokens = 1.0 / (all_rows * lax.axis_size("dp"))
    dense_grad = (
        lax.dot_general(
            saved_normed.reshape(all_rows, features),
            saved_grad.reshape(all_rows, features),
            (((0,), (0,)), ((), ())),
            preferred_element_type=jnp.float32,
        )
        * inverse_tokens
    ).astype(jnp.bfloat16)
    partial = pack_dense(dense_grad, live_index)
    own_grad = lax.psum_scatter(partial, "dp", scatter_dimension=0, tiled=True)
    gradient = (
        own_grad.reshape(live_count * block_size, own_columns, block_size)
        .transpose(1, 2, 0)
        .astype(jnp.float32)
    )

    rate = 0.1 / math.sqrt(live_count * block_size)
    moment_new = 0.9 * moment[0] + 0.1 * gradient
    second_new = 0.95 * second[0] + 0.05 * gradient * gradient
    stepped = weights[0].astype(jnp.float32) - rate * moment_new / (jnp.sqrt(second_new) + 1e-08)
    own_index = lax.dynamic_slice_in_dim(
        live_index, lax.axis_index("dp") * own_columns, own_columns, 0
    )
    blocked = stepped.reshape(own_columns, block_size, live_count, block_size)
    magnitude = jnp.sqrt(jnp.sum(blocked * blocked, axis=(1, 3)))
    leafed = (
        blocked * shrink(magnitude, 0.15 * math.sqrt(block_size / live_count))[:, None, :, None]
    )
    block_squares = jnp.sum(leafed * leafed, axis=(1, 3))
    head_count = features // HEAD
    head_index = own_index // (HEAD // block_size)
    onehot = (
        head_index[:, :, None] == jnp.arange(head_count, dtype=jnp.int32)[None, None, :]
    ).astype(jnp.float32)
    head_partial = jnp.sum(onehot * block_squares[:, :, None], axis=(0, 1))
    head_squares = spread_sum(head_partial)
    head_factor = shrink(jnp.sqrt(head_squares), 0.45 * math.sqrt(HEAD))
    headed = leafed * jnp.sum(onehot * head_factor[None, None, :], axis=2)[:, None, :, None]
    layer_squares = jnp.sum(head_factor * head_factor * head_squares)
    layer_factor = shrink(jnp.sqrt(layer_squares), 0.45 * math.sqrt(features))
    weights_out = (
        (headed * layer_factor)
        .astype(jnp.bfloat16)
        .reshape(own_columns, block_size, live_count * block_size)
    )
    return (weights_out[None], moment_new[None], second_new[None])


def solution(mesh):
    placed = (
        P(None, "dp", None),
        P(None, "dp", None),
        P("pipe", "dp", None, None),
        P("pipe", None, None),
        P("pipe", "dp", None, None),
        P("pipe", "dp", None, None),
    )
    return jax.shard_map(
        local,
        mesh=mesh,
        in_specs=placed,
        out_specs=(
            P("pipe", "dp", None, None),
            P("pipe", "dp", None, None),
            P("pipe", "dp", None, None),
        ),
        check_vma=False,
    )
```

```python
import math

import jax
import jax.numpy as jnp
from jax import lax
from jax.experimental import pallas as pl
from jax.experimental.pallas import tpu as pltpu
from jax.sharding import PartitionSpec as P

HEAD = 128


def shifted(value, axis, steps):
    count = lax.axis_size(axis)
    leading, last = (max(0, -steps), min(count, count - steps))
    return lax.ppermute(value, axis, [(source, source + steps) for source in range(leading, last)])


def shrink(magnitude, threshold):
    return jnp.maximum(magnitude - threshold, 0.0) / jnp.maximum(magnitude, threshold)


def expand_kernel(table_ref, t_ref, o_ref):
    per_step = t_ref.shape[0]
    block = 64
    blocks = o_ref.shape[0] // block
    lane = lax.broadcasted_iota(jnp.int32, (block, 2 * block), 1)
    for pp in range(per_step):
        p = pl.program_id(0) * per_step + pp
        for r in range(blocks):
            k0 = table_ref[(2 * p) * blocks + r]
            k1 = table_ref[(2 * p + 1) * blocks + r]
            s0 = pl.multiple_of(jnp.maximum(k0, 0) * block, block)
            s1 = pl.multiple_of(jnp.maximum(k1, 0) * block, block)
            t0 = t_ref[pp, pl.ds(s0, block), :]
            t1 = t_ref[pp, pl.ds(s1, block), :]
            zero = jnp.zeros_like(t0)
            t0 = jnp.where(k0 >= 0, t0, zero)
            t1 = jnp.where(k1 >= 0, t1, zero)
            o_ref[r * block:(r + 1) * block, pp * 2 * block:(pp + 1) * 2 * block] = jnp.where(
                lane < block, t0, t1
            )


def pack_kernel(table_ref, g_ref, o_ref):
    per_step = o_ref.shape[0]
    block = 64
    live_count = o_ref.shape[1] // block
    lane = lax.broadcasted_iota(jnp.int32, (block, 2 * block), 1)
    for pp in range(per_step):
        p = pl.program_id(0) * per_step + pp
        for k in range(live_count):
            r0 = table_ref[(2 * p) * live_count + k]
            r1 = table_ref[(2 * p + 1) * live_count + k]
            s0 = pl.multiple_of(r0 * block, block)
            s1 = pl.multiple_of(r1 * block, block)
            t0 = g_ref[pl.ds(s0, block), pp * 2 * block:(pp + 1) * 2 * block]
            t1 = g_ref[pl.ds(s1, block), pp * 2 * block:(pp + 1) * 2 * block]
            o_ref[pp, k * block:(k + 1) * block, :] = jnp.where(lane < block, t0, t1)


PAIRS_PER_STEP = 8


def expand_dense(paired_weights, live_index):
    pair_count, wide, two_blocks = paired_weights.shape
    column_count, live_count = live_index.shape
    block_size = two_blocks // 2
    features = column_count * block_size
    targets = jnp.arange(column_count, dtype=jnp.int32)
    hit = live_index[:, :, None] == targets[None, None, :]
    k_ids = jnp.arange(live_count, dtype=jnp.int32)[None, :, None]
    inverse = jnp.where(
        jnp.any(hit, axis=1), jnp.sum(jnp.where(hit, k_ids, 0), axis=1), -1
    ).astype(jnp.int32)
    return pl.pallas_call(
        expand_kernel,
        out_shape=jax.ShapeDtypeStruct((features, features), paired_weights.dtype),
        grid_spec=pltpu.PrefetchScalarGridSpec(
            num_scalar_prefetch=1,
            grid=(pair_count // PAIRS_PER_STEP,),
            in_specs=[pl.BlockSpec((PAIRS_PER_STEP, wide, two_blocks), lambda q, tbl: (q, 0, 0))],
            out_specs=pl.BlockSpec((features, PAIRS_PER_STEP * two_blocks), lambda q, tbl: (0, q)),
        ),
        cost_estimate=pl.CostEstimate(
            flops=0, transcendentals=0, bytes_accessed=3 * pair_count * wide * two_blocks * 2
        ),
    )(inverse.reshape(-1), paired_weights)


def pack_dense(dense_grad, live_index):
    column_count, live_count = live_index.shape
    features = dense_grad.shape[0]
    block_size = features // column_count
    wide = live_count * block_size
    pair_count = column_count // 2
    return pl.pallas_call(
        pack_kernel,
        out_shape=jax.ShapeDtypeStruct((pair_count, wide, 2 * block_size), dense_grad.dtype),
        grid_spec=pltpu.PrefetchScalarGridSpec(
            num_scalar_prefetch=1,
            grid=(pair_count // PAIRS_PER_STEP,),
            in_specs=[
                pl.BlockSpec((features, PAIRS_PER_STEP * 2 * block_size), lambda q, tbl: (0, q))
            ],
            out_specs=pl.BlockSpec((PAIRS_PER_STEP, wide, 2 * block_size), lambda q, tbl: (q, 0, 0)),
        ),
        cost_estimate=pl.CostEstimate(
            flops=0, transcendentals=0, bytes_accessed=3 * pair_count * wide * 2 * block_size * 2
        ),
    )(live_index.reshape(-1).astype(jnp.int32), dense_grad)


def spread_kernel(x_ref, o_ref, recv_ref, send_sem, recv_sem):
    count = recv_ref.shape[0]
    me = lax.axis_index("dp")
    pipe = lax.axis_index("pipe")
    barrier = pltpu.get_barrier_semaphore()
    for step in range(1, count):
        peer = lax.rem(me + step, count)
        pl.semaphore_signal(barrier, inc=1, device_id=(pipe, peer), device_id_type=pl.DeviceIdType.MESH)
    pl.semaphore_wait(barrier, count - 1)
    copies = []
    for step in range(1, count):
        peer = lax.rem(me + step, count)
        copy = pltpu.make_async_remote_copy(
            src_ref=x_ref,
            dst_ref=recv_ref.at[me],
            send_sem=send_sem.at[step],
            recv_sem=recv_sem.at[me],
            device_id=(pipe, peer),
            device_id_type=pl.DeviceIdType.MESH,
        )
        copy.start()
        copies.append(copy)
    total = x_ref[...]
    for step in range(1, count):
        source = lax.rem(me + count - step, count)
        arrival = pltpu.make_async_remote_copy(
            src_ref=x_ref,
            dst_ref=recv_ref.at[source],
            send_sem=send_sem.at[step],
            recv_sem=recv_sem.at[source],
            device_id=(pipe, source),
            device_id_type=pl.DeviceIdType.MESH,
        )
        arrival.wait_recv()
        total = total + recv_ref[source]
    for copy in copies:
        copy.wait_send()
    o_ref[...] = total


def spread_sum(values):
    count = lax.axis_size("dp")
    padded = jnp.zeros((8, 128), jnp.float32).at[0, : values.shape[0]].set(values)
    out = pl.pallas_call(
        spread_kernel,
        out_shape=jax.ShapeDtypeStruct((8, 128), jnp.float32),
        in_specs=[pl.BlockSpec(memory_space=pltpu.VMEM)],
        out_specs=pl.BlockSpec(memory_space=pltpu.VMEM),
        scratch_shapes=[
            pltpu.VMEM((count, 8, 128), jnp.float32),
            pltpu.SemaphoreType.DMA((count,)),
            pltpu.SemaphoreType.DMA((count,)),
        ],
        compiler_params=pltpu.CompilerParams(collective_id=0, has_side_effects=True),
    )(padded)
    return out[0, : values.shape[0]]


def layer_forward(entering, dense_w):
    as_float = entering.astype(jnp.float32)
    inverse_rms = lax.rsqrt(jnp.mean(as_float * as_float, axis=-1, keepdims=True) + 1e-05)
    normed = (as_float * inverse_rms).astype(jnp.bfloat16)
    pre_act = jnp.dot(normed, dense_w, preferred_element_type=jnp.float32)
    return ((as_float + jax.nn.silu(pre_act)).astype(jnp.bfloat16), normed, pre_act)


def layer_backward(arriving, entering, pre_act, dense_w):
    as_float = entering.astype(jnp.float32)
    inverse_rms = lax.rsqrt(jnp.mean(as_float * as_float, axis=-1, keepdims=True) + 1e-05)
    sigmoid_z = jax.nn.sigmoid(pre_act)
    grad_pre = (
        arriving.astype(jnp.float32) * (sigmoid_z * (1.0 + pre_act * (1.0 - sigmoid_z)))
    ).astype(jnp.bfloat16)
    grad_normed = lax.dot_general(
        grad_pre, dense_w, (((1,), (1,)), ((), ())), preferred_element_type=jnp.float32
    )
    scaled = as_float * inverse_rms
    leaving = (
        arriving.astype(jnp.float32)
        + inverse_rms
        * (grad_normed - scaled * jnp.mean(grad_normed * scaled, axis=-1, keepdims=True))
    ).astype(jnp.bfloat16)
    return (leaving, grad_pre)


def local(x_in, cotangent, weights, live_rows, moment, second):
    sections = lax.axis_size("pipe")
    section_index = lax.axis_index("pipe")
    group = 2
    micro_total, micro_tokens, features = x_in.shape
    micro_count = micro_total // group
    tokens = micro_tokens * group
    x_in = x_in.reshape(micro_count, tokens, features)
    cotangent = cotangent.reshape(micro_count, tokens, features)
    column_count = live_rows.shape[1]
    live_count = live_rows.shape[2]
    own_columns = weights.shape[1]
    block_size = weights.shape[2]
    live_index = live_rows[0]
    own_pair = weights[0].transpose(2, 0, 1).reshape(1, live_count * block_size, own_columns * block_size)
    paired_weights = lax.all_gather(own_pair, "dp", axis=0, tiled=True)
    dense_w = expand_dense(paired_weights, live_index)
    tick_count = micro_count + sections - 1

    incoming = jnp.zeros((tokens, features), jnp.bfloat16)
    kept_in, kept_normed, kept_pre = [], [], []
    for tick_index in range(tick_count):
        entering = jnp.where(section_index == 0, x_in[min(tick_index, micro_count - 1)], incoming)
        outgoing, normed, pre_act = layer_forward(entering, dense_w)
        kept_in.append(entering)
        kept_normed.append(normed)
        kept_pre.append(pre_act)
        if tick_index + 1 < tick_count:
            incoming = shifted(outgoing, "pipe", 1)
    saved_in = lax.dynamic_slice_in_dim(jnp.stack(kept_in), section_index, micro_count, 0)
    saved_normed = lax.dynamic_slice_in_dim(jnp.stack(kept_normed), section_index, micro_count, 0)
    saved_pre = lax.dynamic_slice_in_dim(jnp.stack(kept_pre), section_index, micro_count, 0)

    incoming_grad = jnp.zeros((tokens, features), jnp.bfloat16)
    kept_grad = []
    for tick_index in range(tick_count):
        slot_index = jnp.clip(tick_index - (sections - 1 - section_index), 0, micro_count - 1)
        arriving = jnp.where(
            section_index == sections - 1,
            cotangent[min(tick_index, micro_count - 1)],
            incoming_grad,
        )
        leaving, grad_pre = layer_backward(
            arriving, saved_in[slot_index], saved_pre[slot_index], dense_w
        )
        kept_grad.append(grad_pre)
        if tick_index + 1 < tick_count:
            incoming_grad = shifted(leaving, "pipe", -1)
    saved_grad = lax.dynamic_slice_in_dim(
        jnp.stack(kept_grad), sections - 1 - section_index, micro_count, 0
    )

    all_rows = micro_count * tokens
    inverse_tokens = 1.0 / (all_rows * lax.axis_size("dp"))
    dense_grad = (
        lax.dot_general(
            saved_normed.reshape(all_rows, features),
            saved_grad.reshape(all_rows, features),
            (((0,), (0,)), ((), ())),
            preferred_element_type=jnp.float32,
        )
        * inverse_tokens
    ).astype(jnp.bfloat16)
    partial = pack_dense(dense_grad, live_index)
    own_grad = lax.psum_scatter(partial, "dp", scatter_dimension=0, tiled=True)
    gradient = (
        own_grad.reshape(live_count * block_size, own_columns, block_size)
        .transpose(1, 2, 0)
        .astype(jnp.float32)
    )

    rate = 0.1 / math.sqrt(live_count * block_size)
    moment_new = 0.9 * moment[0] + 0.1 * gradient
    second_new = 0.95 * second[0] + 0.05 * gradient * gradient
    stepped = weights[0].astype(jnp.float32) - rate * moment_new / (jnp.sqrt(second_new) + 1e-08)
    own_index = lax.dynamic_slice_in_dim(
        live_index, lax.axis_index("dp") * own_columns, own_columns, 0
    )
    blocked = stepped.reshape(own_columns, block_size, live_count, block_size)
    magnitude = jnp.sqrt(jnp.sum(blocked * blocked, axis=(1, 3)))
    leafed = (
        blocked * shrink(magnitude, 0.15 * math.sqrt(block_size / live_count))[:, None, :, None]
    )
    block_squares = jnp.sum(leafed * leafed, axis=(1, 3))
    head_count = features // HEAD
    head_index = own_index // (HEAD // block_size)
    onehot = (
        head_index[:, :, None] == jnp.arange(head_count, dtype=jnp.int32)[None, None, :]
    ).astype(jnp.float32)
    head_partial = jnp.sum(onehot * block_squares[:, :, None], axis=(0, 1))
    head_squares = spread_sum(head_partial)
    head_factor = shrink(jnp.sqrt(head_squares), 0.45 * math.sqrt(HEAD))
    headed = leafed * jnp.sum(onehot * head_factor[None, None, :], axis=2)[:, None, :, None]
    layer_squares = jnp.sum(head_factor * head_factor * head_squares)
    layer_factor = shrink(jnp.sqrt(layer_squares), 0.45 * math.sqrt(features))
    weights_out = (
        (headed * layer_factor)
        .astype(jnp.bfloat16)
        .reshape(own_columns, block_size, live_count * block_size)
    )
    return (weights_out[None], moment_new[None], second_new[None])


def solution(mesh):
    placed = (
        P(None, "dp", None),
        P(None, "dp", None),
        P("pipe", "dp", None, None),
        P("pipe", None, None),
        P("pipe", "dp", None, None),
        P("pipe", "dp", None, None),
    )
    return jax.shard_map(
        local,
        mesh=mesh,
        in_specs=placed,
        out_specs=(
            P("pipe", "dp", None, None),
            P("pipe", "dp", None, None),
            P("pipe", "dp", None, None),
        ),
        check_vma=False,
    )
```

```python
import functools
import math

import jax
import jax.numpy as jnp
from jax import lax
from jax.experimental import pallas as pl
from jax.experimental.pallas import tpu as pltpu
from jax.sharding import PartitionSpec as P

HEAD = 128


def shifted(value, axis, steps):
    count = lax.axis_size(axis)
    leading, last = (max(0, -steps), min(count, count - steps))
    return lax.ppermute(value, axis, [(source, source + steps) for source in range(leading, last)])


def shrink(magnitude, threshold):
    return jnp.maximum(magnitude - threshold, 0.0) / jnp.maximum(magnitude, threshold)


def expand_kernel(table_ref, t_ref, o_ref):
    per_step = t_ref.shape[0]
    block = 64
    blocks = o_ref.shape[0] // block
    lane = lax.broadcasted_iota(jnp.int32, (block, 2 * block), 1)
    for pp in range(per_step):
        p = pl.program_id(0) * per_step + pp
        for r in range(blocks):
            k0 = table_ref[(2 * p) * blocks + r]
            k1 = table_ref[(2 * p + 1) * blocks + r]
            s0 = pl.multiple_of(jnp.maximum(k0, 0) * block, block)
            s1 = pl.multiple_of(jnp.maximum(k1, 0) * block, block)
            t0 = t_ref[pp, pl.ds(s0, block), :]
            t1 = t_ref[pp, pl.ds(s1, block), :]
            zero = jnp.zeros_like(t0)
            t0 = jnp.where(k0 >= 0, t0, zero)
            t1 = jnp.where(k1 >= 0, t1, zero)
            o_ref[r * block:(r + 1) * block, pp * 2 * block:(pp + 1) * 2 * block] = jnp.where(
                lane < block, t0, t1
            )


def grad_pack_kernel(scale, table_ref, ut_ref, gz_ref, o_ref, g_ref):
    per_step = o_ref.shape[0]
    block = 64
    live_count = o_ref.shape[1] // block
    rows = g_ref.shape[0]
    chunk = 512
    for c in range(rows // chunk):
        g_ref[c * chunk:(c + 1) * chunk, :] = (
            jnp.dot(ut_ref[c * chunk:(c + 1) * chunk, :], gz_ref[...], preferred_element_type=jnp.float32)
            * scale
        ).astype(g_ref.dtype)
    lane = lax.broadcasted_iota(jnp.int32, (block, 2 * block), 1)
    for pp in range(per_step):
        p = pl.program_id(0) * per_step + pp
        for k in range(live_count):
            r0 = table_ref[(2 * p) * live_count + k]
            r1 = table_ref[(2 * p + 1) * live_count + k]
            s0 = pl.multiple_of(r0 * block, block)
            s1 = pl.multiple_of(r1 * block, block)
            t0 = g_ref[pl.ds(s0, block), pp * 2 * block:(pp + 1) * 2 * block]
            t1 = g_ref[pl.ds(s1, block), pp * 2 * block:(pp + 1) * 2 * block]
            o_ref[pp, k * block:(k + 1) * block, :] = jnp.where(lane < block, t0, t1)


PAIRS_PER_STEP = 4


def expand_dense(paired_weights, live_index):
    pair_count, wide, two_blocks = paired_weights.shape
    column_count, live_count = live_index.shape
    block_size = two_blocks // 2
    features = column_count * block_size
    targets = jnp.arange(column_count, dtype=jnp.int32)
    hit = live_index[:, :, None] == targets[None, None, :]
    k_ids = jnp.arange(live_count, dtype=jnp.int32)[None, :, None]
    inverse = jnp.where(
        jnp.any(hit, axis=1), jnp.sum(jnp.where(hit, k_ids, 0), axis=1), -1
    ).astype(jnp.int32)
    return pl.pallas_call(
        expand_kernel,
        out_shape=jax.ShapeDtypeStruct((features, features), paired_weights.dtype),
        grid_spec=pltpu.PrefetchScalarGridSpec(
            num_scalar_prefetch=1,
            grid=(pair_count // PAIRS_PER_STEP,),
            in_specs=[pl.BlockSpec((PAIRS_PER_STEP, wide, two_blocks), lambda q, tbl: (q, 0, 0))],
            out_specs=pl.BlockSpec((features, PAIRS_PER_STEP * two_blocks), lambda q, tbl: (0, q)),
        ),
        cost_estimate=pl.CostEstimate(
            flops=0, transcendentals=0, bytes_accessed=3 * pair_count * wide * two_blocks * 2
        ),
    )(inverse.reshape(-1), paired_weights)


def grad_pack(normed_rows, grad_rows, live_index, scale):
    column_count, live_count = live_index.shape
    all_rows, features = normed_rows.shape
    block_size = features // column_count
    wide = live_count * block_size
    pair_count = column_count // 2
    stripe = PAIRS_PER_STEP * 2 * block_size
    return pl.pallas_call(
        functools.partial(grad_pack_kernel, scale),
        out_shape=jax.ShapeDtypeStruct((pair_count, wide, 2 * block_size), jnp.bfloat16),
        grid_spec=pltpu.PrefetchScalarGridSpec(
            num_scalar_prefetch=1,
            grid=(pair_count // PAIRS_PER_STEP,),
            in_specs=[
                pl.BlockSpec((features, all_rows), lambda q, tbl: (0, 0)),
                pl.BlockSpec((all_rows, stripe), lambda q, tbl: (0, q)),
            ],
            out_specs=pl.BlockSpec((PAIRS_PER_STEP, wide, 2 * block_size), lambda q, tbl: (q, 0, 0)),
            scratch_shapes=[pltpu.VMEM((features, stripe), jnp.bfloat16)],
        ),
        cost_estimate=pl.CostEstimate(
            flops=2 * all_rows * features * features,
            transcendentals=0,
            bytes_accessed=2 * all_rows * features * 2 + pair_count * wide * 2 * block_size * 2,
        ),
    )(live_index.reshape(-1).astype(jnp.int32), normed_rows.T, grad_rows)


def spread_kernel(x_ref, o_ref, recv_ref, send_sem, recv_sem):
    count = recv_ref.shape[0]
    me = lax.axis_index("dp")
    pipe = lax.axis_index("pipe")
    barrier = pltpu.get_barrier_semaphore()
    for step in range(1, count):
        peer = lax.rem(me + step, count)
        pl.semaphore_signal(barrier, inc=1, device_id=(pipe, peer), device_id_type=pl.DeviceIdType.MESH)
    pl.semaphore_wait(barrier, count - 1)
    copies = []
    for step in range(1, count):
        peer = lax.rem(me + step, count)
        copy = pltpu.make_async_remote_copy(
            src_ref=x_ref,
            dst_ref=recv_ref.at[me],
            send_sem=send_sem.at[step],
            recv_sem=recv_sem.at[me],
            device_id=(pipe, peer),
            device_id_type=pl.DeviceIdType.MESH,
        )
        copy.start()
        copies.append(copy)
    total = x_ref[...]
    for step in range(1, count):
        source = lax.rem(me + count - step, count)
        arrival = pltpu.make_async_remote_copy(
            src_ref=x_ref,
            dst_ref=recv_ref.at[source],
            send_sem=send_sem.at[step],
            recv_sem=recv_sem.at[source],
            device_id=(pipe, source),
            device_id_type=pl.DeviceIdType.MESH,
        )
        arrival.wait_recv()
        total = total + recv_ref[source]
    for copy in copies:
        copy.wait_send()
    o_ref[...] = total


def spread_sum(values):
    count = lax.axis_size("dp")
    padded = jnp.zeros((8, 128), jnp.float32).at[0, : values.shape[0]].set(values)
    out = pl.pallas_call(
        spread_kernel,
        out_shape=jax.ShapeDtypeStruct((8, 128), jnp.float32),
        in_specs=[pl.BlockSpec(memory_space=pltpu.VMEM)],
        out_specs=pl.BlockSpec(memory_space=pltpu.VMEM),
        scratch_shapes=[
            pltpu.VMEM((count, 8, 128), jnp.float32),
            pltpu.SemaphoreType.DMA((count,)),
            pltpu.SemaphoreType.DMA((count,)),
        ],
        compiler_params=pltpu.CompilerParams(collective_id=0, has_side_effects=True),
    )(padded)
    return out[0, : values.shape[0]]


def layer_forward(entering, dense_w):
    as_float = entering.astype(jnp.float32)
    inverse_rms = lax.rsqrt(jnp.mean(as_float * as_float, axis=-1, keepdims=True) + 1e-05)
    normed = (as_float * inverse_rms).astype(jnp.bfloat16)
    pre_act = jnp.dot(normed, dense_w, preferred_element_type=jnp.float32)
    return ((as_float + jax.nn.silu(pre_act)).astype(jnp.bfloat16), normed, pre_act)


def layer_backward(arriving, entering, pre_act, dense_w):
    as_float = entering.astype(jnp.float32)
    inverse_rms = lax.rsqrt(jnp.mean(as_float * as_float, axis=-1, keepdims=True) + 1e-05)
    sigmoid_z = jax.nn.sigmoid(pre_act)
    grad_pre = (
        arriving.astype(jnp.float32) * (sigmoid_z * (1.0 + pre_act * (1.0 - sigmoid_z)))
    ).astype(jnp.bfloat16)
    grad_normed = lax.dot_general(
        grad_pre, dense_w, (((1,), (1,)), ((), ())), preferred_element_type=jnp.float32
    )
    scaled = as_float * inverse_rms
    leaving = (
        arriving.astype(jnp.float32)
        + inverse_rms
        * (grad_normed - scaled * jnp.mean(grad_normed * scaled, axis=-1, keepdims=True))
    ).astype(jnp.bfloat16)
    return (leaving, grad_pre)


def local(x_in, cotangent, weights, live_rows, moment, second):
    sections = lax.axis_size("pipe")
    section_index = lax.axis_index("pipe")
    group = 2
    micro_total, micro_tokens, features = x_in.shape
    micro_count = micro_total // group
    tokens = micro_tokens * group
    x_in = x_in.reshape(micro_count, tokens, features)
    cotangent = cotangent.reshape(micro_count, tokens, features)
    column_count = live_rows.shape[1]
    live_count = live_rows.shape[2]
    own_columns = weights.shape[1]
    block_size = weights.shape[2]
    live_index = live_rows[0]
    own_pair = weights[0].transpose(2, 0, 1).reshape(1, live_count * block_size, own_columns * block_size)
    paired_weights = lax.all_gather(own_pair, "dp", axis=0, tiled=True)
    dense_w = expand_dense(paired_weights, live_index)
    tick_count = micro_count + sections - 1

    incoming = jnp.zeros((tokens, features), jnp.bfloat16)
    kept_in, kept_normed, kept_pre = [], [], []
    for tick_index in range(tick_count):
        entering = jnp.where(section_index == 0, x_in[min(tick_index, micro_count - 1)], incoming)
        outgoing, normed, pre_act = layer_forward(entering, dense_w)
        kept_in.append(entering)
        kept_normed.append(normed)
        kept_pre.append(pre_act)
        if tick_index + 1 < tick_count:
            incoming = shifted(outgoing, "pipe", 1)
    saved_in = lax.dynamic_slice_in_dim(jnp.stack(kept_in), section_index, micro_count, 0)
    saved_normed = lax.dynamic_slice_in_dim(jnp.stack(kept_normed), section_index, micro_count, 0)
    saved_pre = lax.dynamic_slice_in_dim(jnp.stack(kept_pre), section_index, micro_count, 0)

    incoming_grad = jnp.zeros((tokens, features), jnp.bfloat16)
    kept_grad = []
    for tick_index in range(tick_count):
        slot_index = jnp.clip(tick_index - (sections - 1 - section_index), 0, micro_count - 1)
        arriving = jnp.where(
            section_index == sections - 1,
            cotangent[min(tick_index, micro_count - 1)],
            incoming_grad,
        )
        leaving, grad_pre = layer_backward(
            arriving, saved_in[slot_index], saved_pre[slot_index], dense_w
        )
        kept_grad.append(grad_pre)
        if tick_index + 1 < tick_count:
            incoming_grad = shifted(leaving, "pipe", -1)
    saved_grad = lax.dynamic_slice_in_dim(
        jnp.stack(kept_grad), sections - 1 - section_index, micro_count, 0
    )

    all_rows = micro_count * tokens
    inverse_tokens = 1.0 / (all_rows * lax.axis_size("dp"))
    partial = grad_pack(
        saved_normed.reshape(all_rows, features),
        saved_grad.reshape(all_rows, features),
        live_index,
        inverse_tokens,
    )
    own_grad = lax.psum_scatter(partial, "dp", scatter_dimension=0, tiled=True)
    gradient = (
        own_grad.reshape(live_count * block_size, own_columns, block_size)
        .transpose(1, 2, 0)
        .astype(jnp.float32)
    )

    rate = 0.1 / math.sqrt(live_count * block_size)
    moment_new = 0.9 * moment[0] + 0.1 * gradient
    second_new = 0.95 * second[0] + 0.05 * gradient * gradient
    stepped = weights[0].astype(jnp.float32) - rate * moment_new / (jnp.sqrt(second_new) + 1e-08)
    own_index = lax.dynamic_slice_in_dim(
        live_index, lax.axis_index("dp") * own_columns, own_columns, 0
    )
    blocked = stepped.reshape(own_columns, block_size, live_count, block_size)
    magnitude = jnp.sqrt(jnp.sum(blocked * blocked, axis=(1, 3)))
    leafed = (
        blocked * shrink(magnitude, 0.15 * math.sqrt(block_size / live_count))[:, None, :, None]
    )
    block_squares = jnp.sum(leafed * leafed, axis=(1, 3))
    head_count = features // HEAD
    head_index = own_index // (HEAD // block_size)
    onehot = (
        head_index[:, :, None] == jnp.arange(head_count, dtype=jnp.int32)[None, None, :]
    ).astype(jnp.float32)
    head_partial = jnp.sum(onehot * block_squares[:, :, None], axis=(0, 1))
    head_squares = spread_sum(head_partial)
    head_factor = shrink(jnp.sqrt(head_squares), 0.45 * math.sqrt(HEAD))
    headed = leafed * jnp.sum(onehot * head_factor[None, None, :], axis=2)[:, None, :, None]
    layer_squares = jnp.sum(head_factor * head_factor * head_squares)
    layer_factor = shrink(jnp.sqrt(layer_squares), 0.45 * math.sqrt(features))
    weights_out = (
        (headed * layer_factor)
        .astype(jnp.bfloat16)
        .reshape(own_columns, block_size, live_count * block_size)
    )
    return (weights_out[None], moment_new[None], second_new[None])


def solution(mesh):
    placed = (
        P(None, "dp", None),
        P(None, "dp", None),
        P("pipe", "dp", None, None),
        P("pipe", None, None),
        P("pipe", "dp", None, None),
        P("pipe", "dp", None, None),
    )
    return jax.shard_map(
        local,
        mesh=mesh,
        in_specs=placed,
        out_specs=(
            P("pipe", "dp", None, None),
            P("pipe", "dp", None, None),
            P("pipe", "dp", None, None),
        ),
        check_vma=False,
    )
```

```python
import functools
import math

import jax
import jax.numpy as jnp
from jax import lax
from jax.experimental import pallas as pl
from jax.experimental.pallas import tpu as pltpu
from jax.sharding import PartitionSpec as P

HEAD = 128


def shifted(value, axis, steps):
    count = lax.axis_size(axis)
    leading, last = (max(0, -steps), min(count, count - steps))
    return lax.ppermute(value, axis, [(source, source + steps) for source in range(leading, last)])


def shrink(magnitude, threshold):
    return jnp.maximum(magnitude - threshold, 0.0) / jnp.maximum(magnitude, threshold)


def expand_kernel(table_ref, t_ref, o_ref):
    per_step = t_ref.shape[0]
    block = 64
    blocks = o_ref.shape[0] // block
    lane = lax.broadcasted_iota(jnp.int32, (block, 2 * block), 1)
    for pp in range(per_step):
        p = pl.program_id(0) * per_step + pp
        for r in range(blocks):
            k0 = table_ref[(2 * p) * blocks + r]
            k1 = table_ref[(2 * p + 1) * blocks + r]
            s0 = pl.multiple_of(k0 * block, block)
            s1 = pl.multiple_of(k1 * block, block)
            t0 = t_ref[pp, pl.ds(s0, block), :]
            t1 = t_ref[pp, pl.ds(s1, block), :]
            o_ref[r * block:(r + 1) * block, pp * 2 * block:(pp + 1) * 2 * block] = jnp.where(
                lane < block, t0, t1
            )


def grad_pack_kernel(scale, table_ref, ut_ref, gz_ref, o_ref, g_ref):
    per_step = o_ref.shape[0]
    block = 64
    live_count = o_ref.shape[1] // block
    rows = g_ref.shape[0]
    chunk = 512
    for c in range(rows // chunk):
        g_ref[c * chunk:(c + 1) * chunk, :] = (
            jnp.dot(ut_ref[c * chunk:(c + 1) * chunk, :], gz_ref[...], preferred_element_type=jnp.float32)
            * scale
        ).astype(g_ref.dtype)
    lane = lax.broadcasted_iota(jnp.int32, (block, 2 * block), 1)
    for pp in range(per_step):
        p = pl.program_id(0) * per_step + pp
        for k in range(live_count):
            r0 = table_ref[(2 * p) * live_count + k]
            r1 = table_ref[(2 * p + 1) * live_count + k]
            s0 = pl.multiple_of(r0 * block, block)
            s1 = pl.multiple_of(r1 * block, block)
            t0 = g_ref[pl.ds(s0, block), pp * 2 * block:(pp + 1) * 2 * block]
            t1 = g_ref[pl.ds(s1, block), pp * 2 * block:(pp + 1) * 2 * block]
            o_ref[pp, k * block:(k + 1) * block, :] = jnp.where(lane < block, t0, t1)


PAIRS_PER_STEP = 4


def expand_dense(paired_weights, live_index):
    pair_count, wide, two_blocks = paired_weights.shape
    column_count, live_count = live_index.shape
    block_size = two_blocks // 2
    features = column_count * block_size
    targets = jnp.arange(column_count, dtype=jnp.int32)
    hit = live_index[:, :, None] == targets[None, None, :]
    k_ids = jnp.arange(live_count, dtype=jnp.int32)[None, :, None]
    inverse = jnp.where(
        jnp.any(hit, axis=1), jnp.sum(jnp.where(hit, k_ids, 0), axis=1), live_count
    ).astype(jnp.int32)
    return pl.pallas_call(
        expand_kernel,
        out_shape=jax.ShapeDtypeStruct((features, features), paired_weights.dtype),
        grid_spec=pltpu.PrefetchScalarGridSpec(
            num_scalar_prefetch=1,
            grid=(pair_count // PAIRS_PER_STEP,),
            in_specs=[pl.BlockSpec((PAIRS_PER_STEP, wide, two_blocks), lambda q, tbl: (q, 0, 0))],
            out_specs=pl.BlockSpec((features, PAIRS_PER_STEP * two_blocks), lambda q, tbl: (0, q)),
        ),
        cost_estimate=pl.CostEstimate(
            flops=0, transcendentals=0, bytes_accessed=3 * pair_count * wide * two_blocks * 2
        ),
    )(inverse.reshape(-1), paired_weights)


def grad_pack(normed_rows, grad_rows, live_index, scale):
    column_count, live_count = live_index.shape
    all_rows, features = normed_rows.shape
    block_size = features // column_count
    wide = live_count * block_size
    pair_count = column_count // 2
    stripe = PAIRS_PER_STEP * 2 * block_size
    return pl.pallas_call(
        functools.partial(grad_pack_kernel, scale),
        out_shape=jax.ShapeDtypeStruct((pair_count, wide, 2 * block_size), jnp.bfloat16),
        grid_spec=pltpu.PrefetchScalarGridSpec(
            num_scalar_prefetch=1,
            grid=(pair_count // PAIRS_PER_STEP,),
            in_specs=[
                pl.BlockSpec((features, all_rows), lambda q, tbl: (0, 0)),
                pl.BlockSpec((all_rows, stripe), lambda q, tbl: (0, q)),
            ],
            out_specs=pl.BlockSpec((PAIRS_PER_STEP, wide, 2 * block_size), lambda q, tbl: (q, 0, 0)),
            scratch_shapes=[pltpu.VMEM((features, stripe), jnp.bfloat16)],
        ),
        cost_estimate=pl.CostEstimate(
            flops=2 * all_rows * features * features,
            transcendentals=0,
            bytes_accessed=2 * all_rows * features * 2 + pair_count * wide * 2 * block_size * 2,
        ),
    )(live_index.reshape(-1).astype(jnp.int32), normed_rows.T, grad_rows)


def spread_kernel(x_ref, o_ref, recv_ref, send_sem, recv_sem):
    count = recv_ref.shape[0]
    me = lax.axis_index("dp")
    pipe = lax.axis_index("pipe")
    barrier = pltpu.get_barrier_semaphore()
    for step in range(1, count):
        peer = lax.rem(me + step, count)
        pl.semaphore_signal(barrier, inc=1, device_id=(pipe, peer), device_id_type=pl.DeviceIdType.MESH)
    pl.semaphore_wait(barrier, count - 1)
    copies = []
    for step in range(1, count):
        peer = lax.rem(me + step, count)
        copy = pltpu.make_async_remote_copy(
            src_ref=x_ref,
            dst_ref=recv_ref.at[me],
            send_sem=send_sem.at[step],
            recv_sem=recv_sem.at[me],
            device_id=(pipe, peer),
            device_id_type=pl.DeviceIdType.MESH,
        )
        copy.start()
        copies.append(copy)
    total = x_ref[...]
    for step in range(1, count):
        source = lax.rem(me + count - step, count)
        arrival = pltpu.make_async_remote_copy(
            src_ref=x_ref,
            dst_ref=recv_ref.at[source],
            send_sem=send_sem.at[step],
            recv_sem=recv_sem.at[source],
            device_id=(pipe, source),
            device_id_type=pl.DeviceIdType.MESH,
        )
        arrival.wait_recv()
        total = total + recv_ref[source]
    for copy in copies:
        copy.wait_send()
    o_ref[...] = total


def spread_sum(values):
    count = lax.axis_size("dp")
    padded = jnp.zeros((8, 128), jnp.float32).at[0, : values.shape[0]].set(values)
    out = pl.pallas_call(
        spread_kernel,
        out_shape=jax.ShapeDtypeStruct((8, 128), jnp.float32),
        in_specs=[pl.BlockSpec(memory_space=pltpu.VMEM)],
        out_specs=pl.BlockSpec(memory_space=pltpu.VMEM),
        scratch_shapes=[
            pltpu.VMEM((count, 8, 128), jnp.float32),
            pltpu.SemaphoreType.DMA((count,)),
            pltpu.SemaphoreType.DMA((count,)),
        ],
        compiler_params=pltpu.CompilerParams(collective_id=0, has_side_effects=True),
    )(padded)
    return out[0, : values.shape[0]]


def layer_forward(entering, dense_w):
    as_float = entering.astype(jnp.float32)
    inverse_rms = lax.rsqrt(jnp.mean(as_float * as_float, axis=-1, keepdims=True) + 1e-05)
    normed = (as_float * inverse_rms).astype(jnp.bfloat16)
    pre_act = jnp.dot(normed, dense_w, preferred_element_type=jnp.float32)
    return ((as_float + jax.nn.silu(pre_act)).astype(jnp.bfloat16), normed, pre_act)


def layer_backward(arriving, entering, pre_act, dense_w):
    as_float = entering.astype(jnp.float32)
    inverse_rms = lax.rsqrt(jnp.mean(as_float * as_float, axis=-1, keepdims=True) + 1e-05)
    sigmoid_z = jax.nn.sigmoid(pre_act)
    grad_pre = (
        arriving.astype(jnp.float32) * (sigmoid_z * (1.0 + pre_act * (1.0 - sigmoid_z)))
    ).astype(jnp.bfloat16)
    grad_normed = lax.dot_general(
        grad_pre, dense_w, (((1,), (1,)), ((), ())), preferred_element_type=jnp.float32
    )
    scaled = as_float * inverse_rms
    leaving = (
        arriving.astype(jnp.float32)
        + inverse_rms
        * (grad_normed - scaled * jnp.mean(grad_normed * scaled, axis=-1, keepdims=True))
    ).astype(jnp.bfloat16)
    return (leaving, grad_pre)


def local(x_in, cotangent, weights, live_rows, moment, second):
    sections = lax.axis_size("pipe")
    section_index = lax.axis_index("pipe")
    group = 2
    micro_total, micro_tokens, features = x_in.shape
    micro_count = micro_total // group
    tokens = micro_tokens * group
    x_in = x_in.reshape(micro_count, tokens, features)
    cotangent = cotangent.reshape(micro_count, tokens, features)
    column_count = live_rows.shape[1]
    live_count = live_rows.shape[2]
    own_columns = weights.shape[1]
    block_size = weights.shape[2]
    live_index = live_rows[0]
    own_pair = weights[0].transpose(2, 0, 1).reshape(1, live_count * block_size, own_columns * block_size)
    own_pair = jnp.pad(own_pair, ((0, 0), (0, block_size), (0, 0)))
    paired_weights = lax.all_gather(own_pair, "dp", axis=0, tiled=True)
    dense_w = expand_dense(paired_weights, live_index)
    tick_count = micro_count + sections - 1

    incoming = jnp.zeros((tokens, features), jnp.bfloat16)
    kept_in, kept_normed, kept_pre = [], [], []
    for tick_index in range(tick_count):
        entering = jnp.where(section_index == 0, x_in[min(tick_index, micro_count - 1)], incoming)
        outgoing, normed, pre_act = layer_forward(entering, dense_w)
        kept_in.append(entering)
        kept_normed.append(normed)
        kept_pre.append(pre_act)
        if tick_index + 1 < tick_count:
            incoming = shifted(outgoing, "pipe", 1)
    saved_in = lax.dynamic_slice_in_dim(jnp.stack(kept_in), section_index, micro_count, 0)
    saved_normed = lax.dynamic_slice_in_dim(jnp.stack(kept_normed), section_index, micro_count, 0)
    saved_pre = lax.dynamic_slice_in_dim(jnp.stack(kept_pre), section_index, micro_count, 0)

    incoming_grad = jnp.zeros((tokens, features), jnp.bfloat16)
    kept_grad = []
    for tick_index in range(tick_count):
        slot_index = jnp.clip(tick_index - (sections - 1 - section_index), 0, micro_count - 1)
        arriving = jnp.where(
            section_index == sections - 1,
            cotangent[min(tick_index, micro_count - 1)],
            incoming_grad,
        )
        leaving, grad_pre = layer_backward(
            arriving, saved_in[slot_index], saved_pre[slot_index], dense_w
        )
        kept_grad.append(grad_pre)
        if tick_index + 1 < tick_count:
            incoming_grad = shifted(leaving, "pipe", -1)
    saved_grad = lax.dynamic_slice_in_dim(
        jnp.stack(kept_grad), sections - 1 - section_index, micro_count, 0
    )

    all_rows = micro_count * tokens
    inverse_tokens = 1.0 / (all_rows * lax.axis_size("dp"))
    partial = grad_pack(
        saved_normed.reshape(all_rows, features),
        saved_grad.reshape(all_rows, features),
        live_index,
        inverse_tokens,
    )
    own_grad = lax.psum_scatter(partial, "dp", scatter_dimension=0, tiled=True)
    gradient = (
        own_grad.reshape(live_count * block_size, own_columns, block_size)
        .transpose(1, 2, 0)
        .astype(jnp.float32)
    )

    rate = 0.1 / math.sqrt(live_count * block_size)
    moment_new = 0.9 * moment[0] + 0.1 * gradient
    second_new = 0.95 * second[0] + 0.05 * gradient * gradient
    stepped = weights[0].astype(jnp.float32) - rate * moment_new / (jnp.sqrt(second_new) + 1e-08)
    own_index = lax.dynamic_slice_in_dim(
        live_index, lax.axis_index("dp") * own_columns, own_columns, 0
    )
    blocked = stepped.reshape(own_columns, block_size, live_count, block_size)
    magnitude = jnp.sqrt(jnp.sum(blocked * blocked, axis=(1, 3)))
    leafed = (
        blocked * shrink(magnitude, 0.15 * math.sqrt(block_size / live_count))[:, None, :, None]
    )
    block_squares = jnp.sum(leafed * leafed, axis=(1, 3))
    head_count = features // HEAD
    head_index = own_index // (HEAD // block_size)
    onehot = (
        head_index[:, :, None] == jnp.arange(head_count, dtype=jnp.int32)[None, None, :]
    ).astype(jnp.float32)
    head_partial = jnp.sum(onehot * block_squares[:, :, None], axis=(0, 1))
    head_squares = spread_sum(head_partial)
    head_factor = shrink(jnp.sqrt(head_squares), 0.45 * math.sqrt(HEAD))
    headed = leafed * jnp.sum(onehot * head_factor[None, None, :], axis=2)[:, None, :, None]
    layer_squares = jnp.sum(head_factor * head_factor * head_squares)
    layer_factor = shrink(jnp.sqrt(layer_squares), 0.45 * math.sqrt(features))
    weights_out = (
        (headed * layer_factor)
        .astype(jnp.bfloat16)
        .reshape(own_columns, block_size, live_count * block_size)
    )
    return (weights_out[None], moment_new[None], second_new[None])


def solution(mesh):
    placed = (
        P(None, "dp", None),
        P(None, "dp", None),
        P("pipe", "dp", None, None),
        P("pipe", None, None),
        P("pipe", "dp", None, None),
        P("pipe", "dp", None, None),
    )
    return jax.shard_map(
        local,
        mesh=mesh,
        in_specs=placed,
        out_specs=(
            P("pipe", "dp", None, None),
            P("pipe", "dp", None, None),
            P("pipe", "dp", None, None),
        ),
        check_vma=False,
    )
```

```python
import functools
import math

import jax
import jax.numpy as jnp
from jax import lax
from jax.experimental import pallas as pl
from jax.experimental.pallas import tpu as pltpu
from jax.sharding import PartitionSpec as P

HEAD = 128


def shifted(value, axis, steps):
    count = lax.axis_size(axis)
    leading, last = (max(0, -steps), min(count, count - steps))
    return lax.ppermute(value, axis, [(source, source + steps) for source in range(leading, last)])


def shrink(magnitude, threshold):
    return jnp.maximum(magnitude - threshold, 0.0) / jnp.maximum(magnitude, threshold)


def expand_kernel(table_ref, t_ref, o_ref):
    per_step = t_ref.shape[0]
    block = 64
    blocks = o_ref.shape[0] // block
    lane = lax.broadcasted_iota(jnp.int32, (block, 2 * block), 1)
    for pp in range(per_step):
        p = pl.program_id(0) * per_step + pp
        for r in range(blocks):
            k0 = table_ref[(2 * p) * blocks + r]
            k1 = table_ref[(2 * p + 1) * blocks + r]
            s0 = pl.multiple_of(jnp.maximum(k0, 0) * block, block)
            s1 = pl.multiple_of(jnp.maximum(k1, 0) * block, block)
            t0 = t_ref[pp, pl.ds(s0, block), :]
            t1 = t_ref[pp, pl.ds(s1, block), :]
            zero = jnp.zeros_like(t0)
            t0 = jnp.where(k0 >= 0, t0, zero)
            t1 = jnp.where(k1 >= 0, t1, zero)
            o_ref[r * block:(r + 1) * block, pp * 2 * block:(pp + 1) * 2 * block] = jnp.where(
                lane < block, t0, t1
            )


def grad_pack_kernel(scale, table_ref, ut_ref, gz_ref, o_ref, g_ref):
    per_step = o_ref.shape[0]
    block = 64
    live_count = o_ref.shape[1] // block
    rows = g_ref.shape[0]
    chunk = 512
    for c in range(rows // chunk):
        g_ref[c * chunk:(c + 1) * chunk, :] = (
            jnp.dot(ut_ref[c * chunk:(c + 1) * chunk, :], gz_ref[...], preferred_element_type=jnp.float32)
            * scale
        ).astype(g_ref.dtype)
    lane = lax.broadcasted_iota(jnp.int32, (block, 2 * block), 1)
    for pp in range(per_step):
        p = pl.program_id(0) * per_step + pp
        for k in range(live_count):
            r0 = table_ref[(2 * p) * live_count + k]
            r1 = table_ref[(2 * p + 1) * live_count + k]
            s0 = pl.multiple_of(r0 * block, block)
            s1 = pl.multiple_of(r1 * block, block)
            t0 = g_ref[pl.ds(s0, block), pp * 2 * block:(pp + 1) * 2 * block]
            t1 = g_ref[pl.ds(s1, block), pp * 2 * block:(pp + 1) * 2 * block]
            o_ref[pp, k * block:(k + 1) * block, :] = jnp.where(lane < block, t0, t1)


PAIRS_PER_STEP = 4


def expand_dense(paired_weights, live_index):
    pair_count, wide, two_blocks = paired_weights.shape
    column_count, live_count = live_index.shape
    block_size = two_blocks // 2
    features = column_count * block_size
    targets = jnp.arange(column_count, dtype=jnp.int32)
    hit = live_index[:, :, None] == targets[None, None, :]
    k_ids = jnp.arange(live_count, dtype=jnp.int32)[None, :, None]
    inverse = jnp.where(
        jnp.any(hit, axis=1), jnp.sum(jnp.where(hit, k_ids, 0), axis=1), -1
    ).astype(jnp.int32)
    return pl.pallas_call(
        expand_kernel,
        out_shape=jax.ShapeDtypeStruct((features, features), paired_weights.dtype),
        grid_spec=pltpu.PrefetchScalarGridSpec(
            num_scalar_prefetch=1,
            grid=(pair_count // PAIRS_PER_STEP,),
            in_specs=[pl.BlockSpec((PAIRS_PER_STEP, wide, two_blocks), lambda q, tbl: (q, 0, 0))],
            out_specs=pl.BlockSpec((features, PAIRS_PER_STEP * two_blocks), lambda q, tbl: (0, q)),
        ),
        cost_estimate=pl.CostEstimate(
            flops=0, transcendentals=0, bytes_accessed=3 * pair_count * wide * two_blocks * 2
        ),
    )(inverse.reshape(-1), paired_weights)


def grad_pack(normed_rows, grad_rows, live_index, scale):
    column_count, live_count = live_index.shape
    all_rows, features = normed_rows.shape
    block_size = features // column_count
    wide = live_count * block_size
    pair_count = column_count // 2
    stripe = PAIRS_PER_STEP * 2 * block_size
    return pl.pallas_call(
        functools.partial(grad_pack_kernel, scale),
        out_shape=jax.ShapeDtypeStruct((pair_count, wide, 2 * block_size), jnp.bfloat16),
        grid_spec=pltpu.PrefetchScalarGridSpec(
            num_scalar_prefetch=1,
            grid=(pair_count // PAIRS_PER_STEP,),
            in_specs=[
                pl.BlockSpec((features, all_rows), lambda q, tbl: (0, 0)),
                pl.BlockSpec((all_rows, stripe), lambda q, tbl: (0, q)),
            ],
            out_specs=pl.BlockSpec((PAIRS_PER_STEP, wide, 2 * block_size), lambda q, tbl: (q, 0, 0)),
            scratch_shapes=[pltpu.VMEM((features, stripe), jnp.bfloat16)],
        ),
        cost_estimate=pl.CostEstimate(
            flops=2 * all_rows * features * features,
            transcendentals=0,
            bytes_accessed=2 * all_rows * features * 2 + pair_count * wide * 2 * block_size * 2,
        ),
    )(live_index.reshape(-1).astype(jnp.int32), normed_rows.T, grad_rows)


def spread_kernel(x_ref, o_ref, pair_ref, chip_sum, recv_ref, pair_send, pair_recv, send_sem, recv_sem):
    chips = recv_ref.shape[0]
    me = lax.axis_index("dp")
    pipe = lax.axis_index("pipe")
    core = me % 2
    chip = me // 2
    partner = chip * 2 + (1 - core)
    barrier = pltpu.get_barrier_semaphore()
    pl.semaphore_signal(barrier, inc=1, device_id=(pipe, partner), device_id_type=pl.DeviceIdType.MESH)
    for step in range(1, chips):
        other = lax.rem(chip + step, chips) * 2 + core
        pl.semaphore_signal(barrier, inc=1, device_id=(pipe, other), device_id_type=pl.DeviceIdType.MESH)
    pl.semaphore_wait(barrier, chips)
    swap = pltpu.make_async_remote_copy(
        src_ref=x_ref,
        dst_ref=pair_ref,
        send_sem=pair_send,
        recv_sem=pair_recv,
        device_id=(pipe, partner),
        device_id_type=pl.DeviceIdType.MESH,
    )
    swap.start()
    swap.wait()
    chip_sum[...] = x_ref[...] + pair_ref[...]
    copies = []
    for step in range(1, chips):
        other = lax.rem(chip + step, chips) * 2 + core
        copy = pltpu.make_async_remote_copy(
            src_ref=chip_sum,
            dst_ref=recv_ref.at[chip],
            send_sem=send_sem.at[step],
            recv_sem=recv_sem.at[chip],
            device_id=(pipe, other),
            device_id_type=pl.DeviceIdType.MESH,
        )
        copy.start()
        copies.append(copy)
    total = chip_sum[...]
    for step in range(1, chips):
        source = lax.rem(chip + chips - step, chips)
        arrival = pltpu.make_async_remote_copy(
            src_ref=chip_sum,
            dst_ref=recv_ref.at[source],
            send_sem=send_sem.at[step],
            recv_sem=recv_sem.at[source],
            device_id=(pipe, source * 2 + core),
            device_id_type=pl.DeviceIdType.MESH,
        )
        arrival.wait_recv()
        total = total + recv_ref[source]
    for copy in copies:
        copy.wait_send()
    o_ref[...] = total


def spread_sum(values):
    chips = lax.axis_size("dp") // 2
    padded = jnp.zeros((8, 128), jnp.float32).at[0, : values.shape[0]].set(values)
    out = pl.pallas_call(
        spread_kernel,
        out_shape=jax.ShapeDtypeStruct((8, 128), jnp.float32),
        in_specs=[pl.BlockSpec(memory_space=pltpu.VMEM)],
        out_specs=pl.BlockSpec(memory_space=pltpu.VMEM),
        scratch_shapes=[
            pltpu.VMEM((8, 128), jnp.float32),
            pltpu.VMEM((8, 128), jnp.float32),
            pltpu.VMEM((chips, 8, 128), jnp.float32),
            pltpu.SemaphoreType.DMA(()),
            pltpu.SemaphoreType.DMA(()),
            pltpu.SemaphoreType.DMA((chips,)),
            pltpu.SemaphoreType.DMA((chips,)),
        ],
        compiler_params=pltpu.CompilerParams(collective_id=0, has_side_effects=True),
    )(padded)
    return out[0, : values.shape[0]]


def layer_forward(entering, dense_w):
    as_float = entering.astype(jnp.float32)
    inverse_rms = lax.rsqrt(jnp.mean(as_float * as_float, axis=-1, keepdims=True) + 1e-05)
    normed = (as_float * inverse_rms).astype(jnp.bfloat16)
    pre_act = jnp.dot(normed, dense_w, preferred_element_type=jnp.float32)
    return ((as_float + jax.nn.silu(pre_act)).astype(jnp.bfloat16), normed, pre_act)


def layer_backward(arriving, entering, pre_act, dense_w):
    as_float = entering.astype(jnp.float32)
    inverse_rms = lax.rsqrt(jnp.mean(as_float * as_float, axis=-1, keepdims=True) + 1e-05)
    sigmoid_z = jax.nn.sigmoid(pre_act)
    grad_pre = (
        arriving.astype(jnp.float32) * (sigmoid_z * (1.0 + pre_act * (1.0 - sigmoid_z)))
    ).astype(jnp.bfloat16)
    grad_normed = lax.dot_general(
        grad_pre, dense_w, (((1,), (1,)), ((), ())), preferred_element_type=jnp.float32
    )
    scaled = as_float * inverse_rms
    leaving = (
        arriving.astype(jnp.float32)
        + inverse_rms
        * (grad_normed - scaled * jnp.mean(grad_normed * scaled, axis=-1, keepdims=True))
    ).astype(jnp.bfloat16)
    return (leaving, grad_pre)


def local(x_in, cotangent, weights, live_rows, moment, second):
    sections = lax.axis_size("pipe")
    section_index = lax.axis_index("pipe")
    group = 2
    micro_total, micro_tokens, features = x_in.shape
    micro_count = micro_total // group
    tokens = micro_tokens * group
    x_in = x_in.reshape(micro_count, tokens, features)
    cotangent = cotangent.reshape(micro_count, tokens, features)
    column_count = live_rows.shape[1]
    live_count = live_rows.shape[2]
    own_columns = weights.shape[1]
    block_size = weights.shape[2]
    live_index = live_rows[0]
    own_pair = weights[0].transpose(2, 0, 1).reshape(1, live_count * block_size, own_columns * block_size)
    paired_weights = lax.all_gather(own_pair, "dp", axis=0, tiled=True)
    dense_w = expand_dense(paired_weights, live_index)
    tick_count = micro_count + sections - 1

    incoming = jnp.zeros((tokens, features), jnp.bfloat16)
    kept_in, kept_normed, kept_pre = [], [], []
    for tick_index in range(tick_count):
        entering = jnp.where(section_index == 0, x_in[min(tick_index, micro_count - 1)], incoming)
        outgoing, normed, pre_act = layer_forward(entering, dense_w)
        kept_in.append(entering)
        kept_normed.append(normed)
        kept_pre.append(pre_act)
        if tick_index + 1 < tick_count:
            incoming = shifted(outgoing, "pipe", 1)
    saved_in = lax.dynamic_slice_in_dim(jnp.stack(kept_in), section_index, micro_count, 0)
    saved_normed = lax.dynamic_slice_in_dim(jnp.stack(kept_normed), section_index, micro_count, 0)
    saved_pre = lax.dynamic_slice_in_dim(jnp.stack(kept_pre), section_index, micro_count, 0)

    incoming_grad = jnp.zeros((tokens, features), jnp.bfloat16)
    kept_grad = []
    for tick_index in range(tick_count):
        slot_index = jnp.clip(tick_index - (sections - 1 - section_index), 0, micro_count - 1)
        arriving = jnp.where(
            section_index == sections - 1,
            cotangent[min(tick_index, micro_count - 1)],
            incoming_grad,
        )
        leaving, grad_pre = layer_backward(
            arriving, saved_in[slot_index], saved_pre[slot_index], dense_w
        )
        kept_grad.append(grad_pre)
        if tick_index + 1 < tick_count:
            incoming_grad = shifted(leaving, "pipe", -1)
    saved_grad = lax.dynamic_slice_in_dim(
        jnp.stack(kept_grad), sections - 1 - section_index, micro_count, 0
    )

    all_rows = micro_count * tokens
    inverse_tokens = 1.0 / (all_rows * lax.axis_size("dp"))
    partial = grad_pack(
        saved_normed.reshape(all_rows, features),
        saved_grad.reshape(all_rows, features),
        live_index,
        inverse_tokens,
    )
    own_grad = lax.psum_scatter(partial, "dp", scatter_dimension=0, tiled=True)
    gradient = (
        own_grad.reshape(live_count * block_size, own_columns, block_size)
        .transpose(1, 2, 0)
        .astype(jnp.float32)
    )

    rate = 0.1 / math.sqrt(live_count * block_size)
    moment_new = 0.9 * moment[0] + 0.1 * gradient
    second_new = 0.95 * second[0] + 0.05 * gradient * gradient
    stepped = weights[0].astype(jnp.float32) - rate * moment_new / (jnp.sqrt(second_new) + 1e-08)
    own_index = lax.dynamic_slice_in_dim(
        live_index, lax.axis_index("dp") * own_columns, own_columns, 0
    )
    blocked = stepped.reshape(own_columns, block_size, live_count, block_size)
    magnitude = jnp.sqrt(jnp.sum(blocked * blocked, axis=(1, 3)))
    leafed = (
        blocked * shrink(magnitude, 0.15 * math.sqrt(block_size / live_count))[:, None, :, None]
    )
    block_squares = jnp.sum(leafed * leafed, axis=(1, 3))
    head_count = features // HEAD
    head_index = own_index // (HEAD // block_size)
    onehot = (
        head_index[:, :, None] == jnp.arange(head_count, dtype=jnp.int32)[None, None, :]
    ).astype(jnp.float32)
    head_partial = jnp.sum(onehot * block_squares[:, :, None], axis=(0, 1))
    head_squares = spread_sum(head_partial)
    head_factor = shrink(jnp.sqrt(head_squares), 0.45 * math.sqrt(HEAD))
    headed = leafed * jnp.sum(onehot * head_factor[None, None, :], axis=2)[:, None, :, None]
    layer_squares = jnp.sum(head_factor * head_factor * head_squares)
    layer_factor = shrink(jnp.sqrt(layer_squares), 0.45 * math.sqrt(features))
    weights_out = (
        (headed * layer_factor)
        .astype(jnp.bfloat16)
        .reshape(own_columns, block_size, live_count * block_size)
    )
    return (weights_out[None], moment_new[None], second_new[None])


def solution(mesh):
    placed = (
        P(None, "dp", None),
        P(None, "dp", None),
        P("pipe", "dp", None, None),
        P("pipe", None, None),
        P("pipe", "dp", None, None),
        P("pipe", "dp", None, None),
    )
    return jax.shard_map(
        local,
        mesh=mesh,
        in_specs=placed,
        out_specs=(
            P("pipe", "dp", None, None),
            P("pipe", "dp", None, None),
            P("pipe", "dp", None, None),
        ),
        check_vma=False,
    )
```

```python
import functools
import math

import jax
import jax.numpy as jnp
from jax import lax
from jax.experimental import pallas as pl
from jax.experimental.pallas import tpu as pltpu
from jax.sharding import PartitionSpec as P

HEAD = 128


def shifted(value, axis, steps):
    count = lax.axis_size(axis)
    leading, last = (max(0, -steps), min(count, count - steps))
    return lax.ppermute(value, axis, [(source, source + steps) for source in range(leading, last)])


def shrink(magnitude, threshold):
    return jnp.maximum(magnitude - threshold, 0.0) / jnp.maximum(magnitude, threshold)


def expand_kernel(table_ref, t_ref, o_ref):
    per_step = t_ref.shape[0]
    block = 64
    blocks = o_ref.shape[0] // block
    lane = lax.broadcasted_iota(jnp.int32, (block, 2 * block), 1)
    for pp in range(per_step):
        p = pl.program_id(0) * per_step + pp
        for r in range(blocks):
            k0 = table_ref[(2 * p) * blocks + r]
            k1 = table_ref[(2 * p + 1) * blocks + r]
            s0 = pl.multiple_of(jnp.maximum(k0, 0) * block, block)
            s1 = pl.multiple_of(jnp.maximum(k1, 0) * block, block)
            t0 = t_ref[pp, pl.ds(s0, block), :]
            t1 = t_ref[pp, pl.ds(s1, block), :]
            zero = jnp.zeros_like(t0)
            t0 = jnp.where(k0 >= 0, t0, zero)
            t1 = jnp.where(k1 >= 0, t1, zero)
            o_ref[r * block:(r + 1) * block, pp * 2 * block:(pp + 1) * 2 * block] = jnp.where(
                lane < block, t0, t1
            )


def grad_pack_kernel(scale, table_ref, ut_ref, gz_ref, o_ref, g_ref):
    per_step = o_ref.shape[0]
    block = 64
    live_count = o_ref.shape[1] // block
    rows = g_ref.shape[0]
    chunk = 512
    for c in range(rows // chunk):
        g_ref[c * chunk:(c + 1) * chunk, :] = (
            jnp.dot(ut_ref[c * chunk:(c + 1) * chunk, :], gz_ref[...], preferred_element_type=jnp.float32)
            * scale
        ).astype(g_ref.dtype)
    lane = lax.broadcasted_iota(jnp.int32, (block, 2 * block), 1)
    for pp in range(per_step):
        p = pl.program_id(0) * per_step + pp
        for k in range(live_count):
            r0 = table_ref[(2 * p) * live_count + k]
            r1 = table_ref[(2 * p + 1) * live_count + k]
            s0 = pl.multiple_of(r0 * block, block)
            s1 = pl.multiple_of(r1 * block, block)
            t0 = g_ref[pl.ds(s0, block), pp * 2 * block:(pp + 1) * 2 * block]
            t1 = g_ref[pl.ds(s1, block), pp * 2 * block:(pp + 1) * 2 * block]
            o_ref[pp, k * block:(k + 1) * block, :] = jnp.where(lane < block, t0, t1)


PAIRS_PER_STEP = 4
GRAD_PAIRS_PER_STEP = 8


def expand_dense(paired_weights, live_index):
    pair_count, wide, two_blocks = paired_weights.shape
    column_count, live_count = live_index.shape
    block_size = two_blocks // 2
    features = column_count * block_size
    targets = jnp.arange(column_count, dtype=jnp.int32)
    hit = live_index[:, :, None] == targets[None, None, :]
    k_ids = jnp.arange(live_count, dtype=jnp.int32)[None, :, None]
    inverse = jnp.where(
        jnp.any(hit, axis=1), jnp.sum(jnp.where(hit, k_ids, 0), axis=1), -1
    ).astype(jnp.int32)
    return pl.pallas_call(
        expand_kernel,
        out_shape=jax.ShapeDtypeStruct((features, features), paired_weights.dtype),
        grid_spec=pltpu.PrefetchScalarGridSpec(
            num_scalar_prefetch=1,
            grid=(pair_count // PAIRS_PER_STEP,),
            in_specs=[pl.BlockSpec((PAIRS_PER_STEP, wide, two_blocks), lambda q, tbl: (q, 0, 0))],
            out_specs=pl.BlockSpec((features, PAIRS_PER_STEP * two_blocks), lambda q, tbl: (0, q)),
        ),
        cost_estimate=pl.CostEstimate(
            flops=0, transcendentals=0, bytes_accessed=3 * pair_count * wide * two_blocks * 2
        ),
    )(inverse.reshape(-1), paired_weights)


def grad_pack(normed_rows, grad_rows, live_index, scale):
    column_count, live_count = live_index.shape
    all_rows, features = normed_rows.shape
    block_size = features // column_count
    wide = live_count * block_size
    pair_count = column_count // 2
    stripe = GRAD_PAIRS_PER_STEP * 2 * block_size
    return pl.pallas_call(
        functools.partial(grad_pack_kernel, scale),
        out_shape=jax.ShapeDtypeStruct((pair_count, wide, 2 * block_size), jnp.bfloat16),
        grid_spec=pltpu.PrefetchScalarGridSpec(
            num_scalar_prefetch=1,
            grid=(pair_count // GRAD_PAIRS_PER_STEP,),
            in_specs=[
                pl.BlockSpec((features, all_rows), lambda q, tbl: (0, 0)),
                pl.BlockSpec((all_rows, stripe), lambda q, tbl: (0, q)),
            ],
            out_specs=pl.BlockSpec((GRAD_PAIRS_PER_STEP, wide, 2 * block_size), lambda q, tbl: (q, 0, 0)),
            scratch_shapes=[pltpu.VMEM((features, stripe), jnp.bfloat16)],
        ),
        cost_estimate=pl.CostEstimate(
            flops=2 * all_rows * features * features,
            transcendentals=0,
            bytes_accessed=2 * all_rows * features * 2 + pair_count * wide * 2 * block_size * 2,
        ),
    )(live_index.reshape(-1).astype(jnp.int32), normed_rows.T, grad_rows)


def spread_kernel(x_ref, o_ref, recv_ref, send_sem, recv_sem):
    count = recv_ref.shape[0]
    me = lax.axis_index("dp")
    pipe = lax.axis_index("pipe")
    barrier = pltpu.get_barrier_semaphore()
    for step in range(1, count):
        peer = lax.rem(me + step, count)
        pl.semaphore_signal(barrier, inc=1, device_id=(pipe, peer), device_id_type=pl.DeviceIdType.MESH)
    pl.semaphore_wait(barrier, count - 1)
    copies = []
    for step in range(1, count):
        peer = lax.rem(me + step, count)
        copy = pltpu.make_async_remote_copy(
            src_ref=x_ref,
            dst_ref=recv_ref.at[me],
            send_sem=send_sem.at[step],
            recv_sem=recv_sem.at[me],
            device_id=(pipe, peer),
            device_id_type=pl.DeviceIdType.MESH,
        )
        copy.start()
        copies.append(copy)
    total = x_ref[...]
    for step in range(1, count):
        source = lax.rem(me + count - step, count)
        arrival = pltpu.make_async_remote_copy(
            src_ref=x_ref,
            dst_ref=recv_ref.at[source],
            send_sem=send_sem.at[step],
            recv_sem=recv_sem.at[source],
            device_id=(pipe, source),
            device_id_type=pl.DeviceIdType.MESH,
        )
        arrival.wait_recv()
        total = total + recv_ref[source]
    for copy in copies:
        copy.wait_send()
    o_ref[...] = total


def spread_sum(values):
    count = lax.axis_size("dp")
    padded = jnp.zeros((8, 128), jnp.float32).at[0, : values.shape[0]].set(values)
    out = pl.pallas_call(
        spread_kernel,
        out_shape=jax.ShapeDtypeStruct((8, 128), jnp.float32),
        in_specs=[pl.BlockSpec(memory_space=pltpu.VMEM)],
        out_specs=pl.BlockSpec(memory_space=pltpu.VMEM),
        scratch_shapes=[
            pltpu.VMEM((count, 8, 128), jnp.float32),
            pltpu.SemaphoreType.DMA((count,)),
            pltpu.SemaphoreType.DMA((count,)),
        ],
        compiler_params=pltpu.CompilerParams(collective_id=0, has_side_effects=True),
    )(padded)
    return out[0, : values.shape[0]]


def layer_forward(entering, dense_w):
    as_float = entering.astype(jnp.float32)
    inverse_rms = lax.rsqrt(jnp.mean(as_float * as_float, axis=-1, keepdims=True) + 1e-05)
    normed = (as_float * inverse_rms).astype(jnp.bfloat16)
    pre_act = jnp.dot(normed, dense_w, preferred_element_type=jnp.float32)
    return ((as_float + jax.nn.silu(pre_act)).astype(jnp.bfloat16), normed, pre_act)


def layer_backward(arriving, entering, pre_act, dense_w):
    as_float = entering.astype(jnp.float32)
    inverse_rms = lax.rsqrt(jnp.mean(as_float * as_float, axis=-1, keepdims=True) + 1e-05)
    sigmoid_z = jax.nn.sigmoid(pre_act)
    grad_pre = (
        arriving.astype(jnp.float32) * (sigmoid_z * (1.0 + pre_act * (1.0 - sigmoid_z)))
    ).astype(jnp.bfloat16)
    grad_normed = lax.dot_general(
        grad_pre, dense_w, (((1,), (1,)), ((), ())), preferred_element_type=jnp.float32
    )
    scaled = as_float * inverse_rms
    leaving = (
        arriving.astype(jnp.float32)
        + inverse_rms
        * (grad_normed - scaled * jnp.mean(grad_normed * scaled, axis=-1, keepdims=True))
    ).astype(jnp.bfloat16)
    return (leaving, grad_pre)


def local(x_in, cotangent, weights, live_rows, moment, second):
    sections = lax.axis_size("pipe")
    section_index = lax.axis_index("pipe")
    group = 2
    micro_total, micro_tokens, features = x_in.shape
    micro_count = micro_total // group
    tokens = micro_tokens * group
    x_in = x_in.reshape(micro_count, tokens, features)
    cotangent = cotangent.reshape(micro_count, tokens, features)
    column_count = live_rows.shape[1]
    live_count = live_rows.shape[2]
    own_columns = weights.shape[1]
    block_size = weights.shape[2]
    live_index = live_rows[0]
    own_pair = weights[0].transpose(2, 0, 1).reshape(1, live_count * block_size, own_columns * block_size)
    paired_weights = lax.all_gather(own_pair, "dp", axis=0, tiled=True)
    dense_w = expand_dense(paired_weights, live_index)
    tick_count = micro_count + sections - 1

    incoming = jnp.zeros((tokens, features), jnp.bfloat16)
    kept_in, kept_normed, kept_pre = [], [], []
    for tick_index in range(tick_count):
        entering = jnp.where(section_index == 0, x_in[min(tick_index, micro_count - 1)], incoming)
        outgoing, normed, pre_act = layer_forward(entering, dense_w)
        kept_in.append(entering)
        kept_normed.append(normed)
        kept_pre.append(pre_act)
        if tick_index + 1 < tick_count:
            incoming = shifted(outgoing, "pipe", 1)
    saved_in = lax.dynamic_slice_in_dim(jnp.stack(kept_in), section_index, micro_count, 0)
    saved_normed = lax.dynamic_slice_in_dim(jnp.stack(kept_normed), section_index, micro_count, 0)
    saved_pre = lax.dynamic_slice_in_dim(jnp.stack(kept_pre), section_index, micro_count, 0)

    incoming_grad = jnp.zeros((tokens, features), jnp.bfloat16)
    kept_grad = []
    for tick_index in range(tick_count):
        slot_index = jnp.clip(tick_index - (sections - 1 - section_index), 0, micro_count - 1)
        arriving = jnp.where(
            section_index == sections - 1,
            cotangent[min(tick_index, micro_count - 1)],
            incoming_grad,
        )
        leaving, grad_pre = layer_backward(
            arriving, saved_in[slot_index], saved_pre[slot_index], dense_w
        )
        kept_grad.append(grad_pre)
        if tick_index + 1 < tick_count:
            incoming_grad = shifted(leaving, "pipe", -1)
    saved_grad = lax.dynamic_slice_in_dim(
        jnp.stack(kept_grad), sections - 1 - section_index, micro_count, 0
    )

    all_rows = micro_count * tokens
    inverse_tokens = 1.0 / (all_rows * lax.axis_size("dp"))
    partial = grad_pack(
        saved_normed.reshape(all_rows, features),
        saved_grad.reshape(all_rows, features),
        live_index,
        inverse_tokens,
    )
    own_grad = lax.psum_scatter(partial, "dp", scatter_dimension=0, tiled=True)
    gradient = (
        own_grad.reshape(live_count * block_size, own_columns, block_size)
        .transpose(1, 2, 0)
        .astype(jnp.float32)
    )

    rate = 0.1 / math.sqrt(live_count * block_size)
    moment_new = 0.9 * moment[0] + 0.1 * gradient
    second_new = 0.95 * second[0] + 0.05 * gradient * gradient
    stepped = weights[0].astype(jnp.float32) - rate * moment_new / (jnp.sqrt(second_new) + 1e-08)
    own_index = lax.dynamic_slice_in_dim(
        live_index, lax.axis_index("dp") * own_columns, own_columns, 0
    )
    blocked = stepped.reshape(own_columns, block_size, live_count, block_size)
    magnitude = jnp.sqrt(jnp.sum(blocked * blocked, axis=(1, 3)))
    leafed = (
        blocked * shrink(magnitude, 0.15 * math.sqrt(block_size / live_count))[:, None, :, None]
    )
    block_squares = jnp.sum(leafed * leafed, axis=(1, 3))
    head_count = features // HEAD
    head_index = own_index // (HEAD // block_size)
    onehot = (
        head_index[:, :, None] == jnp.arange(head_count, dtype=jnp.int32)[None, None, :]
    ).astype(jnp.float32)
    head_partial = jnp.sum(onehot * block_squares[:, :, None], axis=(0, 1))
    head_squares = spread_sum(head_partial)
    head_factor = shrink(jnp.sqrt(head_squares), 0.45 * math.sqrt(HEAD))
    headed = leafed * jnp.sum(onehot * head_factor[None, None, :], axis=2)[:, None, :, None]
    layer_squares = jnp.sum(head_factor * head_factor * head_squares)
    layer_factor = shrink(jnp.sqrt(layer_squares), 0.45 * math.sqrt(features))
    weights_out = (
        (headed * layer_factor)
        .astype(jnp.bfloat16)
        .reshape(own_columns, block_size, live_count * block_size)
    )
    return (weights_out[None], moment_new[None], second_new[None])


def solution(mesh):
    placed = (
        P(None, "dp", None),
        P(None, "dp", None),
        P("pipe", "dp", None, None),
        P("pipe", None, None),
        P("pipe", "dp", None, None),
        P("pipe", "dp", None, None),
    )
    return jax.shard_map(
        local,
        mesh=mesh,
        in_specs=placed,
        out_specs=(
            P("pipe", "dp", None, None),
            P("pipe", "dp", None, None),
            P("pipe", "dp", None, None),
        ),
        check_vma=False,
    )
```

```python
import functools
import math

import jax
import jax.numpy as jnp
from jax import lax
from jax.experimental import pallas as pl
from jax.experimental.pallas import tpu as pltpu
from jax.sharding import PartitionSpec as P

HEAD = 128


def shifted(value, axis, steps):
    count = lax.axis_size(axis)
    leading, last = (max(0, -steps), min(count, count - steps))
    return lax.ppermute(value, axis, [(source, source + steps) for source in range(leading, last)])


def shrink(magnitude, threshold):
    return jnp.maximum(magnitude - threshold, 0.0) / jnp.maximum(magnitude, threshold)


def expand_kernel(table_ref, t_ref, o_ref):
    per_step = t_ref.shape[0]
    block = 64
    blocks = o_ref.shape[0] // block
    lane = lax.broadcasted_iota(jnp.int32, (block, 2 * block), 1)
    for pp in range(per_step):
        p = pl.program_id(0) * per_step + pp
        for r in range(blocks):
            k0 = table_ref[(2 * p) * blocks + r]
            k1 = table_ref[(2 * p + 1) * blocks + r]
            s0 = pl.multiple_of(jnp.maximum(k0, 0) * block, block)
            s1 = pl.multiple_of(jnp.maximum(k1, 0) * block, block)
            t0 = t_ref[pp, pl.ds(s0, block), :]
            t1 = t_ref[pp, pl.ds(s1, block), :]
            zero = jnp.zeros_like(t0)
            t0 = jnp.where(k0 >= 0, t0, zero)
            t1 = jnp.where(k1 >= 0, t1, zero)
            o_ref[r * block:(r + 1) * block, pp * 2 * block:(pp + 1) * 2 * block] = jnp.where(
                lane < block, t0, t1
            )


def grad_pack_kernel(scale, table_ref, ut_ref, gz_ref, o_ref, g_ref):
    per_step = o_ref.shape[0]
    block = 64
    live_count = o_ref.shape[1] // block
    rows = g_ref.shape[0]
    chunk = 512
    for c in range(rows // chunk):
        g_ref[c * chunk:(c + 1) * chunk, :] = (
            jnp.dot(ut_ref[c * chunk:(c + 1) * chunk, :], gz_ref[...], preferred_element_type=jnp.float32)
            * scale
        ).astype(g_ref.dtype)
    lane = lax.broadcasted_iota(jnp.int32, (block, 2 * block), 1)
    for pp in range(per_step):
        p = pl.program_id(0) * per_step + pp
        for k in range(live_count):
            r0 = table_ref[(2 * p) * live_count + k]
            r1 = table_ref[(2 * p + 1) * live_count + k]
            s0 = pl.multiple_of(r0 * block, block)
            s1 = pl.multiple_of(r1 * block, block)
            t0 = g_ref[pl.ds(s0, block), pp * 2 * block:(pp + 1) * 2 * block]
            t1 = g_ref[pl.ds(s1, block), pp * 2 * block:(pp + 1) * 2 * block]
            o_ref[pp, k * block:(k + 1) * block, :] = jnp.where(lane < block, t0, t1)


PAIRS_PER_STEP = 4
GRAD_PAIRS_PER_STEP = 2


def expand_dense(paired_weights, live_index):
    pair_count, wide, two_blocks = paired_weights.shape
    column_count, live_count = live_index.shape
    block_size = two_blocks // 2
    features = column_count * block_size
    targets = jnp.arange(column_count, dtype=jnp.int32)
    hit = live_index[:, :, None] == targets[None, None, :]
    k_ids = jnp.arange(live_count, dtype=jnp.int32)[None, :, None]
    inverse = jnp.where(
        jnp.any(hit, axis=1), jnp.sum(jnp.where(hit, k_ids, 0), axis=1), -1
    ).astype(jnp.int32)
    return pl.pallas_call(
        expand_kernel,
        out_shape=jax.ShapeDtypeStruct((features, features), paired_weights.dtype),
        grid_spec=pltpu.PrefetchScalarGridSpec(
            num_scalar_prefetch=1,
            grid=(pair_count // PAIRS_PER_STEP,),
            in_specs=[pl.BlockSpec((PAIRS_PER_STEP, wide, two_blocks), lambda q, tbl: (q, 0, 0))],
            out_specs=pl.BlockSpec((features, PAIRS_PER_STEP * two_blocks), lambda q, tbl: (0, q)),
        ),
        cost_estimate=pl.CostEstimate(
            flops=0, transcendentals=0, bytes_accessed=3 * pair_count * wide * two_blocks * 2
        ),
    )(inverse.reshape(-1), paired_weights)


def grad_pack(normed_rows, grad_rows, live_index, scale):
    column_count, live_count = live_index.shape
    all_rows, features = normed_rows.shape
    block_size = features // column_count
    wide = live_count * block_size
    pair_count = column_count // 2
    stripe = GRAD_PAIRS_PER_STEP * 2 * block_size
    return pl.pallas_call(
        functools.partial(grad_pack_kernel, scale),
        out_shape=jax.ShapeDtypeStruct((pair_count, wide, 2 * block_size), jnp.bfloat16),
        grid_spec=pltpu.PrefetchScalarGridSpec(
            num_scalar_prefetch=1,
            grid=(pair_count // GRAD_PAIRS_PER_STEP,),
            in_specs=[
                pl.BlockSpec((features, all_rows), lambda q, tbl: (0, 0)),
                pl.BlockSpec((all_rows, stripe), lambda q, tbl: (0, q)),
            ],
            out_specs=pl.BlockSpec((GRAD_PAIRS_PER_STEP, wide, 2 * block_size), lambda q, tbl: (q, 0, 0)),
            scratch_shapes=[pltpu.VMEM((features, stripe), jnp.bfloat16)],
        ),
        cost_estimate=pl.CostEstimate(
            flops=2 * all_rows * features * features,
            transcendentals=0,
            bytes_accessed=2 * all_rows * features * 2 + pair_count * wide * 2 * block_size * 2,
        ),
    )(live_index.reshape(-1).astype(jnp.int32), normed_rows.T, grad_rows)


def spread_kernel(x_ref, o_ref, recv_ref, send_sem, recv_sem):
    count = recv_ref.shape[0]
    me = lax.axis_index("dp")
    pipe = lax.axis_index("pipe")
    barrier = pltpu.get_barrier_semaphore()
    for step in range(1, count):
        peer = lax.rem(me + step, count)
        pl.semaphore_signal(barrier, inc=1, device_id=(pipe, peer), device_id_type=pl.DeviceIdType.MESH)
    pl.semaphore_wait(barrier, count - 1)
    copies = []
    for step in range(1, count):
        peer = lax.rem(me + step, count)
        copy = pltpu.make_async_remote_copy(
            src_ref=x_ref,
            dst_ref=recv_ref.at[me],
            send_sem=send_sem.at[step],
            recv_sem=recv_sem.at[me],
            device_id=(pipe, peer),
            device_id_type=pl.DeviceIdType.MESH,
        )
        copy.start()
        copies.append(copy)
    total = x_ref[...]
    for step in range(1, count):
        source = lax.rem(me + count - step, count)
        arrival = pltpu.make_async_remote_copy(
            src_ref=x_ref,
            dst_ref=recv_ref.at[source],
            send_sem=send_sem.at[step],
            recv_sem=recv_sem.at[source],
            device_id=(pipe, source),
            device_id_type=pl.DeviceIdType.MESH,
        )
        arrival.wait_recv()
        total = total + recv_ref[source]
    for copy in copies:
        copy.wait_send()
    o_ref[...] = total


def spread_sum(values):
    count = lax.axis_size("dp")
    padded = jnp.zeros((8, 128), jnp.float32).at[0, : values.shape[0]].set(values)
    out = pl.pallas_call(
        spread_kernel,
        out_shape=jax.ShapeDtypeStruct((8, 128), jnp.float32),
        in_specs=[pl.BlockSpec(memory_space=pltpu.VMEM)],
        out_specs=pl.BlockSpec(memory_space=pltpu.VMEM),
        scratch_shapes=[
            pltpu.VMEM((count, 8, 128), jnp.float32),
            pltpu.SemaphoreType.DMA((count,)),
            pltpu.SemaphoreType.DMA((count,)),
        ],
        compiler_params=pltpu.CompilerParams(collective_id=0, has_side_effects=True),
    )(padded)
    return out[0, : values.shape[0]]


def layer_forward(entering, dense_w):
    as_float = entering.astype(jnp.float32)
    inverse_rms = lax.rsqrt(jnp.mean(as_float * as_float, axis=-1, keepdims=True) + 1e-05)
    normed = (as_float * inverse_rms).astype(jnp.bfloat16)
    pre_act = jnp.dot(normed, dense_w, preferred_element_type=jnp.float32)
    return ((as_float + jax.nn.silu(pre_act)).astype(jnp.bfloat16), normed, pre_act)


def layer_backward(arriving, entering, pre_act, dense_w):
    as_float = entering.astype(jnp.float32)
    inverse_rms = lax.rsqrt(jnp.mean(as_float * as_float, axis=-1, keepdims=True) + 1e-05)
    sigmoid_z = jax.nn.sigmoid(pre_act)
    grad_pre = (
        arriving.astype(jnp.float32) * (sigmoid_z * (1.0 + pre_act * (1.0 - sigmoid_z)))
    ).astype(jnp.bfloat16)
    grad_normed = lax.dot_general(
        grad_pre, dense_w, (((1,), (1,)), ((), ())), preferred_element_type=jnp.float32
    )
    scaled = as_float * inverse_rms
    leaving = (
        arriving.astype(jnp.float32)
        + inverse_rms
        * (grad_normed - scaled * jnp.mean(grad_normed * scaled, axis=-1, keepdims=True))
    ).astype(jnp.bfloat16)
    return (leaving, grad_pre)


def local(x_in, cotangent, weights, live_rows, moment, second):
    sections = lax.axis_size("pipe")
    section_index = lax.axis_index("pipe")
    group = 2
    micro_total, micro_tokens, features = x_in.shape
    micro_count = micro_total // group
    tokens = micro_tokens * group
    x_in = x_in.reshape(micro_count, tokens, features)
    cotangent = cotangent.reshape(micro_count, tokens, features)
    column_count = live_rows.shape[1]
    live_count = live_rows.shape[2]
    own_columns = weights.shape[1]
    block_size = weights.shape[2]
    live_index = live_rows[0]
    own_pair = weights[0].transpose(2, 0, 1).reshape(1, live_count * block_size, own_columns * block_size)
    paired_weights = lax.all_gather(own_pair, "dp", axis=0, tiled=True)
    dense_w = expand_dense(paired_weights, live_index)
    tick_count = micro_count + sections - 1

    incoming = jnp.zeros((tokens, features), jnp.bfloat16)
    kept_in, kept_normed, kept_pre = [], [], []
    for tick_index in range(tick_count):
        entering = jnp.where(section_index == 0, x_in[min(tick_index, micro_count - 1)], incoming)
        outgoing, normed, pre_act = layer_forward(entering, dense_w)
        kept_in.append(entering)
        kept_normed.append(normed)
        kept_pre.append(pre_act)
        if tick_index + 1 < tick_count:
            incoming = shifted(outgoing, "pipe", 1)
    saved_in = lax.dynamic_slice_in_dim(jnp.stack(kept_in), section_index, micro_count, 0)
    saved_normed = lax.dynamic_slice_in_dim(jnp.stack(kept_normed), section_index, micro_count, 0)
    saved_pre = lax.dynamic_slice_in_dim(jnp.stack(kept_pre), section_index, micro_count, 0)

    incoming_grad = jnp.zeros((tokens, features), jnp.bfloat16)
    kept_grad = []
    for tick_index in range(tick_count):
        slot_index = jnp.clip(tick_index - (sections - 1 - section_index), 0, micro_count - 1)
        arriving = jnp.where(
            section_index == sections - 1,
            cotangent[min(tick_index, micro_count - 1)],
            incoming_grad,
        )
        leaving, grad_pre = layer_backward(
            arriving, saved_in[slot_index], saved_pre[slot_index], dense_w
        )
        kept_grad.append(grad_pre)
        if tick_index + 1 < tick_count:
            incoming_grad = shifted(leaving, "pipe", -1)
    saved_grad = lax.dynamic_slice_in_dim(
        jnp.stack(kept_grad), sections - 1 - section_index, micro_count, 0
    )

    all_rows = micro_count * tokens
    inverse_tokens = 1.0 / (all_rows * lax.axis_size("dp"))
    partial = grad_pack(
        saved_normed.reshape(all_rows, features),
        saved_grad.reshape(all_rows, features),
        live_index,
        inverse_tokens,
    )
    own_grad = lax.psum_scatter(partial, "dp", scatter_dimension=0, tiled=True)
    gradient = (
        own_grad.reshape(live_count * block_size, own_columns, block_size)
        .transpose(1, 2, 0)
        .astype(jnp.float32)
    )

    rate = 0.1 / math.sqrt(live_count * block_size)
    moment_new = 0.9 * moment[0] + 0.1 * gradient
    second_new = 0.95 * second[0] + 0.05 * gradient * gradient
    stepped = weights[0].astype(jnp.float32) - rate * moment_new / (jnp.sqrt(second_new) + 1e-08)
    own_index = lax.dynamic_slice_in_dim(
        live_index, lax.axis_index("dp") * own_columns, own_columns, 0
    )
    blocked = stepped.reshape(own_columns, block_size, live_count, block_size)
    magnitude = jnp.sqrt(jnp.sum(blocked * blocked, axis=(1, 3)))
    leafed = (
        blocked * shrink(magnitude, 0.15 * math.sqrt(block_size / live_count))[:, None, :, None]
    )
    block_squares = jnp.sum(leafed * leafed, axis=(1, 3))
    head_count = features // HEAD
    head_index = own_index // (HEAD // block_size)
    onehot = (
        head_index[:, :, None] == jnp.arange(head_count, dtype=jnp.int32)[None, None, :]
    ).astype(jnp.float32)
    head_partial = jnp.sum(onehot * block_squares[:, :, None], axis=(0, 1))
    head_squares = spread_sum(head_partial)
    head_factor = shrink(jnp.sqrt(head_squares), 0.45 * math.sqrt(HEAD))
    headed = leafed * jnp.sum(onehot * head_factor[None, None, :], axis=2)[:, None, :, None]
    layer_squares = jnp.sum(head_factor * head_factor * head_squares)
    layer_factor = shrink(jnp.sqrt(layer_squares), 0.45 * math.sqrt(features))
    weights_out = (
        (headed * layer_factor)
        .astype(jnp.bfloat16)
        .reshape(own_columns, block_size, live_count * block_size)
    )
    return (weights_out[None], moment_new[None], second_new[None])


def solution(mesh):
    placed = (
        P(None, "dp", None),
        P(None, "dp", None),
        P("pipe", "dp", None, None),
        P("pipe", None, None),
        P("pipe", "dp", None, None),
        P("pipe", "dp", None, None),
    )
    return jax.shard_map(
        local,
        mesh=mesh,
        in_specs=placed,
        out_specs=(
            P("pipe", "dp", None, None),
            P("pipe", "dp", None, None),
            P("pipe", "dp", None, None),
        ),
        check_vma=False,
    )
```
